32 devices in a mesh: gx: 4 (over x, core), gy: 8 (over z, y).
Axes of the slice: x: 2, y: 2, z: 4, core: 2. Of those that a mesh axis runs over, the one named last changes fastest.
Arguments:
- velocity: float32 [3, 64, 128, 128], P(None, 'gx', 'gy'), may hold values from -6 to 6
- tile_cells: int32 [4, 8, 96], P('gx', 'gy'), may hold values from 0 to 255, as said below
- owner: int32 [4, 16], P('gx'), may hold values from 0 to 7, as said below
- point_slot: int32 [4, 16, 384], P('gx'), may hold values from 0 to 767
- point_z: int32 [4, 16, 384], P('gx'), may hold values from 0 to 127
- loading: float32 [4, 16, 384], P('gx'), may hold values from 0.45 to 2
Outputs:
- velocity_out: float32 [3, 64, 128, 128], P(None, 'gx', 'gy')
The draws below stay inside these ranges and needn't reach their ends.
Inputs may be any that keep to these rules, and one draw needn't show every extreme that they name: `tile_cells`: the 96 cells of one tile are distinct. `owner`: in every column of tiles one index of gy owns exactly 6 turbines and none owns more.
All inputs are finite; a program needn't handle non-finite values.
Results may differ from the reference program's by a relative error of at most 0.0016.
Values may be sent and summed in bfloat16 or wider, within the bound.
No kernel may reach another device: no remote copies, remote signals or barrier semaphores. Data moves between devices by JAX's collectives and lax.ppermute only.
A program may use at most 256 MiB of HBM per device.

```python
import math
import jax
import jax.numpy as jnp
from jax import lax

CX = 16
CY = 16
NZ = 128
R_DEV = 96
PTS = 384
T_DEV = 2
STEPS = 2
GROUPS_X = 4
TILES_Y = 8
TURB_GROUP = 16
NX = 64
NY = 128
N_GX = 4
N_GY = 8


def draw_tile_cells(key, part):
    total = CX * CY
    key_list = jax.random.split(key, GROUPS_X * TILES_Y)

    def draw_tile(sub_key):
        inner = jax.random.permutation(sub_key, jnp.arange(1, total - 1, dtype=jnp.int32))[:R_DEV - 2]
        chosen = jnp.concatenate([jnp.array([0, total - 1], dtype=jnp.int32), inner])
        return jax.random.permutation(jax.random.fold_in(sub_key, 7), chosen).astype(jnp.int32)
    return jax.vmap(draw_tile)(key_list).reshape(GROUPS_X, TILES_Y, R_DEV)


def draw_owner(key, part):
    busiest = 3 * T_DEV
    remaining = TURB_GROUP - busiest
    base_owner = jnp.concatenate([jnp.zeros((busiest,), jnp.int32), 1 + jnp.arange(remaining, dtype=jnp.int32) % (TILES_Y - 2)])

    def draw_group(sub_key):
        relabel = jax.random.permutation(sub_key, jnp.arange(TILES_Y, dtype=jnp.int32))
        turb_order = jax.random.permutation(jax.random.fold_in(sub_key, 3), jnp.arange(TURB_GROUP, dtype=jnp.int32))
        return relabel[base_owner[turb_order]].astype(jnp.int32)
    return jax.vmap(draw_group)(jax.random.split(key, GROUPS_X))


def draw_point_slot(key, part):
    key_home, key_side, key_row = jax.random.split(key, 3)
    home = jax.random.randint(key_home, (GROUPS_X, TURB_GROUP, 1), 0, TILES_Y, dtype=jnp.int32)
    side = jax.random.randint(key_side, (GROUPS_X, TURB_GROUP, PTS), 0, 2, dtype=jnp.int32)
    tile = jnp.minimum(home + side, TILES_Y - 1)
    row_pick = jax.random.randint(key_row, (GROUPS_X, TURB_GROUP, PTS), 0, R_DEV, dtype=jnp.int32)
    slots = tile * R_DEV + row_pick
    slots = slots.at[:, 0, 0].set(0)
    slots = slots.at[:, TURB_GROUP - 1, PTS - 1].set(TILES_Y * R_DEV - 1)
    return slots.astype(jnp.int32)


def draw_loading(key, part):
    key_turb, key_point = jax.random.split(key)
    shape = (GROUPS_X, TURB_GROUP, PTS)
    turbine_factor = jnp.exp(jax.random.uniform(key_turb, (GROUPS_X, TURB_GROUP, 1), jnp.float32, math.log(0.7), math.log(1.4)))
    point_factor = jnp.exp(jax.random.uniform(key_point, shape, jnp.float32, math.log(0.8), math.log(1.25)))
    return (turbine_factor * point_factor).astype(jnp.float32)


def with_ends(entries, stream_key, low, top_value):
    longest = entries.shape.index(max(entries.shape))
    spots = []
    for shift in (0, 1):
        where = [jax.random.randint(jax.random.fold_in(stream_key, axis), (), 0, length) for axis, length in enumerate(entries.shape)]
        where[longest] = (where[longest] + shift) % entries.shape[longest]
        spots.append(tuple(where))
    return entries.at[spots[0]].set(low).at[spots[1]].set(top_value)


def block_levels(rng, shape, pieces, least, high):
    def one(axis_at, shards_of):
        heights = jax.random.uniform(jax.random.fold_in(jax.random.fold_in(rng, 6), axis_at), (shards_of,), jnp.float32, least / len(pieces), high / len(pieces))
        return jnp.repeat(jnp.exp(heights), shape[axis_at] // shards_of).reshape((-1,) + (1,) * (len(shape) - axis_at - 1))

    gain = one(*pieces[0])
    for cut in pieces[1:]:
        gain = gain * one(*cut)
    return gain


def scatter_about(rng, extent, scale, most, cuts=(), held_as=jnp.bfloat16):
    factor_of = block_levels(rng, extent, cuts, -0.22, 0.18) if cuts else 1.0
    entries = jax.random.normal(rng, extent, jnp.float32) * scale * factor_of
    return jnp.minimum(jnp.maximum(entries, -most), most).astype(held_as)


def setup_inputs(seed: int = 0) -> dict:
    seeds = jax.random.split(jax.random.key(seed), 7)
    velocity = scatter_about(seeds[0], (3, NX, NY, NZ), 1.0, 6.0, ((1, 4), (2, 8)), jnp.float32)
    tile_cells = draw_tile_cells(jax.random.fold_in(seeds[6], 71), 0)
    owner = draw_owner(jax.random.fold_in(seeds[6], 71), 0)
    point_slot = draw_point_slot(jax.random.fold_in(seeds[6], 71), 0)
    point_z = with_ends(jax.random.randint(seeds[4], (GROUPS_X, TURB_GROUP, PTS), 0, NZ), jax.random.fold_in(seeds[4], 1), 0, NZ - 1).astype(jnp.int32)
    loading = draw_loading(jax.random.fold_in(seeds[6], 71), 0)
    return {"velocity": velocity, "tile_cells": tile_cells, "owner": owner, "point_slot": point_slot, "point_z": point_z, "loading": loading}


SPREAD = 0.12
CARRY = 0.25
FREE_WIND = 1.0
LOAD = 0.6


def stencil(velocity, force):
    padded = jnp.pad(velocity, ((0, 0), (1, 1), (1, 1), (1, 1)))
    beside = padded[:, 2:, 1:-1, 1:-1] + padded[:, :-2, 1:-1, 1:-1]
    beside = beside + padded[:, 1:-1, 2:, 1:-1] + padded[:, 1:-1, :-2, 1:-1]
    beside = beside + padded[:, 1:-1, 1:-1, 2:] + padded[:, 1:-1, 1:-1, :-2]
    laplace = beside - 6.0 * velocity
    upwind = velocity - padded[:, :-2, 1:-1, 1:-1]
    return velocity + SPREAD * laplace - CARRY * upwind + force


def reference(velocity, tile_cells, owner, point_slot, point_z, loading):
    slot_count = N_GY * R_DEV
    for substep in range(STEPS):
        field_flat = velocity.reshape(3, NX * NY, NZ)
        force = jnp.zeros((3, NX * NY, NZ), jnp.float32)
        for column in range(N_GX):
            cells = tile_cells[column]
            local_x = cells // CY
            local_y = cells % CY
            global_x = column * CX + local_x
            global_y = jnp.arange(N_GY, dtype=jnp.int32)[:, None] * CY + local_y
            flat_index = (global_x * NY + global_y).reshape(-1).astype(jnp.int32)
            rows = field_flat[:, flat_index, :].astype(jnp.bfloat16)
            sampled = rows[:, point_slot[column], point_z[column]].astype(jnp.float32)
            disk_wind = FREE_WIND + jnp.mean(sampled[0], axis=-1)
            load_sums = jnp.sum(loading[column], axis=-1)
            member = owner[column][:, None] == owner[column][None, :]
            group_sum = jnp.sum(jnp.where(member, load_sums[None, :], 0.0), axis=-1)
            group_count = jnp.sum(member.astype(jnp.float32), axis=-1)
            load_mean = group_sum / (group_count * PTS)
            load_scale = LOAD / load_mean
            load_coeff = -(load_scale * disk_wind)[:, None] * loading[column]
            blade_push = (load_coeff[None] * sampled).astype(jnp.bfloat16)
            blade_push = lax.optimization_barrier(blade_push).astype(jnp.float32)
            force_rows = jnp.zeros((3, slot_count, NZ), jnp.float32)
            force_rows = force_rows.at[:, point_slot[column], point_z[column]].add(blade_push)
            force = force.at[:, flat_index, :].add(force_rows)
        velocity = stencil(velocity, force.reshape(3, NX, NY, NZ))
    return velocity
```

```python
import jax
import jax.numpy as jnp
from jax import lax
from jax.experimental import pallas as pl
from jax.experimental.pallas import tpu as pltpu
from jax.sharding import PartitionSpec as P

SPREAD = 0.12
CARRY = 0.25
FREE_WIND = 1.0
LOAD = 0.6

F32 = jnp.float32
BF16 = jnp.bfloat16
NT = (((1,), (1,)), ((), ()))
LANES = 128
OWN = 8
PLANE = 32
EDGE = 24


def iota(shape, axis):
    return lax.broadcasted_iota(jnp.int32, shape, axis)


def rounded(x):
    return x.astype(BF16).astype(F32)


def even(axis):
    return lax.rem(lax.axis_index(axis), 2) == 0


def swap_pairs(count, first):
    pairs = []
    for i in range(first, count - 1, 2):
        pairs += [(i, i + 1), (i + 1, i)]
    return pairs


def swap(x, axis, first):
    return lax.ppermute(x, axis, swap_pairs(lax.axis_size(axis), first))


def call(kernel, name, outs, args, scratch=(), flops=0, nbytes=0):
    return pl.pallas_call(
        kernel,
        out_shape=[jax.ShapeDtypeStruct(s, d) for s, d in outs],
        in_specs=[pl.BlockSpec(memory_space=pltpu.VMEM)] * len(args),
        out_specs=[pl.BlockSpec(memory_space=pltpu.VMEM)] * len(outs),
        scratch_shapes=list(scratch),
        compiler_params=pltpu.CompilerParams(vmem_limit_bytes=40 << 20),
        cost_estimate=pl.CostEstimate(flops=flops, bytes_accessed=nbytes, transcendentals=0),
        name=name,
    )(*args)


def lane_edge(center):
    lane = iota(center.shape, 2)
    last = center.shape[2] - 1
    below = jnp.where(lane == 0, 0.0, pltpu.roll(center, 1, 2))
    above = jnp.where(lane == last, 0.0, pltpu.roll(center, last, 2))
    return below + above


def stencil(ref, c, x0, nx, r0, nr):
    center = ref[c, x0 : x0 + nx, r0 : r0 + nr, :]
    before = ref[c, x0 - 1 : x0 - 1 + nx, r0 : r0 + nr, :]
    after = ref[c, x0 + 1 : x0 + 1 + nx, r0 : r0 + nr, :]
    beside = before + after
    beside = beside + ref[c, x0 : x0 + nx, r0 - 1 : r0 - 1 + nr, :]
    beside = beside + ref[c, x0 : x0 + nx, r0 + 1 : r0 + 1 + nr, :]
    beside = beside + lane_edge(center)
    return center + SPREAD * (beside - 6.0 * center) - CARRY * (center - before)


def pack_y(v, tc, to_even, to_odd):
    comps, nx, ny, _ = v.shape
    ev = even("gy")
    at = 0
    for c in range(comps):
        for k in range(2):
            high = v[c, :, ny - 2 + k, :]
            low = v[c, :, k, :]
            to_even[at : at + nx, :] = jnp.where(ev, high, low)
            to_odd[at : at + nx, :] = jnp.where(ev, low, high)
            at += nx
    cells = tc[0, :, :].astype(F32) + 1.0
    slots = cells.shape[1]
    for out in (to_even, to_odd):
        out[at : at + 8, :] = jnp.zeros((8, LANES), F32)
        out[at : at + 1, 0:slots] = cells


def histogram(v, tc, owner, slot, height, load, count_ref, load_ref, sum_ref, scale_ref, code_ref):
    turbines, points = slot.shape[1:]
    cells, levels = count_ref.shape[1:]
    slots = tc.shape[2]
    first = lax.axis_index("gy") * slots
    cell_row = jnp.broadcast_to((tc[0, :, :].astype(F32) + 1.0).astype(BF16), (8, slots))
    rows = rounded(v[0, :, :, :].reshape(cells, levels))

    def one(t, carry):
        which = slot[0, pl.ds(t, 1), :] - first
        z = height[0, pl.ds(t, 1), :]
        weight = load[0, pl.ds(t, 1), :]
        hit = jnp.where(iota((slots, points), 0) == which, 1.0, 0.0).astype(BF16)
        cell = jnp.dot(cell_row, hit, preferred_element_type=F32)[0:1, :].astype(jnp.int32) - 1
        code_ref[pl.ds(t, 1), :] = jnp.where(cell >= 0, cell * levels + z + 1, 0).astype(F32)
        a = jnp.where(iota((cells, points), 0) == cell, 1.0, 0.0).astype(BF16)
        at_z = iota((levels, points), 0) == z
        high = rounded(weight)
        b = jnp.concatenate(
            [
                jnp.where(at_z, 1.0, 0.0).astype(BF16),
                jnp.where(at_z, high, 0.0).astype(BF16),
                jnp.where(at_z, weight - high, 0.0).astype(BF16),
            ],
            axis=0,
        )
        both = lax.dot_general(a, b, NT, preferred_element_type=F32)
        count = both[:, :levels]
        count_ref[t] = count.astype(BF16)
        load_ref[t] = both[:, levels : 2 * levels] + both[:, 2 * levels :]
        sum_ref[pl.ds(t, 1), :] = jnp.sum(count * rows, axis=0, keepdims=True)
        return carry

    lax.fori_loop(0, turbines, one, 0, unroll=2)
    same = iota((turbines, turbines), 0) == iota((turbines, turbines), 1)
    owner_row = jnp.broadcast_to(owner[...].astype(F32), (turbines, turbines))
    owner_col = jnp.sum(jnp.where(same, owner_row, 0.0), axis=1, keepdims=True)
    member = owner_row == owner_col
    load_col = jnp.sum(load[0, :, :], axis=1, keepdims=True)
    load_row = jnp.sum(jnp.where(same, load_col, 0.0), axis=0, keepdims=True)
    total = jnp.sum(jnp.where(member, load_row, 0.0), axis=1, keepdims=True)
    number = jnp.sum(jnp.where(member, 1.0, 0.0), axis=1, keepdims=True)
    scale_ref[...] = jnp.broadcast_to(LOAD / (total / (number * points)), scale_ref.shape)


def pack_x(v, ye, yo, sums, scale, code, load, to_even, to_odd):
    comps, nx, ny, _ = v.shape
    turbines, points = code.shape
    ev_x, ev_y = even("gx"), even("gy")
    at = 0
    for c in range(comps):
        for k in range(2):
            low_at, high_at = (c * 2 + 1) * nx, (c * 2) * nx
            sides = []
            for x in (nx - 2 + k, k):
                below = jnp.where(ev_y, yo[low_at + x : low_at + x + 1, :], ye[low_at + x : low_at + x + 1, :])
                above = jnp.where(ev_y, ye[high_at + x : high_at + x + 1, :], yo[high_at + x : high_at + x + 1, :])
                sides.append((v[c, x, :, :], below, above))
            (own_r, below_r, above_r), (own_l, below_l, above_l) = sides
            for out, pick in ((to_even, ev_x), (to_odd, jnp.logical_not(ev_x))):
                out[at : at + EDGE, :] = jnp.zeros((EDGE, LANES), F32)
                out[at + 4 : at + 4 + ny, :] = jnp.where(pick, own_r, own_l)
                out[at + 3 : at + 4, :] = jnp.where(pick, below_r, below_l)
                out[at + 4 + ny : at + 5 + ny, :] = jnp.where(pick, above_r, above_l)
            at += EDGE
    parts = [code[:, k : k + LANES] for k in range(0, points, LANES)]
    parts += [load[0, :, k : k + LANES] for k in range(0, points, LANES)]
    parts += [sums[...], scale[...]]
    for part in parts:
        to_even[at : at + turbines, :] = part
        to_odd[at : at + turbines, :] = part
        at += turbines


def picked(flag, a, b, lo, hi):
    return jnp.where(flag, a[lo:hi, :], b[lo:hi, :])


def extend(v, ye, yo, xe, xo, field, comps):
    _, nx, ny, _ = v.shape
    ev_x, ev_y = even("gx"), even("gy")
    for c in comps:
        out = c if len(comps) > 1 else 0
        field[out, 2 : 2 + nx, 0:OWN, :] = jnp.zeros((nx, OWN, LANES), F32)
        field[out, 2 : 2 + nx, OWN + ny : PLANE, :] = jnp.zeros((nx, PLANE - OWN - ny, LANES), F32)
        field[out, 2 : 2 + nx, OWN : OWN + ny, :] = v[c, :, :, :]
        for k in range(2):
            at = (c * 2 + k) * nx
            field[out, 2 : 2 + nx, OWN - 2 + k, :] = picked(ev_y, yo, ye, at, at + nx)
            field[out, 2 : 2 + nx, OWN + ny + k, :] = picked(ev_y, ye, yo, at, at + nx)
            at = (c * 2 + k) * EDGE
            for x, a, b in ((k, xo, xe), (2 + nx + k, xe, xo)):
                field[out, x, 0:OWN, :] = jnp.zeros((OWN, LANES), F32)
                field[out, x, PLANE - OWN : PLANE, :] = jnp.zeros((OWN, LANES), F32)
                field[out, x, 4 : 4 + EDGE, :] = picked(ev_x, a, b, at, at + EDGE)


def reduce_sums(v, ye, yo, xe, xo, counts, loads, sums, out, field, products):
    comps, nx, ny, levels = v.shape
    turbines, cells, _ = counts.shape
    extend(v, ye, yo, xe, xo, field, (0,))
    update = stencil(field, 0, 2, nx, OWN, ny).reshape(cells, levels)
    rows = rounded(v[0, :, :, :].reshape(cells, levels))
    for t in range(turbines):
        products[t] = (rows * loads[t]).astype(BF16)
    products[turbines] = update.astype(BF16)
    block = 16
    wide, more = turbines * block, (turbines + 1) * block
    gram = jnp.zeros((wide, more), F32)
    for b in range(0, cells, block):
        left = counts[:, b : b + block, :].reshape(wide, levels)
        right = products[:, b : b + block, :].reshape(more, levels)
        gram = gram + lax.dot_general(left, right, NT, preferred_element_type=F32)
    keep = (iota((wide, more), 0) & (block - 1)) == (iota((wide, more), 1) & (block - 1))
    gram = jnp.sum(jnp.where(keep, gram, 0.0).reshape(turbines, block, more), axis=1)
    select = jnp.where(iota((more, LANES), 0) // block == iota((more, LANES), 1), 1.0, 0.0)
    result = jnp.dot(gram, select, precision=lax.Precision.HIGHEST, preferred_element_type=F32)
    lane = iota((turbines, LANES), 1)
    ev_x = even("gx")
    at = xe.shape[0] - 2 * turbines
    left_sums = picked(ev_x, xo, xe, at, at + turbines)
    right_sums = picked(ev_x, xe, xo, at, at + turbines)
    for k, part in enumerate((sums[...], left_sums, right_sums)):
        result = jnp.where(lane == turbines + 1 + k, jnp.sum(part, axis=1, keepdims=True), result)
    for k in range(out.shape[0]):
        out[k] = result


def edges(slots, v, slot, height, load, ye, yo, xe, xo, edge_ref, update_ref, field):
    comps, nx, ny, levels = v.shape
    turbines, points = slot.shape[1:]
    shift, level_shift = ny.bit_length() - 1, levels.bit_length() - 1
    ev_x, ev_y = even("gx"), even("gy")
    me = lax.axis_index("gy")
    extend(v, ye, yo, xe, xo, field, tuple(range(comps)))
    for c in range(comps):
        update_ref[c, :, OWN - 1 : OWN + ny + 1, :] = stencil(field, c, 1, nx + 2, OWN - 1, ny + 2)

    at = comps * 2 * nx
    columns = []
    for a, b, row in ((yo, ye, ny - 1), (ye, yo, 0)):
        cell = picked(ev_y, a, b, at, at + 1)[:, :slots].astype(jnp.int32) - 1
        valid = (cell >= 0) & ((cell & (ny - 1)) == row)
        x = jnp.where(valid, (cell >> shift) + 1, 0).astype(F32).astype(BF16)
        columns.append(jnp.broadcast_to(x, (8, slots)))

    pieces = points // LANES
    code_at = comps * 2 * EDGE
    load_at = code_at + pieces * turbines

    def row_of(flag, a, b, base, t):
        rows = [pl.ds(base + k * turbines + t, 1) for k in range(pieces)]
        return jnp.concatenate([jnp.where(flag, a[r, :], b[r, :]) for r in rows], axis=1)

    def spread(where, count, z, weight):
        high = rounded(weight)
        low = weight - high
        at_z = jnp.where(iota((levels, points), 0) == z, 1.0, 0.0).astype(BF16)
        left = []
        for place in where:
            hit = iota((count, points), 0) == place
            left += [jnp.where(hit, high, 0.0).astype(BF16), jnp.where(hit, low, 0.0).astype(BF16)]
        both = lax.dot_general(jnp.concatenate(left, axis=0), at_z, NT, preferred_element_type=F32)
        return [both[2 * k * count : (2 * k + 1) * count] + both[(2 * k + 1) * count : (2 * k + 2) * count] for k in range(len(where))]

    def one(t, carry):
        z = height[0, pl.ds(t, 1), :]
        weight = load[0, pl.ds(t, 1), :]
        where = []
        for k, x in enumerate(columns):
            which = slot[0, pl.ds(t, 1), :] - (me + 2 * k - 1) * slots
            hit = jnp.where(iota((slots, points), 0) == which, 1.0, 0.0).astype(BF16)
            where.append(jnp.dot(x, hit, preferred_element_type=F32)[0:1, :].astype(jnp.int32) - 1)
        edge_ref[2, t], edge_ref[3, t] = spread(where, nx, z, weight)
        for k, (a, b) in enumerate(((xo, xe), (xe, xo))):
            code = row_of(ev_x, a, b, code_at, t).astype(jnp.int32) - 1
            there = row_of(ev_x, a, b, load_at, t)
            place = (code >> level_shift) - (1 - k) * (nx - 1) * ny
            (edge_ref[k, t],) = spread([place], ny, code & (levels - 1), there)
        return carry

    lax.fori_loop(0, turbines, one, 0, unroll=2)


def advance(points, got, v, ye, yo, xe, xo, scale, loads, edge_ref, update_ref, out, field, weights):
    comps, nx, ny, _ = v.shape
    turbines = scale.shape[0]
    ev_x, ev_y = even("gx"), even("gy")
    total = got[0]
    for k in range(1, got.shape[0]):
        total = total + got[k]
    lane = iota((turbines, LANES), 1)

    def column(k):
        return jnp.sum(jnp.where(lane == k, total, 0.0), axis=1, keepdims=True)

    def coefs(scales, sums):
        return -(scales * (FREE_WIND + sums / points))

    scale_at = xe.shape[0] - turbines
    own = coefs(scale[...], column(turbines + 1))
    left = coefs(picked(ev_x, xo, xe, scale_at, scale_at + turbines), column(turbines + 2))
    right = coefs(picked(ev_x, xe, xo, scale_at, scale_at + turbines), column(turbines + 3))
    as_row = jnp.sum(jnp.where(iota((turbines, LANES), 0) == lane, own, 0.0), axis=0, keepdims=True)
    forced = jnp.sum(jnp.where(lane < turbines, total * as_row, 0.0), axis=1, keepdims=True)
    later = coefs(scale[...], column(turbines) + forced)

    for x in range(nx):
        first = jnp.zeros((ny, LANES), F32)
        second = first
        for t in range(turbines):
            part = loads[t, x * ny : (x + 1) * ny, :]
            first = first + own[t : t + 1, :] * part
            second = second + later[t : t + 1, :] * part
        weights[x] = second
        for c in range(comps):
            push = rounded(rounded(v[c, x, :, :]) * first)
            field[c, 1 + x, OWN : OWN + ny, :] = update_ref[c, 1 + x, OWN : OWN + ny, :] + push

    sums = []
    for k, coef in enumerate((left, right, own, own)):
        side = coef[0:1, :] * edge_ref[k, 0]
        for t in range(1, turbines):
            side = side + coef[t : t + 1, :] * edge_ref[k, t]
        sums.append(side)
    ix, iy = lax.axis_index("gx"), lax.axis_index("gy")
    for c in range(comps):
        for k, (a, b, there) in enumerate(((xo, xe, ix > 0), (xe, xo, ix < lax.axis_size("gx") - 1))):
            at = (c * 2 + 1 - k) * EDGE + 4
            x = k * (nx + 1)
            push = rounded(rounded(picked(ev_x, a, b, at, at + ny)) * sums[k])
            moved = update_ref[c, x, OWN : OWN + ny, :] + push
            field[c, x, OWN : OWN + ny, :] = jnp.where(there, moved, 0.0)
        for k, (a, b, there) in enumerate(((yo, ye, iy > 0), (ye, yo, iy < lax.axis_size("gy") - 1))):
            at = (c * 2 + 1 - k) * nx
            y = OWN - 1 + k * (ny + 1)
            push = rounded(rounded(picked(ev_y, a, b, at, at + nx)) * sums[2 + k])
            moved = update_ref[c, 1 : 1 + nx, y, :] + push
            field[c, 1 : 1 + nx, y, :] = jnp.where(there, moved, 0.0)
    for c in range(comps):
        now = field[c, 1 : 1 + nx, OWN : OWN + ny, :]
        out[c] = stencil(field, c, 1, nx, OWN, ny) + rounded(rounded(now) * weights[...])


def body(velocity, tile_cells, owner, point_slot, point_z, loading):
    comps, nx, ny, levels = velocity.shape
    turbines, points = point_slot.shape[1:]
    slots = tile_cells.shape[2]
    cells = nx * ny
    tiles_y = lax.axis_size("gy")
    rows_y = comps * 2 * nx + 8
    rows_x = comps * 2 * EDGE + 2 * (points // LANES) * turbines + 2 * turbines

    def field(n, planes):
        return pltpu.VMEM((n, planes, PLANE, levels), F32)

    y_even, y_odd = call(pack_y, "pack_y", [((rows_y, levels), F32)] * 2, (velocity, tile_cells))
    ye, yo = swap(y_even, "gy", 0), swap(y_odd, "gy", 1)
    counts, loads, sums, scale, code = call(
        histogram,
        "histogram",
        [
            ((turbines, cells, levels), BF16),
            ((turbines, cells, levels), F32),
            ((turbines, levels), F32),
            ((turbines, levels), F32),
            ((turbines, points), F32),
        ],
        (velocity, tile_cells, owner, point_slot, point_z, loading),
        flops=6 * turbines * cells * points * levels,
        nbytes=4 << 20,
    )
    x_even, x_odd = call(
        pack_x, "pack_x", [((rows_x, levels), F32)] * 2, (velocity, ye, yo, sums, scale, code, loading)
    )
    xe, xo = swap(x_even, "gx", 0), swap(x_odd, "gx", 1)
    (chunk,) = call(
        reduce_sums,
        "reduce_sums",
        [((tiles_y, turbines, LANES), F32)],
        (velocity, ye, yo, xe, xo, counts, loads, sums),
        [field(1, nx + 4), pltpu.VMEM((turbines + 1, cells, levels), BF16)],
    )
    got = lax.all_to_all(chunk, "gy", 0, 0)

    def edges_of(*args):
        return edges(slots, *args)

    edge, update = call(
        edges_of,
        "edges",
        [((4, turbines, nx, levels), F32), ((comps, nx + 2, PLANE, levels), F32)],
        (velocity, point_slot, point_z, loading, ye, yo, xe, xo),
        [field(comps, nx + 4)],
        flops=6 * turbines * cells * points * levels,
        nbytes=4 << 20,
    )

    def advance_by(*args):
        return advance(points, *args)

    (out,) = call(
        advance_by,
        "advance",
        [(velocity.shape, F32)],
        (got, velocity, ye, yo, xe, xo, scale, loads, edge, update),
        [field(comps, nx + 2), pltpu.VMEM((nx, ny, levels), F32)],
    )
    return out


def solution(mesh):
    in_specs = (
        P(None, "gx", "gy", None),
        P("gx", "gy", None),
        P("gx", None),
        P("gx", None, None),
        P("gx", None, None),
        P("gx", None, None),
    )
    out_specs = P(None, "gx", "gy", None)
    return jax.shard_map(body, mesh=mesh, in_specs=in_specs, out_specs=out_specs, check_vma=False)
```

```python
import jax
import jax.numpy as jnp
from jax import lax
from jax.experimental import pallas as pl
from jax.experimental.pallas import tpu as pltpu
from jax.sharding import PartitionSpec as P

SPREAD = 0.12
CARRY = 0.25
FREE_WIND = 1.0
LOAD = 0.6

F32 = jnp.float32
BF16 = jnp.bfloat16
NT = (((1,), (1,)), ((), ()))
LANES = 128
OWN = 8
PLANE = 32
EDGE = 24


def iota(shape, axis):
    return lax.broadcasted_iota(jnp.int32, shape, axis)


def rounded(x):
    return x.astype(BF16).astype(F32)


def one_hot(count, row):
    places = iota((count, row.shape[1]), 0).astype(BF16)
    return places == row.astype(BF16)


def ones_at(mask):
    return jnp.where(mask, jnp.ones((), BF16), jnp.zeros((), BF16))


def pick_slots(tc, cells):
    slots = tc.shape[2]
    row = jnp.broadcast_to(tc[0, :, :].astype(F32), (slots, slots))
    same = iota((slots, slots), 0) == iota((slots, slots), 1)
    column = jnp.sum(jnp.where(same, row, 0.0), axis=1, keepdims=True).astype(jnp.int32)
    return jnp.where(iota((slots, cells), 1) == column, 1.0, 0.0).astype(BF16)


def even(axis):
    return lax.rem(lax.axis_index(axis), 2) == 0


def swap_pairs(count, first):
    pairs = []
    for i in range(first, count - 1, 2):
        pairs += [(i, i + 1), (i + 1, i)]
    return pairs


def swap(x, axis, first):
    return lax.ppermute(x, axis, swap_pairs(lax.axis_size(axis), first))


def call(kernel, name, outs, args, scratch=(), flops=0, nbytes=0, space=pltpu.VMEM):
    return pl.pallas_call(
        kernel,
        out_shape=[jax.ShapeDtypeStruct(s, d) for s, d in outs],
        in_specs=[pl.BlockSpec(memory_space=space)] * len(args),
        out_specs=[pl.BlockSpec(memory_space=pltpu.VMEM)] * len(outs),
        scratch_shapes=list(scratch),
        compiler_params=pltpu.CompilerParams(vmem_limit_bytes=16 << 20),
        cost_estimate=pl.CostEstimate(flops=flops, bytes_accessed=nbytes, transcendentals=0),
        name=name,
    )(*args)


def lane_edge(center):
    lane = iota(center.shape, 2)
    last = center.shape[2] - 1
    below = jnp.where(lane == 0, 0.0, pltpu.roll(center, 1, 2))
    above = jnp.where(lane == last, 0.0, pltpu.roll(center, last, 2))
    return below + above


def stencil(ref, c, x0, nx, r0, nr):
    center = ref[c, x0 : x0 + nx, r0 : r0 + nr, :]
    before = ref[c, x0 - 1 : x0 - 1 + nx, r0 : r0 + nr, :]
    after = ref[c, x0 + 1 : x0 + 1 + nx, r0 : r0 + nr, :]
    beside = before + after
    beside = beside + ref[c, x0 : x0 + nx, r0 - 1 : r0 - 1 + nr, :]
    beside = beside + ref[c, x0 : x0 + nx, r0 + 1 : r0 + 1 + nr, :]
    beside = beside + lane_edge(center)
    return center + SPREAD * (beside - 6.0 * center) - CARRY * (center - before)


def stage(v_hbm, tc_hbm, owner_hbm, slot_hbm, height_hbm, load_hbm, v, tc, owner, slot, height, load, to_even, to_odd, sems):
    pairs = ((v_hbm, v), (tc_hbm, tc), (slot_hbm, slot), (height_hbm, height), (load_hbm, load), (owner_hbm, owner))
    copies = [pltpu.make_async_copy(a, b, sems.at[i]) for i, (a, b) in enumerate(pairs)]
    for copy in copies:
        copy.start()
    copies[0].wait()
    comps, nx, ny, _ = v.shape
    ev = even("gy")
    at = 0
    for c in range(comps):
        for k in range(2):
            high = v[c, :, ny - 2 + k, :]
            low = v[c, :, k, :]
            to_even[at : at + nx, :] = jnp.where(ev, high, low)
            to_odd[at : at + nx, :] = jnp.where(ev, low, high)
            at += nx
    copies[1].wait()
    cells = tc[0, :, :].astype(F32) + 1.0
    slots = cells.shape[1]
    for out in (to_even, to_odd):
        out[at : at + 8, :] = jnp.zeros((8, LANES), F32)
        out[at : at + 1, 0:slots] = cells
    for copy in copies[2:]:
        copy.wait()


def histogram(v, tc, owner, slot, height, load, count_ref, load_ref, sum_ref, scale_ref, code_ref):
    _, turbines, points = slot.shape
    slots, levels = count_ref.shape[1:]
    cells = v.shape[1] * v.shape[2]
    first = lax.axis_index("gy") * slots
    values = v[0, :, :, :].reshape(cells, levels).astype(BF16)
    rows = jnp.dot(pick_slots(tc, cells), values, preferred_element_type=F32)
    local = slot[0, :, :] - first
    inside = (local >= 0) & (local < slots)
    code_ref[...] = jnp.where(inside, local * levels + height[0, :, :] + 1, 0).astype(F32)
    zero = jnp.zeros((), BF16)
    for t in range(turbines):
        a = ones_at(one_hot(slots, slot[0, t : t + 1, :] - first))
        at_z = one_hot(levels, height[0, t : t + 1, :])
        weight = load[0, t : t + 1, :]
        high = weight.astype(BF16)
        low = (weight - high.astype(F32)).astype(BF16)
        b = jnp.concatenate([ones_at(at_z), jnp.where(at_z, high, zero), jnp.where(at_z, low, zero)], axis=0)
        both = lax.dot_general(a, b, NT, preferred_element_type=F32)
        count = both[:, :levels]
        count_ref[t] = count.astype(BF16)
        load_ref[t] = both[:, levels : 2 * levels] + both[:, 2 * levels :]
        sum_ref[t : t + 1, :] = jnp.sum(count * rows, axis=0, keepdims=True)
    same = iota((turbines, turbines), 0) == iota((turbines, turbines), 1)
    owner_row = jnp.broadcast_to(owner[...].astype(F32), (turbines, turbines))
    owner_col = jnp.sum(jnp.where(same, owner_row, 0.0), axis=1, keepdims=True)
    member = owner_row == owner_col
    load_col = jnp.sum(load[0, :, :], axis=1, keepdims=True)
    load_row = jnp.sum(jnp.where(same, load_col, 0.0), axis=0, keepdims=True)
    total = jnp.sum(jnp.where(member, load_row, 0.0), axis=1, keepdims=True)
    number = jnp.sum(jnp.where(member, 1.0, 0.0), axis=1, keepdims=True)
    scale_ref[...] = jnp.broadcast_to(LOAD / (total / (number * points)), scale_ref.shape)


def pack_x(v, tc, ye, yo, sums, scale, code, load, to_even, to_odd):
    comps, nx, ny, _ = v.shape
    turbines, points = code.shape
    ev_x, ev_y = even("gx"), even("gy")
    at = 0
    for c in range(comps):
        for k in range(2):
            low_at, high_at = (c * 2 + 1) * nx, (c * 2) * nx
            sides = []
            for x in (nx - 2 + k, k):
                below = picked(ev_y, yo, ye, low_at + x, low_at + x + 1)
                above = picked(ev_y, ye, yo, high_at + x, high_at + x + 1)
                sides.append((v[c, x, :, :], below, above))
            (own_r, below_r, above_r), (own_l, below_l, above_l) = sides
            for out, pick in ((to_even, ev_x), (to_odd, jnp.logical_not(ev_x))):
                out[at : at + EDGE, :] = jnp.zeros((EDGE, LANES), F32)
                out[at + 4 : at + 4 + ny, :] = jnp.where(pick, own_r, own_l)
                out[at + 3 : at + 4, :] = jnp.where(pick, below_r, below_l)
                out[at + 4 + ny : at + 5 + ny, :] = jnp.where(pick, above_r, above_l)
            at += EDGE
    parts = [code[:, k : k + LANES] for k in range(0, points, LANES)]
    parts += [load[0, :, k : k + LANES] for k in range(0, points, LANES)]
    parts += [sums[...], scale[...]]
    cells = tc[0, :, :].astype(F32) + 1.0
    for out in (to_even, to_odd):
        end = at
        for part in parts:
            out[end : end + turbines, :] = part
            end += turbines
        out[end : end + 8, :] = jnp.zeros((8, LANES), F32)
        out[end : end + 1, 0 : cells.shape[1]] = cells


def picked(flag, a, b, lo, hi):
    return jnp.where(flag, a[lo:hi, :], b[lo:hi, :])


def extend(v, ye, yo, xe, xo, field, comps):
    _, nx, ny, _ = v.shape
    ev_x, ev_y = even("gx"), even("gy")
    for c in comps:
        out = c if len(comps) > 1 else 0
        field[out, 2 : 2 + nx, 0:OWN, :] = jnp.zeros((nx, OWN, LANES), F32)
        field[out, 2 : 2 + nx, OWN + ny : PLANE, :] = jnp.zeros((nx, PLANE - OWN - ny, LANES), F32)
        field[out, 2 : 2 + nx, OWN : OWN + ny, :] = v[c, :, :, :]
        for k in range(2):
            at = (c * 2 + k) * nx
            field[out, 2 : 2 + nx, OWN - 2 + k, :] = picked(ev_y, yo, ye, at, at + nx)
            field[out, 2 : 2 + nx, OWN + ny + k, :] = picked(ev_y, ye, yo, at, at + nx)
            at = (c * 2 + k) * EDGE
            for x, a, b in ((k, xo, xe), (2 + nx + k, xe, xo)):
                field[out, x, 0:OWN, :] = jnp.zeros((OWN, LANES), F32)
                field[out, x, PLANE - OWN : PLANE, :] = jnp.zeros((OWN, LANES), F32)
                field[out, x, 4 : 4 + EDGE, :] = picked(ev_x, a, b, at, at + EDGE)


def reduce_sums(v, tc, ye, yo, xe, xo, counts, loads, sums, out, field, products):
    _, nx, ny, levels = v.shape
    turbines, slots, _ = counts.shape
    cells = nx * ny
    extend(v, ye, yo, xe, xo, field, (0,))
    update = stencil(field, 0, 2, nx, OWN, ny).reshape(cells, levels).astype(BF16)
    values = v[0, :, :, :].reshape(cells, levels).astype(BF16)
    pair = jnp.concatenate([values, update], axis=1)
    rows = jnp.dot(pick_slots(tc, cells), pair, preferred_element_type=F32)
    products[turbines] = rows[:, levels:].astype(BF16)
    rows = rows[:, :levels]
    for t in range(turbines):
        products[t] = (rows * loads[t]).astype(BF16)
    block = 16
    wide, more = turbines * block, (turbines + 1) * block
    gram = jnp.zeros((wide, more), F32)
    for b in range(0, slots, block):
        left = counts[:, b : b + block, :].reshape(wide, levels)
        right = products[:, b : b + block, :].reshape(more, levels)
        gram = gram + lax.dot_general(left, right, NT, preferred_element_type=F32)
    keep = (iota((wide, more), 0) & (block - 1)) == (iota((wide, more), 1) & (block - 1))
    gram = jnp.sum(jnp.where(keep, gram, 0.0).reshape(turbines, block, more), axis=1)
    select = jnp.where(iota((more, LANES), 0) // block == iota((more, LANES), 1), 1.0, 0.0)
    result = jnp.dot(gram, select, precision=lax.Precision.HIGHEST, preferred_element_type=F32)
    lane = iota((turbines, LANES), 1)
    ev_x = even("gx")
    at = xe.shape[0] - 8 - 2 * turbines
    left_sums = picked(ev_x, xo, xe, at, at + turbines)
    right_sums = picked(ev_x, xe, xo, at, at + turbines)
    for k, part in enumerate((sums[...], left_sums, right_sums)):
        result = jnp.where(lane == turbines + 1 + k, jnp.sum(part, axis=1, keepdims=True), result)
    for k in range(out.shape[0]):
        out[k] = result


def spread(wheres, hits, z, weight):
    high = weight.astype(BF16)
    low = (weight - high.astype(F32)).astype(BF16)
    at_z = ones_at(one_hot(LANES, z))
    left = []
    for where, hit in zip(wheres, hits):
        place = jnp.dot(where, hit, preferred_element_type=F32).astype(BF16)
        left += [place * high, place * low]
    both = lax.dot_general(jnp.concatenate(left, axis=0), at_z, NT, preferred_element_type=F32)
    n = wheres[0].shape[0]
    return [both[2 * k * n : (2 * k + 1) * n] + both[(2 * k + 1) * n : (2 * k + 2) * n] for k in range(len(wheres))]


def edges_y(slots, nx, ny, slot, height, load, ye, yo, edge_ref):
    turbines = slot.shape[1]
    ev = even("gy")
    me = lax.axis_index("gy")
    at = ye.shape[0] - 8
    wheres = []
    for a, b, y in ((yo, ye, ny - 1), (ye, yo, 0)):
        cell = picked(ev, a, b, at, at + 1)[:, :slots].astype(jnp.int32) - 1
        wheres.append(jnp.where(iota((nx, slots), 0) * ny + y == cell, 1.0, 0.0).astype(BF16))
    for t in range(turbines):
        row = slot[0, t : t + 1, :]
        hits = [ones_at(one_hot(slots, row - (me + k) * slots)) for k in (-1, 1)]
        edge_ref[0, t], edge_ref[1, t] = spread(wheres, hits, height[0, t : t + 1, :], load[0, t : t + 1, :])


def edges_x(slots, pieces, v, ye, yo, xe, xo, edge_ref, update_ref, field):
    comps, nx, ny, levels = v.shape
    turbines = edge_ref.shape[1]
    ev = even("gx")
    extend(v, ye, yo, xe, xo, field, tuple(range(comps)))
    for c in range(comps):
        update_ref[c, :, OWN - 1 : OWN + ny + 1, :] = stencil(field, c, 1, nx + 2, OWN - 1, ny + 2)

    at = xe.shape[0] - 8
    code_at = comps * 2 * EDGE
    load_at = code_at + pieces * turbines
    shift = levels.bit_length() - 1
    for k, (a, b) in enumerate(((xo, xe), (xe, xo))):
        cell = picked(ev, a, b, at, at + 1)[:, :slots].astype(jnp.int32) - 1
        where = jnp.where(iota((ny, slots), 0) + (1 - k) * (nx - 1) * ny == cell, 1.0, 0.0).astype(BF16)
        codes = [picked(ev, a, b, code_at + i * turbines, code_at + (i + 1) * turbines) for i in range(pieces)]
        codes = jnp.concatenate(codes, axis=1).astype(jnp.int32) - 1
        there = [picked(ev, a, b, load_at + i * turbines, load_at + (i + 1) * turbines) for i in range(pieces)]
        there = jnp.concatenate(there, axis=1)
        for t in range(turbines):
            code = codes[t : t + 1, :]
            hit = ones_at(one_hot(slots, code >> shift))
            (edge_ref[k, t],) = spread([where], [hit], code & (levels - 1), there[t : t + 1, :])


def advance(points, got, v, tc, ye, yo, xe, xo, scale, loads, edge_x, edge_y, update_ref, out, field, parts):
    comps, nx, ny, levels = v.shape
    turbines, slots, _ = loads.shape
    cells = nx * ny
    ev_x, ev_y = even("gx"), even("gy")
    total = got[0]
    for k in range(1, got.shape[0]):
        total = total + got[k]
    lane = iota((turbines, LANES), 1)

    def column(k):
        return jnp.sum(jnp.where(lane == k, total, 0.0), axis=1, keepdims=True)

    def coefs(scales, sums):
        return -(scales * (FREE_WIND + sums / points))

    scale_at = xe.shape[0] - 8 - turbines
    own = coefs(scale[...], column(turbines + 1))
    left = coefs(picked(ev_x, xo, xe, scale_at, scale_at + turbines), column(turbines + 2))
    right = coefs(picked(ev_x, xe, xo, scale_at, scale_at + turbines), column(turbines + 3))
    as_row = jnp.sum(jnp.where(iota((turbines, LANES), 0) == lane, own, 0.0), axis=0, keepdims=True)
    forced = jnp.sum(jnp.where(lane < turbines, total * as_row, 0.0), axis=1, keepdims=True)
    later = coefs(scale[...], column(turbines) + forced)

    for s in range(0, slots, 16):
        first = jnp.zeros((16, levels), F32)
        second = first
        for t in range(turbines):
            part = loads[t, s : s + 16, :]
            first = first + own[t : t + 1, :] * part
            second = second + later[t : t + 1, :] * part
        for i, rest in enumerate((first, second)):
            for k in range(3):
                piece = rest.astype(BF16)
                rest = rest - piece.astype(F32)
                at = (3 * i + k) * levels
                parts[s : s + 16, at : at + levels] = piece
    row = tc[0, :, :]
    put = jnp.where(iota((cells, slots), 0) == row, 1.0, 0.0).astype(BF16)
    spread_out = jnp.dot(put, parts[...], preferred_element_type=F32)
    pieces = [spread_out[:, k * levels : (k + 1) * levels] for k in range(6)]
    first = ((pieces[0] + pieces[1]) + pieces[2]).reshape(nx, ny, levels)
    second = ((pieces[3] + pieces[4]) + pieces[5]).reshape(nx, ny, levels)
    for c in range(comps):
        push = rounded(rounded(v[c, :, :, :]) * first)
        field[c, 1 : 1 + nx, OWN : OWN + ny, :] = update_ref[c, 1 : 1 + nx, OWN : OWN + ny, :] + push

    sums = []
    for edge, coef in ((edge_x.at[0], left), (edge_x.at[1], right), (edge_y.at[0], own), (edge_y.at[1], own)):
        side = coef[0:1, :] * edge[0]
        for t in range(1, turbines):
            side = side + coef[t : t + 1, :] * edge[t]
        sums.append(side)
    ix, iy = lax.axis_index("gx"), lax.axis_index("gy")
    for c in range(comps):
        for k, (a, b, there) in enumerate(((xo, xe, ix > 0), (xe, xo, ix < lax.axis_size("gx") - 1))):
            at = (c * 2 + 1 - k) * EDGE + 4
            x = k * (nx + 1)
            push = rounded(rounded(picked(ev_x, a, b, at, at + ny)) * sums[k])
            moved = update_ref[c, x, OWN : OWN + ny, :] + push
            field[c, x, OWN : OWN + ny, :] = jnp.where(there, moved, 0.0)
        for k, (a, b, there) in enumerate(((yo, ye, iy > 0), (ye, yo, iy < lax.axis_size("gy") - 1))):
            at = (c * 2 + 1 - k) * nx
            y = OWN - 1 + k * (ny + 1)
            push = rounded(rounded(picked(ev_y, a, b, at, at + nx)) * sums[2 + k])
            moved = update_ref[c, 1 : 1 + nx, y, :] + push
            field[c, 1 : 1 + nx, y, :] = jnp.where(there, moved, 0.0)
    for c in range(comps):
        now = field[c, 1 : 1 + nx, OWN : OWN + ny, :]
        out[c] = stencil(field, c, 1, nx, OWN, ny) + rounded(rounded(now) * second)


def body(velocity, tile_cells, owner, point_slot, point_z, loading):
    comps, nx, ny, levels = velocity.shape
    _, turbines, points = point_slot.shape
    slots = tile_cells.shape[2]
    tiles_y = lax.axis_size("gy")
    pieces = points // LANES
    rows_y = comps * 2 * nx + 8
    rows_x = comps * 2 * EDGE + 2 * pieces * turbines + 2 * turbines + 8
    args = (velocity, tile_cells, owner, point_slot, point_z, loading)
    work = {"flops": 2 * turbines * slots * points * levels, "nbytes": 1 << 20}

    def field(n, planes):
        return pltpu.VMEM((n, planes, PLANE, levels), F32)

    v, tc, own, slot, height, load, y_even, y_odd = call(
        stage,
        "stage",
        [(x.shape, x.dtype) for x in args] + [((rows_y, levels), F32)] * 2,
        args,
        [pltpu.SemaphoreType.DMA((len(args),))],
        space=pltpu.HBM,
    )
    ye, yo = swap(y_even, "gy", 0), swap(y_odd, "gy", 1)
    counts, loads, sums, scale, code = call(
        histogram,
        "histogram",
        [
            ((turbines, slots, levels), BF16),
            ((turbines, slots, levels), F32),
            ((turbines, levels), F32),
            ((turbines, levels), F32),
            ((turbines, points), F32),
        ],
        (v, tc, own, slot, height, load),
        **work,
    )
    x_even, x_odd = call(
        pack_x, "pack_x", [((rows_x, levels), F32)] * 2, (v, tc, ye, yo, sums, scale, code, load)
    )
    xe, xo = swap(x_even, "gx", 0), swap(x_odd, "gx", 1)

    def edges_y_of(*refs):
        return edges_y(slots, nx, ny, *refs)

    (edge_y,) = call(
        edges_y_of, "edges_y", [((2, turbines, nx, levels), F32)], (slot, height, load, ye, yo), **work
    )
    (chunk,) = call(
        reduce_sums,
        "reduce_sums",
        [((tiles_y, turbines, LANES), F32)],
        (v, tc, ye, yo, xe, xo, counts, loads, sums),
        [field(1, nx + 4), pltpu.VMEM((turbines + 1, slots, levels), BF16)],
    )
    got = lax.all_to_all(chunk, "gy", 0, 0)

    def edges_x_of(*refs):
        return edges_x(slots, pieces, *refs)

    edge_x, update = call(
        edges_x_of,
        "edges_x",
        [((2, turbines, ny, levels), F32), ((comps, nx + 2, PLANE, levels), F32)],
        (v, ye, yo, xe, xo),
        [field(comps, nx + 4)],
        **work,
    )

    def advance_by(*refs):
        return advance(points, *refs)

    (out,) = call(
        advance_by,
        "advance",
        [(velocity.shape, F32)],
        (got, v, tc, ye, yo, xe, xo, scale, loads, edge_x, edge_y, update),
        [field(comps, nx + 2), pltpu.VMEM((slots, 6 * levels), BF16)],
    )
    return out


def solution(mesh):
    in_specs = (
        P(None, "gx", "gy", None),
        P("gx", "gy", None),
        P("gx", None),
        P("gx", None, None),
        P("gx", None, None),
        P("gx", None, None),
    )
    out_specs = P(None, "gx", "gy", None)
    return jax.shard_map(body, mesh=mesh, in_specs=in_specs, out_specs=out_specs, check_vma=False)
```

```python
import jax
import jax.numpy as jnp
from jax import lax
from jax.experimental import pallas as pl
from jax.experimental.pallas import tpu as pltpu
from jax.sharding import PartitionSpec as P

SPREAD = 0.12
CARRY = 0.25
FREE_WIND = 1.0
LOAD = 0.6

F32 = jnp.float32
BF16 = jnp.bfloat16
NT = (((1,), (1,)), ((), ()))
LANES = 128
OWN = 8
PLANE = 32
SUMS, SCALE, CELLS = 0, 1, 2


def iota(shape, axis):
    return lax.broadcasted_iota(jnp.int32, shape, axis)


def rounded(x):
    return x.astype(BF16).astype(F32)


def one_hot(count, row):
    places = iota((count, row.shape[1]), 0).astype(BF16)
    return places == row.astype(BF16)


def ones_at(mask):
    return jnp.where(mask, jnp.ones((), BF16), jnp.zeros((), BF16))


def pick_slots(tc, cells):
    slots = tc.shape[2]
    row = jnp.broadcast_to(tc[0, :, :].astype(F32), (slots, slots))
    same = iota((slots, slots), 0) == iota((slots, slots), 1)
    column = jnp.sum(jnp.where(same, row, 0.0), axis=1, keepdims=True).astype(jnp.int32)
    return jnp.where(iota((slots, cells), 1) == column, 1.0, 0.0).astype(BF16)


def even(axis):
    return lax.rem(lax.axis_index(axis), 2) == 0


def swap_pairs(count, first):
    pairs = []
    for i in range(first, count - 1, 2):
        pairs += [(i, i + 1), (i + 1, i)]
    return pairs


def swap(x, axis, first):
    return lax.ppermute(x, axis, swap_pairs(lax.axis_size(axis), first))


def call(kernel, name, outs, args, scratch=(), flops=0, nbytes=0, space=pltpu.VMEM):
    return pl.pallas_call(
        kernel,
        out_shape=[jax.ShapeDtypeStruct(s, d) for s, d in outs],
        in_specs=[pl.BlockSpec(memory_space=space)] * len(args),
        out_specs=[pl.BlockSpec(memory_space=pltpu.VMEM)] * len(outs),
        scratch_shapes=list(scratch),
        compiler_params=pltpu.CompilerParams(vmem_limit_bytes=16 << 20),
        cost_estimate=pl.CostEstimate(flops=flops, bytes_accessed=nbytes, transcendentals=0),
        name=name,
    )(*(pltpu.with_memory_space_constraint(a, space) if space is pltpu.HBM else a for a in args))


def lane_edge(center):
    axis = center.ndim - 1
    lane = iota(center.shape, axis)
    last = center.shape[axis] - 1
    below = jnp.where(lane == 0, 0.0, pltpu.roll(center, 1, axis))
    above = jnp.where(lane == last, 0.0, pltpu.roll(center, last, axis))
    return below + above


def moved(center, before, after, beside):
    beside = beside + before + after
    return center + SPREAD * (beside - 6.0 * center) - CARRY * (center - before)


def stencil(ref, c, x0, nx, ny):
    center = ref[c, x0 : x0 + nx, OWN : OWN + ny, :]
    before = ref[c, x0 - 1 : x0 - 1 + nx, OWN : OWN + ny, :]
    after = ref[c, x0 + 1 : x0 + 1 + nx, OWN : OWN + ny, :]
    beside = ref[c, x0 : x0 + nx, OWN - 1 : OWN - 1 + ny, :] + ref[c, x0 : x0 + nx, OWN + 1 : OWN + 1 + ny, :]
    return moved(center, before, after, beside + lane_edge(center))


def stage(v_hbm, tc_hbm, owner_hbm, slot_hbm, height_hbm, load_hbm, v, tc, owner, slot, height, load, to_even, to_odd, sems):
    pairs = ((v_hbm, v), (tc_hbm, tc), (slot_hbm, slot), (height_hbm, height), (load_hbm, load), (owner_hbm, owner))
    copies = [pltpu.make_async_copy(a, b, sems.at[i]) for i, (a, b) in enumerate(pairs)]
    for copy in copies:
        copy.start()
    copies[0].wait()
    comps, nx, ny, _ = v.shape
    ev = even("gy")
    at = 0
    for c in range(comps):
        for k in range(2):
            high = v[c, :, ny - 2 + k, :]
            low = v[c, :, k, :]
            to_even[at : at + nx, :] = jnp.where(ev, high, low)
            to_odd[at : at + nx, :] = jnp.where(ev, low, high)
            at += nx
    copies[1].wait()
    cells = tc[0, :, :].astype(F32) + 1.0
    slots = cells.shape[1]
    for out in (to_even, to_odd):
        out[at : at + 8, :] = jnp.zeros((8, LANES), F32)
        out[at : at + 1, 0:slots] = cells
    for copy in copies[2:]:
        copy.wait()


def as_column(row, n):
    same = iota((n, n), 0) == iota((n, n), 1)
    return jnp.sum(jnp.where(same, row, 0.0), axis=1, keepdims=True)


def as_row(column, n):
    same = iota((n, n), 0) == iota((n, n), 1)
    return jnp.sum(jnp.where(same, column, 0.0), axis=0, keepdims=True)


def picked(flag, a, b, lo, hi):
    return jnp.where(flag, a[lo:hi, :], b[lo:hi, :])


def histogram(v, tc, owner, slot, height, load, count_ref, load_ref, line, to_even, to_odd, sum_ref):
    _, turbines, points = slot.shape
    slots, levels = count_ref.shape[1:]
    comps, nx, ny, _ = v.shape
    cells = nx * ny
    first = lax.axis_index("gy") * slots
    values = v[0, :, :, :].reshape(cells, levels).astype(BF16)
    rows = jnp.dot(pick_slots(tc, cells), values, preferred_element_type=F32)
    zero = jnp.zeros((), BF16)
    for t in range(turbines):
        a = ones_at(one_hot(slots, slot[0, t : t + 1, :] - first))
        at_z = one_hot(levels, height[0, t : t + 1, :])
        weight = load[0, t : t + 1, :]
        high = weight.astype(BF16)
        low = (weight - high.astype(F32)).astype(BF16)
        b = jnp.concatenate([ones_at(at_z), jnp.where(at_z, high, zero), jnp.where(at_z, low, zero)], axis=0)
        both = lax.dot_general(a, b, NT, preferred_element_type=F32)
        count = both[:, :levels]
        count_ref[t] = count.astype(BF16)
        load_ref[t] = both[:, levels : 2 * levels] + both[:, 2 * levels :]
        sum_ref[t : t + 1, :] = jnp.sum(count * rows, axis=0, keepdims=True)

    owner_row = jnp.broadcast_to(owner[...].astype(F32), (turbines, turbines))
    member = owner_row == as_column(owner_row, turbines)
    load_row = as_row(jnp.sum(load[0, :, :], axis=1, keepdims=True), turbines)
    total = jnp.sum(jnp.where(member, load_row, 0.0), axis=1, keepdims=True)
    number = jnp.sum(jnp.where(member, 1.0, 0.0), axis=1, keepdims=True)
    line[...] = jnp.zeros((8, LANES), F32)
    line[SUMS : SUMS + 1, 0:turbines] = as_row(jnp.sum(sum_ref[...], axis=1, keepdims=True), turbines)
    line[SCALE : SCALE + 1, 0:turbines] = as_row(LOAD / (total / (number * points)), turbines)
    line[CELLS : CELLS + 1, 0:slots] = tc[0, :, :].astype(F32) + 1.0

    local = slot[0, :, :] - first
    inside = (local >= 0) & (local < slots)
    code = jnp.where(inside, local * levels + height[0, :, :] + 1, 0).astype(F32)
    ev = even("gx")
    at = 0
    for c in range(comps):
        for k in range(2):
            right, left = v[c, nx - 2 + k, :, :], v[c, k, :, :]
            to_even[at : at + ny, :] = jnp.where(ev, right, left)
            to_odd[at : at + ny, :] = jnp.where(ev, left, right)
            at += ny
    for part in (code, load[0, :, :]):
        for k in range(0, points, LANES):
            for out in (to_even, to_odd):
                out[at : at + turbines, :] = part[:, k : k + LANES]
            at += turbines
    for out in (to_even, to_odd):
        out[at : at + 8, :] = line[...]


def extend(v, ye, yo, xe, xo, field, comps):
    _, nx, ny, _ = v.shape
    ev_x, ev_y = even("gx"), even("gy")
    for c in comps:
        out = c if len(comps) > 1 else 0
        field[out, 2 : 2 + nx, OWN : OWN + ny, :] = v[c, :, :, :]
        for k in range(2):
            at = (c * 2 + k) * nx
            field[out, 2 : 2 + nx, OWN - 2 + k, :] = picked(ev_y, yo, ye, at, at + nx)
            field[out, 2 : 2 + nx, OWN + ny + k, :] = picked(ev_y, ye, yo, at, at + nx)
            at = (c * 2 + k) * ny
            for x, a, b in ((k, xo, xe), (2 + nx + k, xe, xo)):
                field[out, x, 0:OWN, :] = jnp.zeros((OWN, LANES), F32)
                field[out, x, OWN + ny : PLANE, :] = jnp.zeros((PLANE - OWN - ny, LANES), F32)
                field[out, x, OWN : OWN + ny, :] = picked(ev_x, a, b, at, at + ny)


def spread(wheres, hits, z, weight):
    high = weight.astype(BF16)
    low = (weight - high.astype(F32)).astype(BF16)
    at_z = ones_at(one_hot(LANES, z))
    left = []
    for where, hit in zip(wheres, hits):
        place = jnp.dot(where, hit, preferred_element_type=F32).astype(BF16)
        left += [place * high, place * low]
    both = lax.dot_general(jnp.concatenate(left, axis=0), at_z, NT, preferred_element_type=F32)
    n = wheres[0].shape[0]
    return [both[2 * k * n : (2 * k + 1) * n] + both[(2 * k + 1) * n : (2 * k + 2) * n] for k in range(len(wheres))]


def beside(v, tc, slot, height, load, ye, yo, counts, loads, edge_ref, couple, products):
    _, turbines, slots, levels = (0,) + counts.shape
    _, nx, ny, _ = v.shape
    cells = nx * ny
    rows = jnp.dot(
        pick_slots(tc, cells), v[0, :, :, :].reshape(cells, levels).astype(BF16), preferred_element_type=F32
    )
    for t in range(turbines):
        products[t] = (rows * loads[t]).astype(BF16)
    block = 16
    wide = turbines * block
    gram = jnp.zeros((wide, wide), F32)
    for b in range(0, slots, block):
        left = counts[:, b : b + block, :].reshape(wide, levels)
        right = products[:, b : b + block, :].reshape(wide, levels)
        gram = gram + lax.dot_general(left, right, NT, preferred_element_type=F32)
    keep = (iota((wide, wide), 0) & (block - 1)) == (iota((wide, wide), 1) & (block - 1))
    gram = jnp.sum(jnp.where(keep, gram, 0.0).reshape(turbines, block, wide), axis=1)
    select = jnp.where(iota((wide, LANES), 0) // block == iota((wide, LANES), 1), 1.0, 0.0)
    couple[...] = jnp.dot(gram, select, precision=lax.Precision.HIGHEST, preferred_element_type=F32)

    ev = even("gy")
    me = lax.axis_index("gy")
    at = ye.shape[0] - 8
    wheres = []
    for a, b, y in ((yo, ye, ny - 1), (ye, yo, 0)):
        cell = picked(ev, a, b, at, at + 1)[:, :slots].astype(jnp.int32) - 1
        wheres.append(jnp.where(iota((nx, slots), 0) * ny + y == cell, 1.0, 0.0).astype(BF16))
    for t in range(turbines):
        row = slot[0, t : t + 1, :]
        hits = [ones_at(one_hot(slots, row - (me + k) * slots)) for k in (-1, 1)]
        edge_ref[0, t], edge_ref[1, t] = spread(wheres, hits, height[0, t : t + 1, :], load[0, t : t + 1, :])


def reduce_sums(v, tc, ye, yo, xe, xo, counts, line, couple, out, field, sums):
    _, nx, ny, levels = v.shape
    comps = v.shape[0]
    turbines = counts.shape[0]
    cells = nx * ny
    extend(v, ye, yo, xe, xo, field, (0,))
    update = stencil(field, 0, 2, nx, ny).reshape(cells, levels).astype(BF16)
    rows = jnp.dot(pick_slots(tc, cells), update, preferred_element_type=F32)
    for t in range(turbines):
        sums[t : t + 1, :] = jnp.sum(counts[t].astype(F32) * rows, axis=0, keepdims=True)
    lane = iota((turbines, LANES), 1)
    ev_x = even("gx")
    at = xe.shape[0] - 8 + SUMS
    result = jnp.where(lane == turbines, jnp.sum(sums[...], axis=1, keepdims=True), couple[...])
    rows_of = (line[SUMS : SUMS + 1, :], picked(ev_x, xo, xe, at, at + 1), picked(ev_x, xe, xo, at, at + 1))
    for k, row in enumerate(rows_of):
        result = jnp.where(lane == turbines + 1 + k, as_column(row[:, :turbines], turbines), result)
    me = lax.axis_index("gy")
    for k in range(out.shape[0]):
        out[k, 0:turbines, :] = result
        out[k, turbines : turbines + 8, :] = jnp.zeros((8, LANES), F32)
    above = []
    below = []
    for c in range(comps):
        for a, b, at in ((xo, xe, (c * 2 + 1) * ny), (xe, xo, c * 2 * ny)):
            above.append(picked(ev_x, a, b, at + ny - 1, at + ny))
            below.append(picked(ev_x, a, b, at, at + 1))
    for i in range(2 * comps):
        for k in range(out.shape[0]):
            out[k, turbines + i : turbines + i + 1, :] = jnp.where(me + 1 == k, above[i], below[i])


def edges_x(slots, pieces, v, ye, yo, xe, xo, edge_ref, update_ref, strip_ref, field):
    comps, nx, ny, levels = v.shape
    turbines = edge_ref.shape[1]
    ev, ev_y = even("gx"), even("gy")
    extend(v, ye, yo, xe, xo, field, tuple(range(comps)))
    ends = iota((nx, LANES), 0)
    for c in range(comps):
        update_ref[c] = stencil(field, c, 1, nx + 2, ny)
        for k, (a, b, y) in enumerate(((yo, ye, 0), (ye, yo, ny - 1))):
            near, far = (c * 2 + 1 - k) * nx, (c * 2 + k) * nx
            center = picked(ev_y, a, b, near, near + nx)
            before = jnp.where(ends == 0, 0.0, pltpu.roll(center, 1, 0))
            after = jnp.where(ends == nx - 1, 0.0, pltpu.roll(center, nx - 1, 0))
            others = picked(ev_y, a, b, far, far + nx) + v[c, :, y, :] + lane_edge(center)
            strip_ref[c, k] = moved(center, before, after, others)

    at = xe.shape[0] - 8 + CELLS
    code_at = comps * 2 * ny
    load_at = code_at + pieces * turbines
    shift = levels.bit_length() - 1
    for k, (a, b) in enumerate(((xo, xe), (xe, xo))):
        cell = picked(ev, a, b, at, at + 1)[:, :slots].astype(jnp.int32) - 1
        where = jnp.where(iota((ny, slots), 0) + (1 - k) * (nx - 1) * ny == cell, 1.0, 0.0).astype(BF16)
        codes = [picked(ev, a, b, code_at + i * turbines, code_at + (i + 1) * turbines) for i in range(pieces)]
        codes = jnp.concatenate(codes, axis=1).astype(jnp.int32) - 1
        there = [picked(ev, a, b, load_at + i * turbines, load_at + (i + 1) * turbines) for i in range(pieces)]
        there = jnp.concatenate(there, axis=1)
        for t in range(turbines):
            code = codes[t : t + 1, :]
            hit = ones_at(one_hot(slots, code >> shift))
            (edge_ref[k, t],) = spread([where], [hit], code & (levels - 1), there[t : t + 1, :])


def advance(points, got, v, tc, ye, yo, xe, xo, line, loads, edge_x, edge_y, update_ref, strip_ref, out, field, parts):
    comps, nx, ny, levels = v.shape
    turbines, slots, _ = loads.shape
    cells = nx * ny
    ev_x, ev_y = even("gx"), even("gy")
    total = got[0, 0:turbines, :]
    for k in range(1, got.shape[0]):
        total = total + got[k, 0:turbines, :]
    lane = iota((turbines, LANES), 1)

    def column(k):
        return jnp.sum(jnp.where(lane == k, total, 0.0), axis=1, keepdims=True)

    def coefs(scales, sums):
        return -(scales * (FREE_WIND + sums / points))

    at = xe.shape[0] - 8 + SCALE
    scale = as_column(line[SCALE : SCALE + 1, :turbines], turbines)
    own = coefs(scale, column(turbines + 1))
    left = coefs(as_column(picked(ev_x, xo, xe, at, at + 1)[:, :turbines], turbines), column(turbines + 2))
    right = coefs(as_column(picked(ev_x, xe, xo, at, at + 1)[:, :turbines], turbines), column(turbines + 3))
    own_row = jnp.sum(jnp.where(iota((turbines, LANES), 0) == lane, own, 0.0), axis=0, keepdims=True)
    forced = jnp.sum(jnp.where(lane < turbines, total * own_row, 0.0), axis=1, keepdims=True)
    later = coefs(scale, column(turbines) + forced)

    for s in range(0, slots, 16):
        first = jnp.zeros((16, levels), F32)
        second = first
        for t in range(turbines):
            part = loads[t, s : s + 16, :]
            first = first + own[t : t + 1, :] * part
            second = second + later[t : t + 1, :] * part
        for i, rest in enumerate((first, second)):
            for k in range(3):
                piece = rest.astype(BF16)
                rest = rest - piece.astype(F32)
                at = (3 * i + k) * levels
                parts[s : s + 16, at : at + levels] = piece
    row = tc[0, :, :]
    put = jnp.where(iota((cells, slots), 0) == row, 1.0, 0.0).astype(BF16)
    spread_out = jnp.dot(put, parts[...], preferred_element_type=F32)
    pieces = [spread_out[:, k * levels : (k + 1) * levels] for k in range(6)]
    first = ((pieces[0] + pieces[1]) + pieces[2]).reshape(nx, ny, levels)
    second = ((pieces[3] + pieces[4]) + pieces[5]).reshape(nx, ny, levels)
    for c in range(comps):
        push = rounded(rounded(v[c, :, :, :]) * first)
        field[c, 1 : 1 + nx, OWN : OWN + ny, :] = update_ref[c, 1 : 1 + nx, :, :] + push

    sums = []
    for edge, coef in ((edge_x.at[0], left), (edge_x.at[1], right), (edge_y.at[0], own), (edge_y.at[1], own)):
        side = coef[0:1, :] * edge[0]
        for t in range(1, turbines):
            side = side + coef[t : t + 1, :] * edge[t]
        sums.append(side)
    ix, iy = lax.axis_index("gx"), lax.axis_index("gy")
    last_y = lax.axis_size("gy") - 1
    there_x = (ix > 0, ix < lax.axis_size("gx") - 1)
    there_y = (iy > 0, iy < last_y)
    beside_y = (jnp.maximum(iy - 1, 0), jnp.minimum(iy + 1, last_y))
    corner_rows = [jnp.where(there_y[k], got[beside_y[k], turbines : turbines + 8, :], 0.0) for k in range(2)]
    row_x, row_y = iota((nx, LANES), 0), iota((ny, LANES), 0)
    for c in range(comps):
        corner = [[corner_rows[y][c * 2 + x : c * 2 + x + 1, :] for y in range(2)] for x in range(2)]
        for k, (a, b) in enumerate(((xo, xe), (xe, xo))):
            at = (c * 2 + 1 - k) * ny
            x = k * (nx + 1)
            push = rounded(rounded(picked(ev_x, a, b, at, at + ny)) * sums[k])
            extra = jnp.where(row_y == 0, corner[k][0], 0.0) + jnp.where(row_y == ny - 1, corner[k][1], 0.0)
            value = update_ref[c, x, :, :] + SPREAD * extra + push
            field[c, x, OWN : OWN + ny, :] = jnp.where(there_x[k], value, 0.0)
        for k, (a, b) in enumerate(((yo, ye), (ye, yo))):
            at = (c * 2 + 1 - k) * nx
            y = OWN - 1 + k * (ny + 1)
            push = rounded(rounded(picked(ev_y, a, b, at, at + nx)) * sums[2 + k])
            extra = jnp.where(row_x == 0, (SPREAD + CARRY) * corner[0][k], 0.0)
            extra = extra + jnp.where(row_x == nx - 1, SPREAD * corner[1][k], 0.0)
            value = strip_ref[c, k] + extra + push
            field[c, 1 : 1 + nx, y, :] = jnp.where(there_y[k], value, 0.0)
    for c in range(comps):
        now = field[c, 1 : 1 + nx, OWN : OWN + ny, :]
        out[c] = stencil(field, c, 1, nx, ny) + rounded(rounded(now) * second)


def body(velocity, tile_cells, owner, point_slot, point_z, loading):
    comps, nx, ny, levels = velocity.shape
    _, turbines, points = point_slot.shape
    slots = tile_cells.shape[2]
    tiles_y = lax.axis_size("gy")
    pieces = points // LANES
    rows_y = comps * 2 * nx + 8
    rows_x = comps * 2 * ny + 2 * pieces * turbines + 8
    args = (velocity, tile_cells, owner, point_slot, point_z, loading)
    work = {"flops": 26 * turbines * slots * points * levels, "nbytes": 1 << 20}

    def field(n, planes):
        return pltpu.VMEM((n, planes, PLANE, levels), F32)

    v, tc, own, slot, height, load, y_even, y_odd = call(
        stage,
        "stage",
        [(x.shape, x.dtype) for x in args] + [((rows_y, levels), F32)] * 2,
        args,
        [pltpu.SemaphoreType.DMA((len(args),))],
        space=pltpu.HBM,
    )
    yo, ye = swap(y_odd, "gy", 1), swap(y_even, "gy", 0)
    counts, loads, line, x_even, x_odd = call(
        histogram,
        "histogram",
        [
            ((turbines, slots, levels), BF16),
            ((turbines, slots, levels), F32),
            ((8, LANES), F32),
            ((rows_x, levels), F32),
            ((rows_x, levels), F32),
        ],
        (v, tc, own, slot, height, load),
        [pltpu.VMEM((turbines, levels), F32)],
        **work,
    )
    xo, xe = swap(x_odd, "gx", 1), swap(x_even, "gx", 0)
    edge_y, couple = call(
        beside,
        "beside",
        [((2, turbines, nx, levels), F32), ((turbines, LANES), F32)],
        (v, tc, slot, height, load, ye, yo, counts, loads),
        [pltpu.VMEM((turbines, slots, levels), BF16)],
        **work,
    )
    (chunk,) = call(
        reduce_sums,
        "reduce_sums",
        [((tiles_y, turbines + 8, LANES), F32)],
        (v, tc, ye, yo, xe, xo, counts, line, couple),
        [field(1, nx + 4), pltpu.VMEM((turbines, levels), F32)],
    )
    got = lax.all_to_all(chunk, "gy", 0, 0)

    def edges_x_of(*refs):
        return edges_x(slots, pieces, *refs)

    edge_x, update, strip = call(
        edges_x_of,
        "edges_x",
        [
            ((2, turbines, ny, levels), F32),
            ((comps, nx + 2, ny, levels), F32),
            ((comps, 2, nx, levels), F32),
        ],
        (v, ye, yo, xe, xo),
        [field(comps, nx + 4)],
        **work,
    )

    def advance_by(*refs):
        return advance(points, *refs)

    (out,) = call(
        advance_by,
        "advance",
        [(velocity.shape, F32)],
        (got, v, tc, ye, yo, xe, xo, line, loads, edge_x, edge_y, update, strip),
        [field(comps, nx + 2), pltpu.VMEM((slots, 6 * levels), BF16)],
    )
    return out


def solution(mesh):
    in_specs = (
        P(None, "gx", "gy", None),
        P("gx", "gy", None),
        P("gx", None),
        P("gx", None, None),
        P("gx", None, None),
        P("gx", None, None),
    )
    out_specs = P(None, "gx", "gy", None)
    return jax.shard_map(body, mesh=mesh, in_specs=in_specs, out_specs=out_specs, check_vma=False)
```

```python
import jax
import jax.numpy as jnp
from jax import lax
from jax.experimental import pallas as pl
from jax.experimental.pallas import tpu as pltpu
from jax.sharding import PartitionSpec as P

SPREAD = 0.12
CARRY = 0.25
FREE_WIND = 1.0
LOAD = 0.6

F32 = jnp.float32
BF16 = jnp.bfloat16
NT = (((1,), (1,)), ((), ()))
LANES = 128
OWN = 8
PLANE = 32
NO_SLOT = -30000.0
SUMS, SCALE, CELLS = 0, 1, 2


def iota(shape, axis):
    return lax.broadcasted_iota(jnp.int32, shape, axis)


def rounded(x):
    return x.astype(BF16).astype(F32)


def one_hot(count, row):
    places = iota((count, row.shape[1]), 0).astype(BF16)
    return places == row.astype(BF16)


def ones_at(mask):
    return jnp.where(mask, jnp.ones((), BF16), jnp.zeros((), BF16))


def pick_slots(tc, cells):
    slots = tc.shape[2]
    row = jnp.broadcast_to(tc[0, :, :].astype(F32), (slots, slots))
    same = iota((slots, slots), 0) == iota((slots, slots), 1)
    column = jnp.sum(jnp.where(same, row, 0.0), axis=1, keepdims=True).astype(jnp.int32)
    return jnp.where(iota((slots, cells), 1) == column, 1.0, 0.0).astype(BF16)


def even(axis):
    return lax.rem(lax.axis_index(axis), 2) == 0


def swap_pairs(count, first):
    pairs = []
    for i in range(first, count - 1, 2):
        pairs += [(i, i + 1), (i + 1, i)]
    return pairs


def swap(x, axis, first):
    return lax.ppermute(x, axis, swap_pairs(lax.axis_size(axis), first))


def call(kernel, name, outs, args, scratch=(), flops=0, nbytes=0, space=pltpu.VMEM):
    return pl.pallas_call(
        kernel,
        out_shape=[jax.ShapeDtypeStruct(s, d) for s, d in outs],
        in_specs=[pl.BlockSpec(memory_space=space)] * len(args),
        out_specs=[pl.BlockSpec(memory_space=pltpu.VMEM)] * len(outs),
        scratch_shapes=list(scratch),
        compiler_params=pltpu.CompilerParams(vmem_limit_bytes=16 << 20),
        cost_estimate=pl.CostEstimate(flops=flops, bytes_accessed=nbytes, transcendentals=0),
        name=name,
    )(*(pltpu.with_memory_space_constraint(a, space) if space is pltpu.HBM else a for a in args))


def lane_edge(center):
    axis = center.ndim - 1
    lane = iota(center.shape, axis)
    last = center.shape[axis] - 1
    below = jnp.where(lane == 0, 0.0, pltpu.roll(center, 1, axis))
    above = jnp.where(lane == last, 0.0, pltpu.roll(center, last, axis))
    return below + above


def moved(center, before, after, beside):
    beside = beside + before + after
    return center + SPREAD * (beside - 6.0 * center) - CARRY * (center - before)


def stencil(ref, c, x0, nx, ny):
    center = ref[c, x0 : x0 + nx, OWN : OWN + ny, :]
    before = ref[c, x0 - 1 : x0 - 1 + nx, OWN : OWN + ny, :]
    after = ref[c, x0 + 1 : x0 + 1 + nx, OWN : OWN + ny, :]
    beside = ref[c, x0 : x0 + nx, OWN - 1 : OWN - 1 + ny, :] + ref[c, x0 : x0 + nx, OWN + 1 : OWN + 1 + ny, :]
    return moved(center, before, after, beside + lane_edge(center))


def stage(v_hbm, tc_hbm, owner_hbm, slot_hbm, height_hbm, load_hbm, v, tc, owner, slot, height, load, to_even, to_odd, sems):
    pairs = ((v_hbm, v), (tc_hbm, tc), (slot_hbm, slot), (height_hbm, height), (load_hbm, load), (owner_hbm, owner))
    copies = [pltpu.make_async_copy(a, b, sems.at[i]) for i, (a, b) in enumerate(pairs)]
    for copy in copies:
        copy.start()
    copies[0].wait()
    comps, nx, ny, _ = v.shape
    ev = even("gy")
    at = 0
    for c in range(comps):
        for k in range(2):
            high = v[c, :, ny - 2 + k, :]
            low = v[c, :, k, :]
            to_even[at : at + nx, :] = jnp.where(ev, high, low)
            to_odd[at : at + nx, :] = jnp.where(ev, low, high)
            at += nx
    copies[1].wait()
    cells = tc[0, :, :].astype(F32) + 1.0
    slots = cells.shape[1]
    for out in (to_even, to_odd):
        out[at : at + 8, :] = jnp.zeros((8, LANES), F32)
        out[at : at + 1, 0:slots] = cells
    for copy in copies[2:]:
        copy.wait()


def as_column(row, n):
    same = iota((n, n), 0) == iota((n, n), 1)
    return jnp.sum(jnp.where(same, row, 0.0), axis=1, keepdims=True)


def as_row(column, n):
    same = iota((n, n), 0) == iota((n, n), 1)
    return jnp.sum(jnp.where(same, column, 0.0), axis=0, keepdims=True)


def picked(flag, a, b, lo, hi):
    return jnp.where(flag, a[lo:hi, :], b[lo:hi, :])


def histogram(v, tc, owner, slot, height, load, count_ref, load_ref, line, to_even, to_odd, sum_ref):
    _, turbines, points = slot.shape
    slots, levels = count_ref.shape[1:]
    comps, nx, ny, _ = v.shape
    cells = nx * ny
    first = lax.axis_index("gy") * slots
    values = v[0, :, :, :].reshape(cells, levels).astype(BF16)
    rows = jnp.dot(pick_slots(tc, cells), values, preferred_element_type=F32)
    zero = jnp.zeros((), BF16)
    for t in range(turbines):
        a = ones_at(one_hot(slots, slot[0, t : t + 1, :] - first))
        at_z = one_hot(levels, height[0, t : t + 1, :])
        weight = load[0, t : t + 1, :]
        high = weight.astype(BF16)
        low = (weight - high.astype(F32)).astype(BF16)
        b = jnp.concatenate([ones_at(at_z), jnp.where(at_z, high, zero), jnp.where(at_z, low, zero)], axis=0)
        both = lax.dot_general(a, b, NT, preferred_element_type=F32)
        count = both[:, :levels]
        count_ref[t] = count.astype(BF16)
        load_ref[t] = both[:, levels : 2 * levels] + both[:, 2 * levels :]
        sum_ref[t : t + 1, :] = jnp.sum(count * rows, axis=0, keepdims=True)

    owner_row = jnp.broadcast_to(owner[...].astype(F32), (turbines, turbines))
    member = owner_row == as_column(owner_row, turbines)
    load_row = as_row(jnp.sum(load[0, :, :], axis=1, keepdims=True), turbines)
    total = jnp.sum(jnp.where(member, load_row, 0.0), axis=1, keepdims=True)
    number = jnp.sum(jnp.where(member, 1.0, 0.0), axis=1, keepdims=True)
    line[...] = jnp.zeros((8, LANES), F32)
    line[SUMS : SUMS + 1, 0:turbines] = as_row(jnp.sum(sum_ref[...], axis=1, keepdims=True), turbines)
    line[SCALE : SCALE + 1, 0:turbines] = as_row(LOAD / (total / (number * points)), turbines)
    line[CELLS : CELLS + 1, 0:slots] = tc[0, :, :].astype(F32) + 1.0

    local = slot[0, :, :] - first
    inside = (local >= 0) & (local < slots)
    code = jnp.where(inside, local * levels + height[0, :, :] + 1, 0).astype(F32)
    ev = even("gx")
    at = 0
    for c in range(comps):
        for k in range(2):
            right, left = v[c, nx - 2 + k, :, :], v[c, k, :, :]
            to_even[at : at + ny, :] = jnp.where(ev, right, left)
            to_odd[at : at + ny, :] = jnp.where(ev, left, right)
            at += ny
    for part in (code, load[0, :, :]):
        for k in range(0, points, LANES):
            for out in (to_even, to_odd):
                out[at : at + turbines, :] = part[:, k : k + LANES]
            at += turbines
    for out in (to_even, to_odd):
        out[at : at + 8, :] = line[...]


def extend(v, yo, ye, xo, xe, field, comps):
    _, nx, ny, _ = v.shape
    ev_x, ev_y = even("gx"), even("gy")
    for c in comps:
        out = c if len(comps) > 1 else 0
        field[out, 2 : 2 + nx, OWN : OWN + ny, :] = v[c, :, :, :]
        for k in range(2):
            at = (c * 2 + k) * nx
            field[out, 2 : 2 + nx, OWN - 2 + k, :] = picked(ev_y, yo, ye, at, at + nx)
            field[out, 2 : 2 + nx, OWN + ny + k, :] = picked(ev_y, ye, yo, at, at + nx)
            at = (c * 2 + k) * ny
            for x, a, b in ((k, xo, xe), (2 + nx + k, xe, xo)):
                field[out, x, 0:OWN, :] = jnp.zeros((OWN, LANES), F32)
                field[out, x, OWN + ny : PLANE, :] = jnp.zeros((PLANE - OWN - ny, LANES), F32)
                field[out, x, OWN : OWN + ny, :] = picked(ev_x, a, b, at, at + ny)


def edge_slots(cell_row, cells):
    n, slots = cells.shape[0], cell_row.shape[1]
    slot = iota((n, slots), 1).astype(F32)
    return jnp.max(jnp.where(cell_row == cells, slot, NO_SLOT), axis=1, keepdims=True).astype(BF16)


def spread(places, z, weight):
    high = weight.astype(BF16)
    low = (weight - high.astype(F32)).astype(BF16)
    zero = jnp.zeros((), BF16)
    at_z = ones_at(one_hot(LANES, z))
    left = []
    for edge, slot in places:
        here = edge == slot.astype(BF16)
        left += [jnp.where(here, high, zero), jnp.where(here, low, zero)]
    both = lax.dot_general(jnp.concatenate(left, axis=0), at_z, NT, preferred_element_type=F32)
    n = both.shape[0] // len(left)
    return [both[2 * k * n : (2 * k + 1) * n] + both[(2 * k + 1) * n : (2 * k + 2) * n] for k in range(len(places))]


def beside(v, tc, yo, ye, counts, loads, couple, edge_counts, products, field, sums):
    turbines, slots, levels = counts.shape
    _, nx, ny, _ = v.shape
    cells = nx * ny
    ev = even("gy")
    field[0, 1 : 1 + nx, OWN : OWN + ny, :] = v[0, :, :, :]
    field[0, 1 : 1 + nx, OWN - 1, :] = picked(ev, yo, ye, nx, 2 * nx)
    field[0, 1 : 1 + nx, OWN + ny, :] = picked(ev, ye, yo, 0, nx)
    for x in (0, nx + 1):
        field[0, x, OWN : OWN + ny, :] = jnp.zeros((ny, levels), F32)
    update = stencil(field, 0, 1, nx, ny).reshape(cells, levels).astype(BF16)
    values = v[0, :, :, :].reshape(cells, levels).astype(BF16)
    both = jnp.dot(pick_slots(tc, cells), jnp.concatenate([values, update], axis=1), preferred_element_type=F32)
    rows, later = both[:, :levels], both[:, levels:]
    row_x = iota((2 * ny, slots), 0)
    edge = jnp.where(row_x < ny, row_x, row_x + (nx - 2) * ny)
    select = jnp.where(edge == tc[0, :, :], 1.0, 0.0).astype(BF16)
    for t in range(turbines):
        products[t] = (rows * loads[t]).astype(BF16)
        sums[t : t + 1, :] = jnp.sum(counts[t].astype(F32) * later, axis=0, keepdims=True)
        edge_counts[t] = jnp.dot(select, counts[t], preferred_element_type=F32)
    block = 16
    wide = turbines * block
    gram = jnp.zeros((wide, wide), F32)
    for b in range(0, slots, block):
        left = counts[:, b : b + block, :].reshape(wide, levels)
        right = products[:, b : b + block, :].reshape(wide, levels)
        gram = gram + lax.dot_general(left, right, NT, preferred_element_type=F32)
    keep = (iota((wide, wide), 0) & (block - 1)) == (iota((wide, wide), 1) & (block - 1))
    gram = jnp.sum(jnp.where(keep, gram, 0.0).reshape(turbines, block, wide), axis=1)
    select = jnp.where(iota((wide, LANES), 0) // block == iota((wide, LANES), 1), 1.0, 0.0)
    matrix = jnp.dot(gram, select, precision=lax.Precision.HIGHEST, preferred_element_type=F32)
    column = jnp.sum(sums[...], axis=1, keepdims=True)
    couple[...] = jnp.where(iota((turbines, LANES), 1) == turbines, column, matrix)


def reduce_sums(comps, ny, yo, ye, xo, xe, edge_counts, line, couple, out, sums):
    turbines = edge_counts.shape[0]
    ev_x = even("gx")
    left = (SPREAD + CARRY) * picked(ev_x, xo, xe, ny, 2 * ny)
    right = SPREAD * picked(ev_x, xe, xo, 0, ny)
    for t in range(turbines):
        sides = edge_counts[t, 0:ny, :] * left + edge_counts[t, ny : 2 * ny, :] * right
        sums[t : t + 1, :] = jnp.sum(sides, axis=0, keepdims=True)
    lane = iota((turbines, LANES), 1)
    at = xe.shape[0] - 8 + SUMS
    result = couple[...] + jnp.where(lane == turbines, jnp.sum(sums[...], axis=1, keepdims=True), 0.0)
    rows_of = (line[SUMS : SUMS + 1, :], picked(ev_x, xo, xe, at, at + 1), picked(ev_x, xe, xo, at, at + 1))
    for k, row in enumerate(rows_of):
        result = jnp.where(lane == turbines + 1 + k, as_column(row[:, :turbines], turbines), result)
    me = lax.axis_index("gy")
    for k in range(out.shape[0]):
        out[k, 0:turbines, :] = result
        out[k, turbines : turbines + 8, :] = jnp.zeros((8, LANES), F32)
    above = []
    below = []
    for c in range(comps):
        for a, b, at in ((xo, xe, (c * 2 + 1) * ny), (xe, xo, c * 2 * ny)):
            above.append(picked(ev_x, a, b, at + ny - 1, at + ny))
            below.append(picked(ev_x, a, b, at, at + 1))
    for i in range(2 * comps):
        for k in range(out.shape[0]):
            out[k, turbines + i : turbines + i + 1, :] = jnp.where(me + 1 == k, above[i], below[i])


def edges(slots, pieces, v, slot, height, load, yo, ye, xo, xe, edge_x, edge_y, update_ref, strip_ref, field):
    comps, nx, ny, levels = v.shape
    turbines = edge_x.shape[1]
    ev, ev_y = even("gx"), even("gy")
    extend(v, yo, ye, xo, xe, field, tuple(range(comps)))
    ends = iota((nx, LANES), 0)
    for c in range(comps):
        update_ref[c] = stencil(field, c, 1, nx + 2, ny)
        for k, (a, b, y) in enumerate(((yo, ye, 0), (ye, yo, ny - 1))):
            near, far = (c * 2 + 1 - k) * nx, (c * 2 + k) * nx
            center = picked(ev_y, a, b, near, near + nx)
            before = jnp.where(ends == 0, 0.0, pltpu.roll(center, 1, 0))
            after = jnp.where(ends == nx - 1, 0.0, pltpu.roll(center, nx - 1, 0))
            others = picked(ev_y, a, b, far, far + nx) + v[c, :, y, :] + lane_edge(center)
            strip_ref[c, k] = moved(center, before, after, others)

    at = xe.shape[0] - 8 + CELLS
    code_at = comps * 2 * ny
    load_at = code_at + pieces * turbines
    shift = levels.bit_length() - 1
    for k, (a, b) in enumerate(((xo, xe), (xe, xo))):
        cell = picked(ev, a, b, at, at + 1)[:, :slots].astype(jnp.int32) - 1
        edge = edge_slots(cell, iota((ny, slots), 0) + (1 - k) * (nx - 1) * ny)
        codes = [picked(ev, a, b, code_at + i * turbines, code_at + (i + 1) * turbines) for i in range(pieces)]
        codes = jnp.concatenate(codes, axis=1).astype(jnp.int32) - 1
        there = [picked(ev, a, b, load_at + i * turbines, load_at + (i + 1) * turbines) for i in range(pieces)]
        there = jnp.concatenate(there, axis=1)
        for t in range(turbines):
            code = codes[t : t + 1, :]
            (edge_x[k, t],) = spread([(edge, code >> shift)], code & (levels - 1), there[t : t + 1, :])

    me = lax.axis_index("gy")
    at = ye.shape[0] - 8
    lists = []
    for a, b, y in ((yo, ye, ny - 1), (ye, yo, 0)):
        cell = picked(ev_y, a, b, at, at + 1)[:, :slots].astype(jnp.int32) - 1
        lists.append(edge_slots(cell, iota((nx, slots), 0) * ny + y))
    for t in range(turbines):
        row = slot[0, t : t + 1, :]
        places = [(edge, row - (me + k) * slots) for edge, k in zip(lists, (-1, 1))]
        edge_y[0, t], edge_y[1, t] = spread(places, height[0, t : t + 1, :], load[0, t : t + 1, :])


def advance(points, got, v, tc, yo, ye, xo, xe, line, loads, edge_x, edge_y, update_ref, strip_ref, out, field, parts):
    comps, nx, ny, levels = v.shape
    turbines, slots, _ = loads.shape
    cells = nx * ny
    ev_x, ev_y = even("gx"), even("gy")
    total = got[0, 0:turbines, :]
    for k in range(1, got.shape[0]):
        total = total + got[k, 0:turbines, :]
    lane = iota((turbines, LANES), 1)

    def column(k):
        return jnp.sum(jnp.where(lane == k, total, 0.0), axis=1, keepdims=True)

    def coefs(scales, sums):
        return -(scales * (FREE_WIND + sums / points))

    at = xe.shape[0] - 8 + SCALE
    scale = as_column(line[SCALE : SCALE + 1, :turbines], turbines)
    own = coefs(scale, column(turbines + 1))
    left = coefs(as_column(picked(ev_x, xo, xe, at, at + 1)[:, :turbines], turbines), column(turbines + 2))
    right = coefs(as_column(picked(ev_x, xe, xo, at, at + 1)[:, :turbines], turbines), column(turbines + 3))
    own_row = jnp.sum(jnp.where(iota((turbines, LANES), 0) == lane, own, 0.0), axis=0, keepdims=True)
    forced = jnp.sum(jnp.where(lane < turbines, total * own_row, 0.0), axis=1, keepdims=True)
    later = coefs(scale, column(turbines) + forced)

    for s in range(0, slots, 16):
        first = jnp.zeros((16, levels), F32)
        second = first
        for t in range(turbines):
            part = loads[t, s : s + 16, :]
            first = first + own[t : t + 1, :] * part
            second = second + later[t : t + 1, :] * part
        for i, rest in enumerate((first, second)):
            for k in range(2):
                piece = rest.astype(BF16)
                rest = rest - piece.astype(F32)
                at = (2 * i + k) * levels
                parts[s : s + 16, at : at + levels] = piece
    row = tc[0, :, :]
    put = jnp.where(iota((cells, slots), 0) == row, 1.0, 0.0).astype(BF16)
    spread_out = jnp.dot(put, parts[...], preferred_element_type=F32)
    pieces = [spread_out[:, k * levels : (k + 1) * levels] for k in range(4)]
    first = (pieces[0] + pieces[1]).reshape(nx, ny, levels)
    second = (pieces[2] + pieces[3]).reshape(nx, ny, levels)
    for c in range(comps):
        push = rounded(rounded(v[c, :, :, :]) * first)
        field[c, 1 : 1 + nx, OWN : OWN + ny, :] = update_ref[c, 1 : 1 + nx, :, :] + push

    sums = []
    for edge, coef in ((edge_x.at[0], left), (edge_x.at[1], right), (edge_y.at[0], own), (edge_y.at[1], own)):
        side = coef[0:1, :] * edge[0]
        for t in range(1, turbines):
            side = side + coef[t : t + 1, :] * edge[t]
        sums.append(side)
    ix, iy = lax.axis_index("gx"), lax.axis_index("gy")
    last_y = lax.axis_size("gy") - 1
    there_x = (ix > 0, ix < lax.axis_size("gx") - 1)
    there_y = (iy > 0, iy < last_y)
    beside_y = (jnp.maximum(iy - 1, 0), jnp.minimum(iy + 1, last_y))
    corner_rows = [jnp.where(there_y[k], got[beside_y[k], turbines : turbines + 8, :], 0.0) for k in range(2)]
    row_x, row_y = iota((nx, LANES), 0), iota((ny, LANES), 0)
    for c in range(comps):
        corner = [[corner_rows[y][c * 2 + x : c * 2 + x + 1, :] for y in range(2)] for x in range(2)]
        for k, (a, b) in enumerate(((xo, xe), (xe, xo))):
            at = (c * 2 + 1 - k) * ny
            x = k * (nx + 1)
            push = rounded(rounded(picked(ev_x, a, b, at, at + ny)) * sums[k])
            extra = jnp.where(row_y == 0, corner[k][0], 0.0) + jnp.where(row_y == ny - 1, corner[k][1], 0.0)
            value = update_ref[c, x, :, :] + SPREAD * extra + push
            field[c, x, OWN : OWN + ny, :] = jnp.where(there_x[k], value, 0.0)
        for k, (a, b) in enumerate(((yo, ye), (ye, yo))):
            at = (c * 2 + 1 - k) * nx
            y = OWN - 1 + k * (ny + 1)
            push = rounded(rounded(picked(ev_y, a, b, at, at + nx)) * sums[2 + k])
            extra = jnp.where(row_x == 0, (SPREAD + CARRY) * corner[0][k], 0.0)
            extra = extra + jnp.where(row_x == nx - 1, SPREAD * corner[1][k], 0.0)
            value = strip_ref[c, k] + extra + push
            field[c, 1 : 1 + nx, y, :] = jnp.where(there_y[k], value, 0.0)
    for c in range(comps):
        now = field[c, 1 : 1 + nx, OWN : OWN + ny, :]
        out[c] = stencil(field, c, 1, nx, ny) + rounded(rounded(now) * second)


def body(velocity, tile_cells, owner, point_slot, point_z, loading):
    comps, nx, ny, levels = velocity.shape
    _, turbines, points = point_slot.shape
    slots = tile_cells.shape[2]
    tiles_y = lax.axis_size("gy")
    pieces = points // LANES
    rows_y = comps * 2 * nx + 8
    rows_x = comps * 2 * ny + 2 * pieces * turbines + 8
    args = (velocity, tile_cells, owner, point_slot, point_z, loading)
    work = {"flops": 26 * turbines * slots * points * levels, "nbytes": 1 << 20}

    def field(n, planes):
        return pltpu.VMEM((n, planes, PLANE, levels), F32)

    v, tc, own, slot, height, load, y_even, y_odd = call(
        stage,
        "stage",
        [(x.shape, x.dtype) for x in args] + [((rows_y, levels), F32)] * 2,
        args,
        [pltpu.SemaphoreType.DMA((len(args),))],
        space=pltpu.HBM,
    )
    yo, ye = swap(y_odd, "gy", 1), swap(y_even, "gy", 0)
    counts, loads, line, x_even, x_odd = call(
        histogram,
        "histogram",
        [
            ((turbines, slots, levels), BF16),
            ((turbines, slots, levels), F32),
            ((8, LANES), F32),
            ((rows_x, levels), F32),
            ((rows_x, levels), F32),
        ],
        (v, tc, own, slot, height, load),
        [pltpu.VMEM((turbines, levels), F32)],
        **work,
    )
    xo, xe = swap(x_odd, "gx", 1), swap(x_even, "gx", 0)
    couple, edge_counts = call(
        beside,
        "beside",
        [((turbines, LANES), F32), ((turbines, 2 * ny, levels), F32)],
        (v, tc, yo, ye, counts, loads),
        [pltpu.VMEM((turbines, slots, levels), BF16), field(1, nx + 2), pltpu.VMEM((turbines, levels), F32)],
        **work,
    )

    def reduce_of(*refs):
        return reduce_sums(comps, ny, *refs)

    (chunk,) = call(
        reduce_of,
        "reduce_sums",
        [((tiles_y, turbines + 8, LANES), F32)],
        (yo, ye, xo, xe, edge_counts, line, couple),
        [pltpu.VMEM((turbines, levels), F32)],
    )
    got = lax.all_to_all(chunk, "gy", 0, 0)

    def edges_of(*refs):
        return edges(slots, pieces, *refs)

    edge_x, edge_y, update, strip = call(
        edges_of,
        "edges",
        [
            ((2, turbines, ny, levels), F32),
            ((2, turbines, nx, levels), F32),
            ((comps, nx + 2, ny, levels), F32),
            ((comps, 2, nx, levels), F32),
        ],
        (v, slot, height, load, yo, ye, xo, xe),
        [field(comps, nx + 4)],
        **work,
    )

    def advance_by(*refs):
        return advance(points, *refs)

    (out,) = call(
        advance_by,
        "advance",
        [(velocity.shape, F32)],
        (got, v, tc, yo, ye, xo, xe, line, loads, edge_x, edge_y, update, strip),
        [field(comps, nx + 2), pltpu.VMEM((slots, 4 * levels), BF16)],
    )
    return out


def solution(mesh):
    in_specs = (
        P(None, "gx", "gy", None),
        P("gx", "gy", None),
        P("gx", None),
        P("gx", None, None),
        P("gx", None, None),
        P("gx", None, None),
    )
    out_specs = P(None, "gx", "gy", None)
    return jax.shard_map(body, mesh=mesh, in_specs=in_specs, out_specs=out_specs, check_vma=False)
```

```python
import jax
import jax.numpy as jnp
from jax import lax
from jax.experimental import pallas as pl
from jax.experimental.pallas import tpu as pltpu
from jax.sharding import PartitionSpec as P

SPREAD = 0.12
CARRY = 0.25
FREE_WIND = 1.0
LOAD = 0.6

F32 = jnp.float32
BF16 = jnp.bfloat16
NT = (((1,), (1,)), ((), ()))
LANES = 128
OWN = 8
PLANE = 32
NO_SLOT = -30000.0
SUMS, SCALE, CELLS = 0, 1, 2


def iota(shape, axis):
    return lax.broadcasted_iota(jnp.int32, shape, axis)


def rounded(x):
    return x.astype(BF16).astype(F32)


def one_hot(count, row):
    places = iota((count, row.shape[1]), 0).astype(BF16)
    return places == row.astype(BF16)


def ones_at(mask):
    return jnp.where(mask, jnp.ones((), BF16), jnp.zeros((), BF16))


def pick_slots(tc, cells):
    slots = tc.shape[2]
    row = jnp.broadcast_to(tc[0, :, :].astype(F32), (slots, slots))
    same = iota((slots, slots), 0) == iota((slots, slots), 1)
    column = jnp.sum(jnp.where(same, row, 0.0), axis=1, keepdims=True).astype(jnp.int32)
    return jnp.where(iota((slots, cells), 1) == column, 1.0, 0.0).astype(BF16)


def even(axis):
    return lax.rem(lax.axis_index(axis), 2) == 0


def swap(x, axis):
    return lax.ppermute(x, axis, [(i, i ^ 1) for i in range(lax.axis_size(axis))])


def hop(x, axis):
    count = lax.axis_size(axis)
    steps = [(i, i + 2 - 4 * (i % 2)) for i in range(count)]
    return lax.ppermute(x, axis, [(i, k) for i, k in steps if 0 <= k < count])


def call(kernel, name, outs, args, scratch=(), flops=0, nbytes=0, space=pltpu.VMEM):
    return pl.pallas_call(
        kernel,
        out_shape=[jax.ShapeDtypeStruct(s, d) for s, d in outs],
        in_specs=[pl.BlockSpec(memory_space=space)] * len(args),
        out_specs=[pl.BlockSpec(memory_space=pltpu.VMEM)] * len(outs),
        scratch_shapes=list(scratch),
        compiler_params=pltpu.CompilerParams(vmem_limit_bytes=16 << 20),
        cost_estimate=pl.CostEstimate(flops=flops, bytes_accessed=nbytes, transcendentals=0),
        name=name,
    )(*(pltpu.with_memory_space_constraint(a, space) if space is pltpu.HBM else a for a in args))


def lane_edge(center):
    axis = center.ndim - 1
    lane = iota(center.shape, axis)
    last = center.shape[axis] - 1
    below = jnp.where(lane == 0, 0.0, pltpu.roll(center, 1, axis))
    above = jnp.where(lane == last, 0.0, pltpu.roll(center, last, axis))
    return below + above


def moved(center, before, after, beside):
    beside = beside + before + after
    return center + SPREAD * (beside - 6.0 * center) - CARRY * (center - before)


def stencil(ref, c, x0, nx, ny):
    center = ref[c, x0 : x0 + nx, OWN : OWN + ny, :]
    before = ref[c, x0 - 1 : x0 - 1 + nx, OWN : OWN + ny, :]
    after = ref[c, x0 + 1 : x0 + 1 + nx, OWN : OWN + ny, :]
    beside = ref[c, x0 : x0 + nx, OWN - 1 : OWN - 1 + ny, :] + ref[c, x0 : x0 + nx, OWN + 1 : OWN + 1 + ny, :]
    return moved(center, before, after, beside + lane_edge(center))


def stage(v_hbm, tc_hbm, owner_hbm, slot_hbm, height_hbm, load_hbm, v, tc, owner, slot, height, load, out, sems):
    pairs = ((v_hbm, v), (tc_hbm, tc), (slot_hbm, slot), (height_hbm, height), (load_hbm, load), (owner_hbm, owner))
    copies = [pltpu.make_async_copy(a, b, sems.at[i]) for i, (a, b) in enumerate(pairs)]
    for copy in copies:
        copy.start()
    copies[0].wait()
    comps, nx, ny, _ = v.shape
    ev = even("gy")
    rest = comps * 2 * nx + 8
    at = 0
    for c in range(comps):
        for k in range(2):
            high = v[c, :, ny - 2 + k, :]
            low = v[c, :, k, :]
            out[at : at + nx, :] = jnp.where(ev, low, high)
            out[at + rest : at + rest + nx, :] = jnp.where(ev, high, low)
            at += nx
    copies[1].wait()
    cells = tc[0, :, :].astype(F32) + 1.0
    slots = cells.shape[1]
    out[at : at + 8, :] = jnp.zeros((8, LANES), F32)
    out[at : at + 1, 0:slots] = cells
    for copy in copies[2:]:
        copy.wait()


def as_column(row, n):
    same = iota((n, n), 0) == iota((n, n), 1)
    return jnp.sum(jnp.where(same, row, 0.0), axis=1, keepdims=True)


def as_row(column, n):
    same = iota((n, n), 0) == iota((n, n), 1)
    return jnp.sum(jnp.where(same, column, 0.0), axis=0, keepdims=True)


def picked(flag, a, b, lo, hi):
    return jnp.where(flag, a[lo:hi, :], b[lo:hi, :])


def edge_rows(flag, low, near, far, lo, hi):
    at = far.shape[0]
    here, there = near[at + lo : at + hi, :], far[lo:hi, :]
    return jnp.where(flag, there, here) if low else jnp.where(flag, here, there)


def pass_on(near, *refs):
    out = refs[-1]
    out[...] = near[0 : out.shape[0], :]


def histogram(v, tc, owner, slot, height, load, count_ref, load_ref, line, out, sum_ref):
    _, turbines, points = slot.shape
    slots, levels = count_ref.shape[1:]
    comps, nx, ny, _ = v.shape
    cells = nx * ny
    first = lax.axis_index("gy") * slots
    values = v[0, :, :, :].reshape(cells, levels).astype(BF16)
    rows = jnp.dot(pick_slots(tc, cells), values, preferred_element_type=F32)
    zero = jnp.zeros((), BF16)
    for t in range(turbines):
        a = ones_at(one_hot(slots, slot[0, t : t + 1, :] - first))
        at_z = one_hot(levels, height[0, t : t + 1, :])
        weight = load[0, t : t + 1, :]
        high = weight.astype(BF16)
        low = (weight - high.astype(F32)).astype(BF16)
        b = jnp.concatenate([ones_at(at_z), jnp.where(at_z, high, zero), jnp.where(at_z, low, zero)], axis=0)
        both = lax.dot_general(a, b, NT, preferred_element_type=F32)
        count = both[:, :levels]
        count_ref[t] = count.astype(BF16)
        load_ref[t] = both[:, levels : 2 * levels] + both[:, 2 * levels :]
        sum_ref[t : t + 1, :] = jnp.sum(count * rows, axis=0, keepdims=True)

    owner_row = jnp.broadcast_to(owner[...].astype(F32), (turbines, turbines))
    member = owner_row == as_column(owner_row, turbines)
    load_row = as_row(jnp.sum(load[0, :, :], axis=1, keepdims=True), turbines)
    total = jnp.sum(jnp.where(member, load_row, 0.0), axis=1, keepdims=True)
    number = jnp.sum(jnp.where(member, 1.0, 0.0), axis=1, keepdims=True)
    line[...] = jnp.zeros((8, LANES), F32)
    line[SUMS : SUMS + 1, 0:turbines] = as_row(jnp.sum(sum_ref[...], axis=1, keepdims=True), turbines)
    line[SCALE : SCALE + 1, 0:turbines] = as_row(LOAD / (total / (number * points)), turbines)
    line[CELLS : CELLS + 1, 0:slots] = tc[0, :, :].astype(F32) + 1.0

    local = slot[0, :, :] - first
    inside = (local >= 0) & (local < slots)
    code = jnp.where(inside, local * levels + height[0, :, :] + 1, 0).astype(F32)
    ev = even("gx")
    rest = out.shape[0] - comps * 2 * ny
    at = 0
    for c in range(comps):
        for k in range(2):
            right, left = v[c, nx - 2 + k, :, :], v[c, k, :, :]
            out[at : at + ny, :] = jnp.where(ev, left, right)
            out[at + rest : at + rest + ny, :] = jnp.where(ev, right, left)
            at += ny
    for part in (code, load[0, :, :]):
        for k in range(0, points, LANES):
            out[at : at + turbines, :] = part[:, k : k + LANES]
            at += turbines
    out[at : at + 8, :] = line[...]


def extend(v, yo, ye, xo, xe, field, comps):
    _, nx, ny, _ = v.shape
    ev_x, ev_y = even("gx"), even("gy")
    for c in comps:
        out = c if len(comps) > 1 else 0
        field[out, 2 : 2 + nx, OWN : OWN + ny, :] = v[c, :, :, :]
        for k in range(2):
            at = (c * 2 + k) * nx
            field[out, 2 : 2 + nx, OWN - 2 + k, :] = edge_rows(ev_y, True, ye, yo, at, at + nx)
            field[out, 2 : 2 + nx, OWN + ny + k, :] = edge_rows(ev_y, False, ye, yo, at, at + nx)
            at = (c * 2 + k) * ny
            for x, low in ((k, True), (2 + nx + k, False)):
                field[out, x, 0:OWN, :] = jnp.zeros((OWN, LANES), F32)
                field[out, x, OWN + ny : PLANE, :] = jnp.zeros((PLANE - OWN - ny, LANES), F32)
                field[out, x, OWN : OWN + ny, :] = edge_rows(ev_x, low, xe, xo, at, at + ny)


def edge_slots(cell_row, cells):
    n, slots = cells.shape[0], cell_row.shape[1]
    slot = iota((n, slots), 1).astype(F32)
    return jnp.max(jnp.where(cell_row == cells, slot, NO_SLOT), axis=1, keepdims=True).astype(BF16)


def spread(places, z, weight):
    high = weight.astype(BF16)
    low = (weight - high.astype(F32)).astype(BF16)
    zero = jnp.zeros((), BF16)
    at_z = ones_at(one_hot(LANES, z))
    left = []
    for edge, slot in places:
        here = edge == slot.astype(BF16)
        left += [jnp.where(here, high, zero), jnp.where(here, low, zero)]
    both = lax.dot_general(jnp.concatenate(left, axis=0), at_z, NT, preferred_element_type=F32)
    n = both.shape[0] // len(left)
    return [both[2 * k * n : (2 * k + 1) * n] + both[(2 * k + 1) * n : (2 * k + 2) * n] for k in range(len(places))]


def pair_up(v, tc, counts, loads, matrix, edge_counts, products):
    turbines, slots, levels = counts.shape
    _, nx, ny, _ = v.shape
    cells = nx * ny
    values = v[0, :, :, :].reshape(cells, levels).astype(BF16)
    rows = jnp.dot(pick_slots(tc, cells), values, preferred_element_type=F32)
    row_x = iota((2 * ny, slots), 0)
    edge = jnp.where(row_x < ny, row_x, row_x + (nx - 2) * ny)
    select = jnp.where(edge == tc[0, :, :], 1.0, 0.0).astype(BF16)
    for t in range(turbines):
        products[t] = (rows * loads[t]).astype(BF16)
        edge_counts[t] = jnp.dot(select, counts[t], preferred_element_type=F32)
    block = 16
    wide = turbines * block
    gram = jnp.zeros((wide, wide), F32)
    for b in range(0, slots, block):
        left = counts[:, b : b + block, :].reshape(wide, levels)
        right = products[:, b : b + block, :].reshape(wide, levels)
        gram = gram + lax.dot_general(left, right, NT, preferred_element_type=F32)
    keep = (iota((wide, wide), 0) & (block - 1)) == (iota((wide, wide), 1) & (block - 1))
    gram = jnp.sum(jnp.where(keep, gram, 0.0).reshape(turbines, block, wide), axis=1)
    select = jnp.where(iota((wide, LANES), 0) // block == iota((wide, LANES), 1), 1.0, 0.0)
    matrix[...] = jnp.dot(gram, select, precision=lax.Precision.HIGHEST, preferred_element_type=F32)


def beside(v, tc, yo, ye, counts, matrix, couple, field, sums):
    turbines, _, levels = counts.shape
    _, nx, ny, _ = v.shape
    cells = nx * ny
    ev = even("gy")
    field[0, 1 : 1 + nx, OWN : OWN + ny, :] = v[0, :, :, :]
    field[0, 1 : 1 + nx, OWN - 1, :] = edge_rows(ev, True, ye, yo, nx, 2 * nx)
    field[0, 1 : 1 + nx, OWN + ny, :] = edge_rows(ev, False, ye, yo, 0, nx)
    for x in (0, nx + 1):
        field[0, x, OWN : OWN + ny, :] = jnp.zeros((ny, levels), F32)
    update = stencil(field, 0, 1, nx, ny).reshape(cells, levels).astype(BF16)
    later = jnp.dot(pick_slots(tc, cells), update, preferred_element_type=F32)
    for t in range(turbines):
        sums[t : t + 1, :] = jnp.sum(counts[t].astype(F32) * later, axis=0, keepdims=True)
    column = jnp.sum(sums[...], axis=1, keepdims=True)
    couple[...] = jnp.where(iota((turbines, LANES), 1) == turbines, column, matrix[...])


def reduce_sums(comps, ny, yo, ye, xo, xe, edge_counts, line, couple, out, sums):
    turbines = edge_counts.shape[0]
    ev_x = even("gx")
    left = (SPREAD + CARRY) * edge_rows(ev_x, True, xe, xo, ny, 2 * ny)
    right = SPREAD * edge_rows(ev_x, False, xe, xo, 0, ny)
    for t in range(turbines):
        sides = edge_counts[t, 0:ny, :] * left + edge_counts[t, ny : 2 * ny, :] * right
        sums[t : t + 1, :] = jnp.sum(sides, axis=0, keepdims=True)
    lane = iota((turbines, LANES), 1)
    at = xo.shape[0] - 8 + SUMS
    result = couple[...] + jnp.where(lane == turbines, jnp.sum(sums[...], axis=1, keepdims=True), 0.0)
    rows_of = (line[SUMS : SUMS + 1, :], picked(ev_x, xo, xe, at, at + 1), picked(ev_x, xe, xo, at, at + 1))
    for k, row in enumerate(rows_of):
        result = jnp.where(lane == turbines + 1 + k, as_column(row[:, :turbines], turbines), result)
    me = lax.axis_index("gy")
    for k in range(out.shape[0]):
        out[k, 0:turbines, :] = result
        out[k, turbines : turbines + 8, :] = jnp.zeros((8, LANES), F32)
    above = []
    below = []
    for c in range(comps):
        for low, at in ((True, (c * 2 + 1) * ny), (False, c * 2 * ny)):
            above.append(edge_rows(ev_x, low, xe, xo, at + ny - 1, at + ny))
            below.append(edge_rows(ev_x, low, xe, xo, at, at + 1))
    for i in range(2 * comps):
        for k in range(out.shape[0]):
            out[k, turbines + i : turbines + i + 1, :] = jnp.where(me + 1 == k, above[i], below[i])


def edges(slots, pieces, v, slot, height, load, yo, ye, xo, xe, edge_x, edge_y, update_ref, strip_ref, field):
    comps, nx, ny, levels = v.shape
    turbines = edge_x.shape[1]
    ev, ev_y = even("gx"), even("gy")
    extend(v, yo, ye, xo, xe, field, tuple(range(comps)))
    ends = iota((nx, LANES), 0)
    for c in range(comps):
        update_ref[c] = stencil(field, c, 1, nx + 2, ny)
        for k, y in enumerate((0, ny - 1)):
            near, far = (c * 2 + 1 - k) * nx, (c * 2 + k) * nx
            center = edge_rows(ev_y, k == 0, ye, yo, near, near + nx)
            before = jnp.where(ends == 0, 0.0, pltpu.roll(center, 1, 0))
            after = jnp.where(ends == nx - 1, 0.0, pltpu.roll(center, nx - 1, 0))
            others = edge_rows(ev_y, k == 0, ye, yo, far, far + nx) + v[c, :, y, :] + lane_edge(center)
            strip_ref[c, k] = moved(center, before, after, others)

    at = xo.shape[0] - 8 + CELLS
    code_at = comps * 2 * ny
    load_at = code_at + pieces * turbines
    shift = levels.bit_length() - 1
    for k, (a, b) in enumerate(((xo, xe), (xe, xo))):
        cell = picked(ev, a, b, at, at + 1)[:, :slots].astype(jnp.int32) - 1
        edge = edge_slots(cell, iota((ny, slots), 0) + (1 - k) * (nx - 1) * ny)
        codes = [picked(ev, a, b, code_at + i * turbines, code_at + (i + 1) * turbines) for i in range(pieces)]
        codes = jnp.concatenate(codes, axis=1).astype(jnp.int32) - 1
        there = [picked(ev, a, b, load_at + i * turbines, load_at + (i + 1) * turbines) for i in range(pieces)]
        there = jnp.concatenate(there, axis=1)
        for t in range(turbines):
            code = codes[t : t + 1, :]
            (edge_x[k, t],) = spread([(edge, code >> shift)], code & (levels - 1), there[t : t + 1, :])

    me = lax.axis_index("gy")
    at = yo.shape[0] - 8
    lists = []
    for a, b, y in ((yo, ye, ny - 1), (ye, yo, 0)):
        cell = picked(ev_y, a, b, at, at + 1)[:, :slots].astype(jnp.int32) - 1
        lists.append(edge_slots(cell, iota((nx, slots), 0) * ny + y))
    for t in range(turbines):
        row = slot[0, t : t + 1, :]
        places = [(edge, row - (me + k) * slots) for edge, k in zip(lists, (-1, 1))]
        edge_y[0, t], edge_y[1, t] = spread(places, height[0, t : t + 1, :], load[0, t : t + 1, :])


def advance(points, got, v, tc, yo, ye, xo, xe, line, loads, edge_x, edge_y, update_ref, strip_ref, out, field, parts):
    comps, nx, ny, levels = v.shape
    turbines, slots, _ = loads.shape
    cells = nx * ny
    ev_x, ev_y = even("gx"), even("gy")
    total = got[0, 0:turbines, :]
    for k in range(1, got.shape[0]):
        total = total + got[k, 0:turbines, :]
    lane = iota((turbines, LANES), 1)

    def column(k):
        return jnp.sum(jnp.where(lane == k, total, 0.0), axis=1, keepdims=True)

    def coefs(scales, sums):
        return -(scales * (FREE_WIND + sums / points))

    at = xo.shape[0] - 8 + SCALE
    scale = as_column(line[SCALE : SCALE + 1, :turbines], turbines)
    own = coefs(scale, column(turbines + 1))
    left = coefs(as_column(picked(ev_x, xo, xe, at, at + 1)[:, :turbines], turbines), column(turbines + 2))
    right = coefs(as_column(picked(ev_x, xe, xo, at, at + 1)[:, :turbines], turbines), column(turbines + 3))
    own_row = jnp.sum(jnp.where(iota((turbines, LANES), 0) == lane, own, 0.0), axis=0, keepdims=True)
    forced = jnp.sum(jnp.where(lane < turbines, total * own_row, 0.0), axis=1, keepdims=True)
    later = coefs(scale, column(turbines) + forced)

    for s in range(0, slots, 16):
        first = jnp.zeros((16, levels), F32)
        second = first
        for t in range(turbines):
            part = loads[t, s : s + 16, :]
            first = first + own[t : t + 1, :] * part
            second = second + later[t : t + 1, :] * part
        for i, rest in enumerate((first, second)):
            for k in range(2):
                piece = rest.astype(BF16)
                rest = rest - piece.astype(F32)
                at = (2 * i + k) * levels
                parts[s : s + 16, at : at + levels] = piece
    row = tc[0, :, :]
    put = jnp.where(iota((cells, slots), 0) == row, 1.0, 0.0).astype(BF16)
    spread_out = jnp.dot(put, parts[...], preferred_element_type=F32)
    pieces = [spread_out[:, k * levels : (k + 1) * levels] for k in range(4)]
    first = (pieces[0] + pieces[1]).reshape(nx, ny, levels)
    second = (pieces[2] + pieces[3]).reshape(nx, ny, levels)
    for c in range(comps):
        push = rounded(rounded(v[c, :, :, :]) * first)
        field[c, 1 : 1 + nx, OWN : OWN + ny, :] = update_ref[c, 1 : 1 + nx, :, :] + push

    sums = []
    for edge, coef in ((edge_x.at[0], left), (edge_x.at[1], right), (edge_y.at[0], own), (edge_y.at[1], own)):
        side = coef[0:1, :] * edge[0]
        for t in range(1, turbines):
            side = side + coef[t : t + 1, :] * edge[t]
        sums.append(side)
    ix, iy = lax.axis_index("gx"), lax.axis_index("gy")
    last_y = lax.axis_size("gy") - 1
    there_x = (ix > 0, ix < lax.axis_size("gx") - 1)
    there_y = (iy > 0, iy < last_y)
    beside_y = (jnp.maximum(iy - 1, 0), jnp.minimum(iy + 1, last_y))
    corner_rows = [jnp.where(there_y[k], got[beside_y[k], turbines : turbines + 8, :], 0.0) for k in range(2)]
    row_x, row_y = iota((nx, LANES), 0), iota((ny, LANES), 0)
    for c in range(comps):
        corner = [[corner_rows[y][c * 2 + x : c * 2 + x + 1, :] for y in range(2)] for x in range(2)]
        for k in range(2):
            at = (c * 2 + 1 - k) * ny
            x = k * (nx + 1)
            push = rounded(rounded(edge_rows(ev_x, k == 0, xe, xo, at, at + ny)) * sums[k])
            extra = jnp.where(row_y == 0, corner[k][0], 0.0) + jnp.where(row_y == ny - 1, corner[k][1], 0.0)
            value = update_ref[c, x, :, :] + SPREAD * extra + push
            field[c, x, OWN : OWN + ny, :] = jnp.where(there_x[k], value, 0.0)
        for k in range(2):
            at = (c * 2 + 1 - k) * nx
            y = OWN - 1 + k * (ny + 1)
            push = rounded(rounded(edge_rows(ev_y, k == 0, ye, yo, at, at + nx)) * sums[2 + k])
            extra = jnp.where(row_x == 0, (SPREAD + CARRY) * corner[0][k], 0.0)
            extra = extra + jnp.where(row_x == nx - 1, SPREAD * corner[1][k], 0.0)
            value = strip_ref[c, k] + extra + push
            field[c, 1 : 1 + nx, y, :] = jnp.where(there_y[k], value, 0.0)
    for c in range(comps):
        now = field[c, 1 : 1 + nx, OWN : OWN + ny, :]
        out[c] = stencil(field, c, 1, nx, ny) + rounded(rounded(now) * second)


def body(velocity, tile_cells, owner, point_slot, point_z, loading):
    comps, nx, ny, levels = velocity.shape
    _, turbines, points = point_slot.shape
    slots = tile_cells.shape[2]
    tiles_y = lax.axis_size("gy")
    pieces = points // LANES
    edge_y_rows, edge_x_rows = comps * 2 * nx, comps * 2 * ny
    rows_y = edge_y_rows + 8
    rows_x = edge_x_rows + 2 * pieces * turbines + 8
    args = (velocity, tile_cells, owner, point_slot, point_z, loading)
    work = {"flops": 104 * turbines * slots * points * levels, "nbytes": 1 << 20}

    def field(n, planes):
        return pltpu.VMEM((n, planes, PLANE, levels), F32)

    v, tc, own, slot, height, load, to_y = call(
        stage,
        "stage",
        [(x.shape, x.dtype) for x in args] + [((edge_y_rows + rows_y, levels), F32)],
        args,
        [pltpu.SemaphoreType.DMA((len(args),))],
        space=pltpu.HBM,
    )
    ye = swap(to_y, "gy")
    counts, loads, line, to_x = call(
        histogram,
        "histogram",
        [
            ((turbines, slots, levels), BF16),
            ((turbines, slots, levels), F32),
            ((8, LANES), F32),
            ((edge_x_rows + rows_x, levels), F32),
        ],
        (v, tc, own, slot, height, load),
        [pltpu.VMEM((turbines, levels), F32)],
        **work,
    )
    xe = swap(to_x, "gx")
    matrix, edge_counts = call(
        pair_up,
        "pair_up",
        [((turbines, LANES), F32), ((turbines, 2 * ny, levels), F32)],
        (v, tc, counts, loads),
        [pltpu.VMEM((turbines, slots, levels), BF16)],
        **work,
    )
    (on_y,) = call(pass_on, "pass_on_y", [((rows_y, levels), F32)], (ye, matrix))
    yo = hop(on_y, "gy")
    (on_x,) = call(pass_on, "pass_on_x", [((rows_x, levels), F32)], (xe,))
    xo = hop(on_x, "gx")
    (couple,) = call(
        beside,
        "beside",
        [((turbines, LANES), F32)],
        (v, tc, yo, ye, counts, matrix),
        [field(1, nx + 2), pltpu.VMEM((turbines, levels), F32)],
        flops=work["flops"] // 4,
        nbytes=work["nbytes"],
    )

    def reduce_of(*refs):
        return reduce_sums(comps, ny, *refs)

    (chunk,) = call(
        reduce_of,
        "reduce_sums",
        [((tiles_y, turbines + 8, LANES), F32)],
        (yo, ye, xo, xe, edge_counts, line, couple),
        [pltpu.VMEM((turbines, levels), F32)],
    )
    got = lax.all_to_all(chunk, "gy", 0, 0)

    def edges_of(*refs):
        return edges(slots, pieces, *refs)

    edge_x, edge_y, update, strip = call(
        edges_of,
        "edges",
        [
            ((2, turbines, ny, levels), F32),
            ((2, turbines, nx, levels), F32),
            ((comps, nx + 2, ny, levels), F32),
            ((comps, 2, nx, levels), F32),
        ],
        (v, slot, height, load, yo, ye, xo, xe),
        [field(comps, nx + 4)],
        **work,
    )

    def advance_by(*refs):
        return advance(points, *refs)

    (out,) = call(
        advance_by,
        "advance",
        [(velocity.shape, F32)],
        (got, v, tc, yo, ye, xo, xe, line, loads, edge_x, edge_y, update, strip),
        [field(comps, nx + 2), pltpu.VMEM((slots, 4 * levels), BF16)],
    )
    return out


def solution(mesh):
    in_specs = (
        P(None, "gx", "gy", None),
        P("gx", "gy", None),
        P("gx", None),
        P("gx", None, None),
        P("gx", None, None),
        P("gx", None, None),
    )
    out_specs = P(None, "gx", "gy", None)
    return jax.shard_map(body, mesh=mesh, in_specs=in_specs, out_specs=out_specs, check_vma=False)
```

```python
import jax
import jax.numpy as jnp
from jax import lax
from jax.experimental import pallas as pl
from jax.experimental.pallas import tpu as pltpu
from jax.sharding import PartitionSpec as P

SPREAD = 0.12
CARRY = 0.25
FREE_WIND = 1.0
LOAD = 0.6

F32 = jnp.float32
BF16 = jnp.bfloat16
NT = (((1,), (1,)), ((), ()))
LANES = 128
OWN = 8
PLANE = 32
NO_SLOT = -30000.0
SUMS, SCALE, CELLS = 0, 1, 2


def iota(shape, axis):
    return lax.broadcasted_iota(jnp.int32, shape, axis)


def rounded(x):
    return x.astype(BF16).astype(F32)


def one_hot(count, row):
    places = iota((count, row.shape[1]), 0).astype(BF16)
    return places == row.astype(BF16)


def ones_at(mask):
    return jnp.where(mask, jnp.ones((), BF16), jnp.zeros((), BF16))


def pick_slots(tc, cells):
    slots = tc.shape[2]
    row = jnp.broadcast_to(tc[0, :, :].astype(F32), (slots, slots))
    same = iota((slots, slots), 0) == iota((slots, slots), 1)
    column = jnp.sum(jnp.where(same, row, 0.0), axis=1, keepdims=True).astype(jnp.int32)
    return jnp.where(iota((slots, cells), 1) == column, 1.0, 0.0).astype(BF16)


def even(axis):
    return lax.rem(lax.axis_index(axis), 2) == 0


def swap(x, axis, first):
    counts = {name: lax.axis_size(name) for name in ("gx", "gy")}
    other = "gy" if axis == "gx" else "gx"

    def device(along, across):
        at = {axis: along, other: across}
        return at["gx"] * counts["gy"] + at["gy"]

    last = counts[axis] - 1
    pairs = [(device(i, k), device(i + 1, k)) for i in range(first, last, 2) for k in range(counts[other])]
    if first:
        pairs += [(device(i, k), device(i, k + 1)) for i in (0, last) for k in range(0, counts[other], 2)]
    return lax.ppermute(x, ("gx", "gy"), pairs + [(b, a) for a, b in pairs])


def call(kernel, name, outs, args, scratch=(), flops=0, nbytes=0, space=pltpu.VMEM):
    return pl.pallas_call(
        kernel,
        out_shape=[jax.ShapeDtypeStruct(s, d) for s, d in outs],
        in_specs=[pl.BlockSpec(memory_space=space)] * len(args),
        out_specs=[pl.BlockSpec(memory_space=pltpu.VMEM)] * len(outs),
        scratch_shapes=list(scratch),
        compiler_params=pltpu.CompilerParams(vmem_limit_bytes=16 << 20),
        cost_estimate=pl.CostEstimate(flops=flops, bytes_accessed=nbytes, transcendentals=0),
        name=name,
    )(*(pltpu.with_memory_space_constraint(a, space) if space is pltpu.HBM else a for a in args))


def lane_edge(center):
    axis = center.ndim - 1
    lane = iota(center.shape, axis)
    last = center.shape[axis] - 1
    below = jnp.where(lane == 0, 0.0, pltpu.roll(center, 1, axis))
    above = jnp.where(lane == last, 0.0, pltpu.roll(center, last, axis))
    return below + above


def moved(center, before, after, beside):
    beside = beside + before + after
    return center + SPREAD * (beside - 6.0 * center) - CARRY * (center - before)


def stencil(ref, c, x0, nx, ny):
    center = ref[c, x0 : x0 + nx, OWN : OWN + ny, :]
    before = ref[c, x0 - 1 : x0 - 1 + nx, OWN : OWN + ny, :]
    after = ref[c, x0 + 1 : x0 + 1 + nx, OWN : OWN + ny, :]
    beside = ref[c, x0 : x0 + nx, OWN - 1 : OWN - 1 + ny, :] + ref[c, x0 : x0 + nx, OWN + 1 : OWN + 1 + ny, :]
    return moved(center, before, after, beside + lane_edge(center))


def stage(v_hbm, tc_hbm, owner_hbm, slot_hbm, height_hbm, load_hbm, v, tc, owner, slot, height, load, to_even, to_odd, sems):
    pairs = ((v_hbm, v), (tc_hbm, tc), (slot_hbm, slot), (height_hbm, height), (load_hbm, load), (owner_hbm, owner))
    copies = [pltpu.make_async_copy(a, b, sems.at[i]) for i, (a, b) in enumerate(pairs)]
    for copy in copies:
        copy.start()
    copies[0].wait()
    comps, nx, ny, _ = v.shape
    ev = even("gy")
    at = 0
    for c in range(comps):
        for k in range(2):
            high = v[c, :, ny - 2 + k, :]
            low = v[c, :, k, :]
            to_even[at : at + nx, :] = jnp.where(ev, high, low)
            to_odd[at : at + nx, :] = jnp.where(ev, low, high)
            at += nx
    copies[1].wait()
    cells = tc[0, :, :].astype(F32) + 1.0
    slots = cells.shape[1]
    for out in (to_even, to_odd):
        out[at : at + 8, :] = jnp.zeros((8, LANES), F32)
        out[at : at + 1, 0:slots] = cells
    for copy in copies[2:]:
        copy.wait()


def as_column(row, n):
    same = iota((n, n), 0) == iota((n, n), 1)
    return jnp.sum(jnp.where(same, row, 0.0), axis=1, keepdims=True)


def as_row(column, n):
    same = iota((n, n), 0) == iota((n, n), 1)
    return jnp.sum(jnp.where(same, column, 0.0), axis=0, keepdims=True)


def picked(flag, a, b, lo, hi):
    return jnp.where(flag, a[lo:hi, :], b[lo:hi, :])


def low_edge(axis, odd, even_, lo, hi):
    return jnp.where(lax.axis_index(axis) > 0, picked(even(axis), odd, even_, lo, hi), 0.0)


def high_edge(axis, odd, even_, lo, hi):
    there = lax.axis_index(axis) < lax.axis_size(axis) - 1
    return jnp.where(there, picked(even(axis), even_, odd, lo, hi), 0.0)


def histogram(v, tc, owner, slot, height, load, count_ref, load_ref, line, to_even, to_odd, sum_ref):
    _, turbines, points = slot.shape
    slots, levels = count_ref.shape[1:]
    comps, nx, ny, _ = v.shape
    cells = nx * ny
    first = lax.axis_index("gy") * slots
    values = v[0, :, :, :].reshape(cells, levels).astype(BF16)
    rows = jnp.dot(pick_slots(tc, cells), values, preferred_element_type=F32)
    zero = jnp.zeros((), BF16)
    for t in range(turbines):
        a = ones_at(one_hot(slots, slot[0, t : t + 1, :] - first))
        at_z = one_hot(levels, height[0, t : t + 1, :])
        weight = load[0, t : t + 1, :]
        high = weight.astype(BF16)
        low = (weight - high.astype(F32)).astype(BF16)
        b = jnp.concatenate([ones_at(at_z), jnp.where(at_z, high, zero), jnp.where(at_z, low, zero)], axis=0)
        both = lax.dot_general(a, b, NT, preferred_element_type=F32)
        count = both[:, :levels]
        count_ref[t] = count.astype(BF16)
        load_ref[t] = both[:, levels : 2 * levels] + both[:, 2 * levels :]
        sum_ref[t : t + 1, :] = jnp.sum(count * rows, axis=0, keepdims=True)

    owner_row = jnp.broadcast_to(owner[...].astype(F32), (turbines, turbines))
    member = owner_row == as_column(owner_row, turbines)
    load_row = as_row(jnp.sum(load[0, :, :], axis=1, keepdims=True), turbines)
    total = jnp.sum(jnp.where(member, load_row, 0.0), axis=1, keepdims=True)
    number = jnp.sum(jnp.where(member, 1.0, 0.0), axis=1, keepdims=True)
    line[...] = jnp.zeros((8, LANES), F32)
    line[SUMS : SUMS + 1, 0:turbines] = as_row(jnp.sum(sum_ref[...], axis=1, keepdims=True), turbines)
    line[SCALE : SCALE + 1, 0:turbines] = as_row(LOAD / (total / (number * points)), turbines)
    line[CELLS : CELLS + 1, 0:slots] = tc[0, :, :].astype(F32) + 1.0

    local = slot[0, :, :] - first
    inside = (local >= 0) & (local < slots)
    code = jnp.where(inside, local * levels + height[0, :, :] + 1, 0).astype(F32)
    ev = even("gx")
    at = 0
    for c in range(comps):
        for k in range(2):
            right, left = v[c, nx - 2 + k, :, :], v[c, k, :, :]
            to_even[at : at + ny, :] = jnp.where(ev, right, left)
            to_odd[at : at + ny, :] = jnp.where(ev, left, right)
            at += ny
    for part in (code, load[0, :, :]):
        for k in range(0, points, LANES):
            for out in (to_even, to_odd):
                out[at : at + turbines, :] = part[:, k : k + LANES]
            at += turbines
    for out in (to_even, to_odd):
        out[at : at + 8, :] = line[...]


def extend(v, yo, ye, xo, xe, field, comps):
    _, nx, ny, _ = v.shape
    for c in comps:
        out = c if len(comps) > 1 else 0
        field[out, 2 : 2 + nx, OWN : OWN + ny, :] = v[c, :, :, :]
        for k in range(2):
            at = (c * 2 + k) * nx
            field[out, 2 : 2 + nx, OWN - 2 + k, :] = low_edge("gy", yo, ye, at, at + nx)
            field[out, 2 : 2 + nx, OWN + ny + k, :] = high_edge("gy", yo, ye, at, at + nx)
            at = (c * 2 + k) * ny
            for x, edge in ((k, low_edge), (2 + nx + k, high_edge)):
                field[out, x, 0:OWN, :] = jnp.zeros((OWN, LANES), F32)
                field[out, x, OWN + ny : PLANE, :] = jnp.zeros((PLANE - OWN - ny, LANES), F32)
                field[out, x, OWN : OWN + ny, :] = edge("gx", xo, xe, at, at + ny)


def edge_slots(cell_row, cells):
    n, slots = cells.shape[0], cell_row.shape[1]
    slot = iota((n, slots), 1).astype(F32)
    return jnp.max(jnp.where(cell_row == cells, slot, NO_SLOT), axis=1, keepdims=True).astype(BF16)


def spread(places, z, weight):
    high = weight.astype(BF16)
    low = (weight - high.astype(F32)).astype(BF16)
    zero = jnp.zeros((), BF16)
    at_z = ones_at(one_hot(LANES, z))
    left = []
    for edge, slot in places:
        here = edge == slot.astype(BF16)
        left += [jnp.where(here, high, zero), jnp.where(here, low, zero)]
    both = lax.dot_general(jnp.concatenate(left, axis=0), at_z, NT, preferred_element_type=F32)
    n = both.shape[0] // len(left)
    return [both[2 * k * n : (2 * k + 1) * n] + both[(2 * k + 1) * n : (2 * k + 2) * n] for k in range(len(places))]


def beside(v, tc, yo, ye, counts, loads, couple, edge_counts, products, field, sums):
    turbines, slots, levels = counts.shape
    _, nx, ny, _ = v.shape
    cells = nx * ny
    field[0, 1 : 1 + nx, OWN : OWN + ny, :] = v[0, :, :, :]
    field[0, 1 : 1 + nx, OWN - 1, :] = low_edge("gy", yo, ye, nx, 2 * nx)
    field[0, 1 : 1 + nx, OWN + ny, :] = high_edge("gy", yo, ye, 0, nx)
    for x in (0, nx + 1):
        field[0, x, OWN : OWN + ny, :] = jnp.zeros((ny, levels), F32)
    update = stencil(field, 0, 1, nx, ny).reshape(cells, levels).astype(BF16)
    values = v[0, :, :, :].reshape(cells, levels).astype(BF16)
    both = jnp.dot(pick_slots(tc, cells), jnp.concatenate([values, update], axis=1), preferred_element_type=F32)
    rows, later = both[:, :levels], both[:, levels:]
    row_x = iota((2 * ny, slots), 0)
    edge = jnp.where(row_x < ny, row_x, row_x + (nx - 2) * ny)
    select = jnp.where(edge == tc[0, :, :], 1.0, 0.0).astype(BF16)
    for t in range(turbines):
        products[t] = (rows * loads[t]).astype(BF16)
        sums[t : t + 1, :] = jnp.sum(counts[t].astype(F32) * later, axis=0, keepdims=True)
        edge_counts[t] = jnp.dot(select, counts[t], preferred_element_type=F32)
    block = 16
    wide = turbines * block
    gram = jnp.zeros((wide, wide), F32)
    for b in range(0, slots, block):
        left = counts[:, b : b + block, :].reshape(wide, levels)
        right = products[:, b : b + block, :].reshape(wide, levels)
        gram = gram + lax.dot_general(left, right, NT, preferred_element_type=F32)
    keep = (iota((wide, wide), 0) & (block - 1)) == (iota((wide, wide), 1) & (block - 1))
    gram = jnp.sum(jnp.where(keep, gram, 0.0).reshape(turbines, block, wide), axis=1)
    select = jnp.where(iota((wide, LANES), 0) // block == iota((wide, LANES), 1), 1.0, 0.0)
    matrix = jnp.dot(gram, select, precision=lax.Precision.HIGHEST, preferred_element_type=F32)
    column = jnp.sum(sums[...], axis=1, keepdims=True)
    couple[...] = jnp.where(iota((turbines, LANES), 1) == turbines, column, matrix)


def reduce_sums(comps, ny, yo, ye, xo, xe, edge_counts, line, couple, out, sums):
    turbines = edge_counts.shape[0]
    ev_x = even("gx")
    left = (SPREAD + CARRY) * low_edge("gx", xo, xe, ny, 2 * ny)
    right = SPREAD * high_edge("gx", xo, xe, 0, ny)
    for t in range(turbines):
        sides = edge_counts[t, 0:ny, :] * left + edge_counts[t, ny : 2 * ny, :] * right
        sums[t : t + 1, :] = jnp.sum(sides, axis=0, keepdims=True)
    lane = iota((turbines, LANES), 1)
    at = xe.shape[0] - 8 + SUMS
    result = couple[...] + jnp.where(lane == turbines, jnp.sum(sums[...], axis=1, keepdims=True), 0.0)
    rows_of = (line[SUMS : SUMS + 1, :], picked(ev_x, xo, xe, at, at + 1), picked(ev_x, xe, xo, at, at + 1))
    for k, row in enumerate(rows_of):
        result = jnp.where(lane == turbines + 1 + k, as_column(row[:, :turbines], turbines), result)
    me = lax.axis_index("gy")
    for k in range(out.shape[0]):
        out[k, 0:turbines, :] = result
        out[k, turbines : turbines + 8, :] = jnp.zeros((8, LANES), F32)
    above = []
    below = []
    for c in range(comps):
        for edge, at in ((low_edge, (c * 2 + 1) * ny), (high_edge, c * 2 * ny)):
            above.append(edge("gx", xo, xe, at + ny - 1, at + ny))
            below.append(edge("gx", xo, xe, at, at + 1))
    for i in range(2 * comps):
        for k in range(out.shape[0]):
            out[k, turbines + i : turbines + i + 1, :] = jnp.where(me + 1 == k, above[i], below[i])


def edges(slots, pieces, v, slot, height, load, yo, ye, xo, xe, edge_x, edge_y, update_ref, strip_ref, field):
    comps, nx, ny, levels = v.shape
    turbines = edge_x.shape[1]
    ev, ev_y = even("gx"), even("gy")
    extend(v, yo, ye, xo, xe, field, tuple(range(comps)))
    ends = iota((nx, LANES), 0)
    for c in range(comps):
        update_ref[c] = stencil(field, c, 1, nx + 2, ny)
        for k, (a, b, y) in enumerate(((yo, ye, 0), (ye, yo, ny - 1))):
            near, far = (c * 2 + 1 - k) * nx, (c * 2 + k) * nx
            center = picked(ev_y, a, b, near, near + nx)
            before = jnp.where(ends == 0, 0.0, pltpu.roll(center, 1, 0))
            after = jnp.where(ends == nx - 1, 0.0, pltpu.roll(center, nx - 1, 0))
            others = picked(ev_y, a, b, far, far + nx) + v[c, :, y, :] + lane_edge(center)
            strip_ref[c, k] = moved(center, before, after, others)

    at = xe.shape[0] - 8 + CELLS
    code_at = comps * 2 * ny
    load_at = code_at + pieces * turbines
    shift = levels.bit_length() - 1
    for k, (a, b) in enumerate(((xo, xe), (xe, xo))):
        cell = picked(ev, a, b, at, at + 1)[:, :slots].astype(jnp.int32) - 1
        edge = edge_slots(cell, iota((ny, slots), 0) + (1 - k) * (nx - 1) * ny)
        codes = [picked(ev, a, b, code_at + i * turbines, code_at + (i + 1) * turbines) for i in range(pieces)]
        codes = jnp.concatenate(codes, axis=1).astype(jnp.int32) - 1
        there = [picked(ev, a, b, load_at + i * turbines, load_at + (i + 1) * turbines) for i in range(pieces)]
        there = jnp.concatenate(there, axis=1)
        for t in range(turbines):
            code = codes[t : t + 1, :]
            (edge_x[k, t],) = spread([(edge, code >> shift)], code & (levels - 1), there[t : t + 1, :])

    me = lax.axis_index("gy")
    at = ye.shape[0] - 8
    lists = []
    for a, b, y in ((yo, ye, ny - 1), (ye, yo, 0)):
        cell = picked(ev_y, a, b, at, at + 1)[:, :slots].astype(jnp.int32) - 1
        lists.append(edge_slots(cell, iota((nx, slots), 0) * ny + y))
    for t in range(turbines):
        row = slot[0, t : t + 1, :]
        places = [(edge, row - (me + k) * slots) for edge, k in zip(lists, (-1, 1))]
        edge_y[0, t], edge_y[1, t] = spread(places, height[0, t : t + 1, :], load[0, t : t + 1, :])


def advance(points, got, v, tc, yo, ye, xo, xe, line, loads, edge_x, edge_y, update_ref, strip_ref, out, field, parts):
    comps, nx, ny, levels = v.shape
    turbines, slots, _ = loads.shape
    cells = nx * ny
    ev_x, ev_y = even("gx"), even("gy")
    total = got[0, 0:turbines, :]
    for k in range(1, got.shape[0]):
        total = total + got[k, 0:turbines, :]
    lane = iota((turbines, LANES), 1)

    def column(k):
        return jnp.sum(jnp.where(lane == k, total, 0.0), axis=1, keepdims=True)

    def coefs(scales, sums):
        return -(scales * (FREE_WIND + sums / points))

    at = xe.shape[0] - 8 + SCALE
    scale = as_column(line[SCALE : SCALE + 1, :turbines], turbines)
    own = coefs(scale, column(turbines + 1))
    left = coefs(as_column(picked(ev_x, xo, xe, at, at + 1)[:, :turbines], turbines), column(turbines + 2))
    right = coefs(as_column(picked(ev_x, xe, xo, at, at + 1)[:, :turbines], turbines), column(turbines + 3))
    own_row = jnp.sum(jnp.where(iota((turbines, LANES), 0) == lane, own, 0.0), axis=0, keepdims=True)
    forced = jnp.sum(jnp.where(lane < turbines, total * own_row, 0.0), axis=1, keepdims=True)
    later = coefs(scale, column(turbines) + forced)

    for s in range(0, slots, 16):
        first = jnp.zeros((16, levels), F32)
        second = first
        for t in range(turbines):
            part = loads[t, s : s + 16, :]
            first = first + own[t : t + 1, :] * part
            second = second + later[t : t + 1, :] * part
        for i, rest in enumerate((first, second)):
            for k in range(2):
                piece = rest.astype(BF16)
                rest = rest - piece.astype(F32)
                at = (2 * i + k) * levels
                parts[s : s + 16, at : at + levels] = piece
    row = tc[0, :, :]
    put = jnp.where(iota((cells, slots), 0) == row, 1.0, 0.0).astype(BF16)
    spread_out = jnp.dot(put, parts[...], preferred_element_type=F32)
    pieces = [spread_out[:, k * levels : (k + 1) * levels] for k in range(4)]
    first = (pieces[0] + pieces[1]).reshape(nx, ny, levels)
    second = (pieces[2] + pieces[3]).reshape(nx, ny, levels)
    for c in range(comps):
        push = rounded(rounded(v[c, :, :, :]) * first)
        field[c, 1 : 1 + nx, OWN : OWN + ny, :] = update_ref[c, 1 : 1 + nx, :, :] + push

    sums = []
    for edge, coef in ((edge_x.at[0], left), (edge_x.at[1], right), (edge_y.at[0], own), (edge_y.at[1], own)):
        side = coef[0:1, :] * edge[0]
        for t in range(1, turbines):
            side = side + coef[t : t + 1, :] * edge[t]
        sums.append(side)
    ix, iy = lax.axis_index("gx"), lax.axis_index("gy")
    last_y = lax.axis_size("gy") - 1
    there_x = (ix > 0, ix < lax.axis_size("gx") - 1)
    there_y = (iy > 0, iy < last_y)
    beside_y = (jnp.maximum(iy - 1, 0), jnp.minimum(iy + 1, last_y))
    corner_rows = [jnp.where(there_y[k], got[beside_y[k], turbines : turbines + 8, :], 0.0) for k in range(2)]
    row_x, row_y = iota((nx, LANES), 0), iota((ny, LANES), 0)
    for c in range(comps):
        corner = [[corner_rows[y][c * 2 + x : c * 2 + x + 1, :] for y in range(2)] for x in range(2)]
        for k, (a, b) in enumerate(((xo, xe), (xe, xo))):
            at = (c * 2 + 1 - k) * ny
            x = k * (nx + 1)
            push = rounded(rounded(picked(ev_x, a, b, at, at + ny)) * sums[k])
            extra = jnp.where(row_y == 0, corner[k][0], 0.0) + jnp.where(row_y == ny - 1, corner[k][1], 0.0)
            value = update_ref[c, x, :, :] + SPREAD * extra + push
            field[c, x, OWN : OWN + ny, :] = jnp.where(there_x[k], value, 0.0)
        for k, (a, b) in enumerate(((yo, ye), (ye, yo))):
            at = (c * 2 + 1 - k) * nx
            y = OWN - 1 + k * (ny + 1)
            push = rounded(rounded(picked(ev_y, a, b, at, at + nx)) * sums[2 + k])
            extra = jnp.where(row_x == 0, (SPREAD + CARRY) * corner[0][k], 0.0)
            extra = extra + jnp.where(row_x == nx - 1, SPREAD * corner[1][k], 0.0)
            value = strip_ref[c, k] + extra + push
            field[c, 1 : 1 + nx, y, :] = jnp.where(there_y[k], value, 0.0)
    for c in range(comps):
        now = field[c, 1 : 1 + nx, OWN : OWN + ny, :]
        out[c] = stencil(field, c, 1, nx, ny) + rounded(rounded(now) * second)


def body(velocity, tile_cells, owner, point_slot, point_z, loading):
    comps, nx, ny, levels = velocity.shape
    _, turbines, points = point_slot.shape
    slots = tile_cells.shape[2]
    tiles_y = lax.axis_size("gy")
    pieces = points // LANES
    rows_y = comps * 2 * nx + 8
    rows_x = comps * 2 * ny + 2 * pieces * turbines + 8
    args = (velocity, tile_cells, owner, point_slot, point_z, loading)
    work = {"flops": 26 * turbines * slots * points * levels, "nbytes": 1 << 20}

    def field(n, planes):
        return pltpu.VMEM((n, planes, PLANE, levels), F32)

    v, tc, own, slot, height, load, y_even, y_odd = call(
        stage,
        "stage",
        [(x.shape, x.dtype) for x in args] + [((rows_y, levels), F32)] * 2,
        args,
        [pltpu.SemaphoreType.DMA((len(args),))],
        space=pltpu.HBM,
    )
    yo, ye = swap(y_odd, "gy", 1), swap(y_even, "gy", 0)
    counts, loads, line, x_even, x_odd = call(
        histogram,
        "histogram",
        [
            ((turbines, slots, levels), BF16),
            ((turbines, slots, levels), F32),
            ((8, LANES), F32),
            ((rows_x, levels), F32),
            ((rows_x, levels), F32),
        ],
        (v, tc, own, slot, height, load),
        [pltpu.VMEM((turbines, levels), F32)],
        **work,
    )
    xo, xe = swap(x_odd, "gx", 1), swap(x_even, "gx", 0)
    couple, edge_counts = call(
        beside,
        "beside",
        [((turbines, LANES), F32), ((turbines, 2 * ny, levels), F32)],
        (v, tc, yo, ye, counts, loads),
        [pltpu.VMEM((turbines, slots, levels), BF16), field(1, nx + 2), pltpu.VMEM((turbines, levels), F32)],
        **work,
    )

    def reduce_of(*refs):
        return reduce_sums(comps, ny, *refs)

    (chunk,) = call(
        reduce_of,
        "reduce_sums",
        [((tiles_y, turbines + 8, LANES), F32)],
        (yo, ye, xo, xe, edge_counts, line, couple),
        [pltpu.VMEM((turbines, levels), F32)],
    )
    got = lax.all_to_all(chunk, "gy", 0, 0)

    def edges_of(*refs):
        return edges(slots, pieces, *refs)

    edge_x, edge_y, update, strip = call(
        edges_of,
        "edges",
        [
            ((2, turbines, ny, levels), F32),
            ((2, turbines, nx, levels), F32),
            ((comps, nx + 2, ny, levels), F32),
            ((comps, 2, nx, levels), F32),
        ],
        (v, slot, height, load, yo, ye, xo, xe),
        [field(comps, nx + 4)],
        **work,
    )

    def advance_by(*refs):
        return advance(points, *refs)

    (out,) = call(
        advance_by,
        "advance",
        [(velocity.shape, F32)],
        (got, v, tc, yo, ye, xo, xe, line, loads, edge_x, edge_y, update, strip),
        [field(comps, nx + 2), pltpu.VMEM((slots, 4 * levels), BF16)],
    )
    return out


def solution(mesh):
    in_specs = (
        P(None, "gx", "gy", None),
        P("gx", "gy", None),
        P("gx", None),
        P("gx", None, None),
        P("gx", None, None),
        P("gx", None, None),
    )
    out_specs = P(None, "gx", "gy", None)
    return jax.shard_map(body, mesh=mesh, in_specs=in_specs, out_specs=out_specs, check_vma=False)
```

```python
import jax
import jax.numpy as jnp
from jax import lax
from jax.experimental import pallas as pl
from jax.experimental.pallas import tpu as pltpu
from jax.sharding import PartitionSpec as P

SPREAD = 0.12
CARRY = 0.25
FREE_WIND = 1.0
LOAD = 0.6

F32 = jnp.float32
BF16 = jnp.bfloat16
NT = (((1,), (1,)), ((), ()))
LANES = 128
OWN = 8
PLANE = 32
NO_SLOT = -30000.0
SUMS, SCALE, CELLS = 0, 1, 2
SIDE = 64


def iota(shape, axis):
    return lax.broadcasted_iota(jnp.int32, shape, axis)


def rounded(x):
    return x.astype(BF16).astype(F32)


def one_hot(count, row):
    places = iota((count, row.shape[1]), 0).astype(BF16)
    return places == row.astype(BF16)


def ones_at(mask):
    return jnp.where(mask, jnp.ones((), BF16), jnp.zeros((), BF16))


def pick_slots(tc, cells):
    slots = tc.shape[2]
    row = jnp.broadcast_to(tc[0, :, :].astype(F32), (slots, slots))
    same = iota((slots, slots), 0) == iota((slots, slots), 1)
    column = jnp.sum(jnp.where(same, row, 0.0), axis=1, keepdims=True).astype(jnp.int32)
    return jnp.where(iota((slots, cells), 1) == column, 1.0, 0.0).astype(BF16)


def even(axis):
    return lax.rem(lax.axis_index(axis), 2) == 0


def swap(x, axis, first):
    counts = {name: lax.axis_size(name) for name in ("gx", "gy")}
    other = "gy" if axis == "gx" else "gx"

    def device(along, across):
        at = {axis: along, other: across}
        return at["gx"] * counts["gy"] + at["gy"]

    last = counts[axis] - 1
    pairs = [(device(i, k), device(i + 1, k)) for i in range(first, last, 2) for k in range(counts[other])]
    if first:
        pairs += [(device(i, k), device(i, k + 1)) for i in (0, last) for k in range(0, counts[other], 2)]
    return lax.ppermute(x, ("gx", "gy"), pairs + [(b, a) for a, b in pairs])


def call(kernel, name, outs, args, scratch=(), flops=0, nbytes=0, space=pltpu.VMEM, out_space=pltpu.VMEM):
    return pl.pallas_call(
        kernel,
        out_shape=[jax.ShapeDtypeStruct(s, d) for s, d in outs],
        in_specs=[pl.BlockSpec(memory_space=space)] * len(args),
        out_specs=[pl.BlockSpec(memory_space=out_space)] * len(outs),
        scratch_shapes=list(scratch),
        compiler_params=pltpu.CompilerParams(vmem_limit_bytes=16 << 20),
        cost_estimate=pl.CostEstimate(flops=flops, bytes_accessed=nbytes, transcendentals=0),
        name=name,
    )(*(pltpu.with_memory_space_constraint(a, space) if space is pltpu.HBM else a for a in args))


def lane_edge(center):
    axis = center.ndim - 1
    lane = iota(center.shape, axis)
    last = center.shape[axis] - 1
    below = jnp.where(lane == 0, 0.0, pltpu.roll(center, 1, axis))
    above = jnp.where(lane == last, 0.0, pltpu.roll(center, last, axis))
    return below + above


def moved(center, before, after, beside):
    beside = beside + before + after
    return center + SPREAD * (beside - 6.0 * center) - CARRY * (center - before)


def stencil(ref, c, x0, nx, ny):
    center = ref[c, x0 : x0 + nx, OWN : OWN + ny, :]
    before = ref[c, x0 - 1 : x0 - 1 + nx, OWN : OWN + ny, :]
    after = ref[c, x0 + 1 : x0 + 1 + nx, OWN : OWN + ny, :]
    beside = ref[c, x0 : x0 + nx, OWN - 1 : OWN - 1 + ny, :] + ref[c, x0 : x0 + nx, OWN + 1 : OWN + 1 + ny, :]
    return moved(center, before, after, beside + lane_edge(center))


def stage(v_hbm, tc_hbm, owner_hbm, slot_hbm, height_hbm, load_hbm, v, tc, owner, slot, height, load, to_even, to_odd, sems):
    pairs = ((v_hbm, v), (tc_hbm, tc), (slot_hbm, slot), (height_hbm, height), (load_hbm, load), (owner_hbm, owner))
    copies = [pltpu.make_async_copy(a, b, sems.at[i]) for i, (a, b) in enumerate(pairs)]
    for copy in copies:
        copy.start()
    copies[0].wait()
    comps, nx, ny, _ = v.shape
    ev = even("gy")
    at = 0
    for c in range(comps):
        for k in range(2):
            high = v[c, :, ny - 2 + k, :]
            low = v[c, :, k, :]
            to_even[at : at + nx, :] = jnp.where(ev, high, low)
            to_odd[at : at + nx, :] = jnp.where(ev, low, high)
            at += nx
    copies[1].wait()
    cells = tc[0, :, :].astype(F32) + 1.0
    slots = cells.shape[1]
    for out in (to_even, to_odd):
        out[at : at + 8, :] = jnp.zeros((8, LANES), F32)
        out[at : at + 1, 0:slots] = cells
    for copy in copies[2:]:
        copy.wait()


def as_column(row, n, start=0):
    shape = (n, row.shape[1])
    return jnp.sum(jnp.where(iota(shape, 0) + start == iota(shape, 1), row, 0.0), axis=1, keepdims=True)


def as_row(column, lanes, start=0):
    shape = (column.shape[0], lanes)
    return jnp.sum(jnp.where(iota(shape, 0) + start == iota(shape, 1), column, 0.0), axis=0, keepdims=True)


def picked(flag, a, b, lo, hi):
    return jnp.where(flag, a[lo:hi, :], b[lo:hi, :])


def low_edge(axis, odd, even_, lo, hi):
    return jnp.where(lax.axis_index(axis) > 0, picked(even(axis), odd, even_, lo, hi), 0.0)


def high_edge(axis, odd, even_, lo, hi):
    there = lax.axis_index(axis) < lax.axis_size(axis) - 1
    return jnp.where(there, picked(even(axis), even_, odd, lo, hi), 0.0)


def histogram(v, tc, owner, slot, height, load, count_ref, line, to_even, to_odd, sum_ref):
    _, turbines, points = slot.shape
    slots, levels = count_ref.shape[1:]
    comps, nx, ny, _ = v.shape
    cells = nx * ny
    first = lax.axis_index("gy") * slots
    values = v[0, :, :, :].reshape(cells, levels).astype(BF16)
    rows = jnp.dot(pick_slots(tc, cells), values, preferred_element_type=F32)
    for t in range(turbines):
        a = ones_at(one_hot(slots, slot[0, t : t + 1, :] - first))
        b = ones_at(one_hot(levels, height[0, t : t + 1, :]))
        count = lax.dot_general(a, b, NT, preferred_element_type=F32)
        count_ref[t] = count.astype(BF16)
        sum_ref[t : t + 1, :] = jnp.sum(count * rows, axis=0, keepdims=True)

    owner_row = jnp.broadcast_to(owner[...].astype(F32), (turbines, turbines))
    member = owner_row == as_column(owner_row, turbines)
    load_row = as_row(jnp.sum(load[0, :, :], axis=1, keepdims=True), turbines)
    total = jnp.sum(jnp.where(member, load_row, 0.0), axis=1, keepdims=True)
    number = jnp.sum(jnp.where(member, 1.0, 0.0), axis=1, keepdims=True)
    line[...] = jnp.zeros((8, LANES), F32)
    line[SUMS : SUMS + 1, :] = as_row(jnp.sum(sum_ref[...], axis=1, keepdims=True), LANES, SIDE)
    line[SCALE : SCALE + 1, :] = as_row(LOAD / (total / (number * points)), LANES)
    line[CELLS : CELLS + 1, 0:slots] = tc[0, :, :].astype(F32) + 1.0

    local = slot[0, :, :] - first
    inside = (local >= 0) & (local < slots)
    code = jnp.where(inside, local * levels + height[0, :, :] + 1, 0).astype(F32)
    ev = even("gx")
    at = 0
    for c in range(comps):
        for k in range(2):
            right, left = v[c, nx - 2 + k, :, :], v[c, k, :, :]
            to_even[at : at + ny, :] = jnp.where(ev, right, left)
            to_odd[at : at + ny, :] = jnp.where(ev, left, right)
            at += ny
    for part in (code, load[0, :, :]):
        for k in range(0, points, LANES):
            for out in (to_even, to_odd):
                out[at : at + turbines, :] = part[:, k : k + LANES]
            at += turbines
    for out in (to_even, to_odd):
        out[at : at + 8, :] = line[...]


def extend(v, yo, ye, xo, xe, field, comps):
    _, nx, ny, _ = v.shape
    for c in comps:
        out = c if len(comps) > 1 else 0
        field[out, 2 : 2 + nx, OWN : OWN + ny, :] = v[c, :, :, :]
        for k in range(2):
            at = (c * 2 + k) * nx
            field[out, 2 : 2 + nx, OWN - 2 + k, :] = low_edge("gy", yo, ye, at, at + nx)
            field[out, 2 : 2 + nx, OWN + ny + k, :] = high_edge("gy", yo, ye, at, at + nx)
            at = (c * 2 + k) * ny
            for x, edge in ((k, low_edge), (2 + nx + k, high_edge)):
                field[out, x, 0:OWN, :] = jnp.zeros((OWN, LANES), F32)
                field[out, x, OWN + ny : PLANE, :] = jnp.zeros((PLANE - OWN - ny, LANES), F32)
                field[out, x, OWN : OWN + ny, :] = edge("gx", xo, xe, at, at + ny)


def edge_slots(cell_row, cells):
    n, slots = cells.shape[0], cell_row.shape[1]
    slot = iota((n, slots), 1).astype(F32)
    return jnp.max(jnp.where(cell_row == cells, slot, NO_SLOT), axis=1, keepdims=True).astype(BF16)


def spread(places, z, weight):
    high = weight.astype(BF16)
    low = (weight - high.astype(F32)).astype(BF16)
    zero = jnp.zeros((), BF16)
    at_z = ones_at(one_hot(LANES, z))
    left = []
    for edge, slot in places:
        here = edge == slot.astype(BF16)
        left += [jnp.where(here, high, zero), jnp.where(here, low, zero)]
    both = lax.dot_general(jnp.concatenate(left, axis=0), at_z, NT, preferred_element_type=F32)
    n = both.shape[0] // len(left)
    return [both[2 * k * n : (2 * k + 1) * n] + both[(2 * k + 1) * n : (2 * k + 2) * n] for k in range(len(places))]


def pair_up(v, tc, slot, height, load, counts, loads, matrix, edge_counts, products):
    turbines, slots, levels = counts.shape
    _, nx, ny, _ = v.shape
    cells = nx * ny
    first = lax.axis_index("gy") * slots
    zero = jnp.zeros((), BF16)
    values = v[0, :, :, :].reshape(cells, levels).astype(BF16)
    rows = jnp.dot(pick_slots(tc, cells), values, preferred_element_type=F32)
    row_x = iota((2 * ny, slots), 0)
    edge = jnp.where(row_x < ny, row_x, row_x + (nx - 2) * ny)
    select = jnp.where(edge == tc[0, :, :], 1.0, 0.0).astype(BF16)
    for t in range(turbines):
        a = ones_at(one_hot(slots, slot[0, t : t + 1, :] - first))
        at_z = one_hot(levels, height[0, t : t + 1, :])
        weight = load[0, t : t + 1, :]
        high = weight.astype(BF16)
        low = (weight - high.astype(F32)).astype(BF16)
        b = jnp.concatenate([jnp.where(at_z, high, zero), jnp.where(at_z, low, zero)], axis=0)
        both = lax.dot_general(a, b, NT, preferred_element_type=F32)
        both = both[:, :levels] + both[:, levels:]
        loads[t] = both
        products[t] = (rows * both).astype(BF16)
        edge_counts[t] = jnp.dot(select, counts[t], preferred_element_type=F32)
    block = 16
    wide = turbines * block
    gram = jnp.zeros((wide, wide), F32)
    for b in range(0, slots, block):
        left = counts[:, b : b + block, :].reshape(wide, levels)
        right = products[:, b : b + block, :].reshape(wide, levels)
        gram = gram + lax.dot_general(left, right, NT, preferred_element_type=F32)
    keep = (iota((wide, wide), 0) & (block - 1)) == (iota((wide, wide), 1) & (block - 1))
    gram = jnp.sum(jnp.where(keep, gram, 0.0).reshape(turbines, block, wide), axis=1)
    select = jnp.where(iota((wide, LANES), 0) // block == iota((wide, LANES), 1), 1.0, 0.0)
    matrix[...] = jnp.dot(gram, select, precision=lax.Precision.HIGHEST, preferred_element_type=F32)


def beside(v, tc, yo, ye, counts, matrix, couple, field, sums):
    turbines, _, levels = counts.shape
    _, nx, ny, _ = v.shape
    cells = nx * ny
    field[0, 1 : 1 + nx, OWN : OWN + ny, :] = v[0, :, :, :]
    field[0, 1 : 1 + nx, OWN - 1, :] = low_edge("gy", yo, ye, nx, 2 * nx)
    field[0, 1 : 1 + nx, OWN + ny, :] = high_edge("gy", yo, ye, 0, nx)
    for x in (0, nx + 1):
        field[0, x, OWN : OWN + ny, :] = jnp.zeros((ny, levels), F32)
    update = stencil(field, 0, 1, nx, ny).reshape(cells, levels).astype(BF16)
    later = jnp.dot(pick_slots(tc, cells), update, preferred_element_type=F32)
    for t in range(turbines):
        sums[t : t + 1, :] = jnp.sum(counts[t].astype(F32) * later, axis=0, keepdims=True)
    column = jnp.sum(sums[...], axis=1, keepdims=True)
    couple[...] = jnp.where(iota((turbines, LANES), 1) == turbines, column, matrix[...])


def reduce_sums(comps, ny, yo, ye, xo, xe, edge_counts, line, couple, out, sums, corners):
    turbines = edge_counts.shape[0]
    ev_x = even("gx")
    left = (SPREAD + CARRY) * low_edge("gx", xo, xe, ny, 2 * ny)
    right = SPREAD * high_edge("gx", xo, xe, 0, ny)
    for t in range(turbines):
        sides = edge_counts[t, 0:ny, :] * left + edge_counts[t, ny : 2 * ny, :] * right
        sums[t : t + 1, :] = jnp.sum(sides, axis=0, keepdims=True)
    corners[...] = jnp.zeros((2, 8, LANES), F32)
    for c in range(comps):
        for i, (edge, at) in enumerate(((low_edge, (c * 2 + 1) * ny), (high_edge, c * 2 * ny))):
            corners[0, 2 * c + i : 2 * c + i + 1, :] = edge("gx", xo, xe, at, at + 1)
            corners[1, 2 * c + i : 2 * c + i + 1, :] = edge("gx", xo, xe, at + ny - 1, at + ny)
    at = xe.shape[0] - 8 + SUMS
    lane, row = iota((turbines, LANES), 1), iota((turbines, LANES), 0)
    result = couple[...]
    rows_of = (line[SUMS : SUMS + 1, :], picked(ev_x, xo, xe, at, at + 1), picked(ev_x, xe, xo, at, at + 1))
    for k, sums_row in enumerate(rows_of):
        result = result + jnp.where(row == k, sums_row, 0.0)
    result = result + jnp.where(lane == turbines, jnp.sum(sums[...], axis=1, keepdims=True), 0.0)
    me = lax.axis_index("gy")
    below, above = corners[0], corners[1]
    for k in range(out.shape[0]):
        out[k, 0:turbines, :] = result
        out[k, turbines : turbines + 8, :] = jnp.where(me + 1 == k, above, below)


def edges(slots, pieces, v, slot, height, load, yo, ye, xo, xe, line, edge_x, edge_y, update_ref, strip_ref, scales, field):
    comps, nx, ny, levels = v.shape
    turbines = edge_x.shape[1]
    ev, ev_y = even("gx"), even("gy")
    extend(v, yo, ye, xo, xe, field, tuple(range(comps)))
    ends = iota((nx, LANES), 0)
    for c in range(comps):
        update_ref[c] = stencil(field, c, 1, nx + 2, ny)
        for k, (a, b, y) in enumerate(((yo, ye, 0), (ye, yo, ny - 1))):
            near, far = (c * 2 + 1 - k) * nx, (c * 2 + k) * nx
            center = picked(ev_y, a, b, near, near + nx)
            before = jnp.where(ends == 0, 0.0, pltpu.roll(center, 1, 0))
            after = jnp.where(ends == nx - 1, 0.0, pltpu.roll(center, nx - 1, 0))
            others = picked(ev_y, a, b, far, far + nx) + v[c, :, y, :] + lane_edge(center)
            strip_ref[c, k] = moved(center, before, after, others)

    at = xe.shape[0] - 8 + SCALE
    rows_of = (line[SCALE : SCALE + 1, :], picked(ev, xo, xe, at, at + 1), picked(ev, xe, xo, at, at + 1))
    for k, row in enumerate(rows_of):
        scales[k] = jnp.broadcast_to(as_column(row, turbines), (turbines, LANES))
    at = xe.shape[0] - 8 + CELLS
    code_at = comps * 2 * ny
    load_at = code_at + pieces * turbines
    shift = levels.bit_length() - 1
    for k, (a, b) in enumerate(((xo, xe), (xe, xo))):
        cell = picked(ev, a, b, at, at + 1)[:, :slots].astype(jnp.int32) - 1
        edge = edge_slots(cell, iota((ny, slots), 0) + (1 - k) * (nx - 1) * ny)
        codes = [picked(ev, a, b, code_at + i * turbines, code_at + (i + 1) * turbines) for i in range(pieces)]
        codes = jnp.concatenate(codes, axis=1).astype(jnp.int32) - 1
        there = [picked(ev, a, b, load_at + i * turbines, load_at + (i + 1) * turbines) for i in range(pieces)]
        there = jnp.concatenate(there, axis=1)
        for t in range(turbines):
            code = codes[t : t + 1, :]
            (edge_x[k, t],) = spread([(edge, code >> shift)], code & (levels - 1), there[t : t + 1, :])

    me = lax.axis_index("gy")
    at = ye.shape[0] - 8
    lists = []
    for a, b, y in ((yo, ye, ny - 1), (ye, yo, 0)):
        cell = picked(ev_y, a, b, at, at + 1)[:, :slots].astype(jnp.int32) - 1
        lists.append(edge_slots(cell, iota((nx, slots), 0) * ny + y))
    for t in range(turbines):
        row = slot[0, t : t + 1, :]
        places = [(edge, row - (me + k) * slots) for edge, k in zip(lists, (-1, 1))]
        edge_y[0, t], edge_y[1, t] = spread(places, height[0, t : t + 1, :], load[0, t : t + 1, :])


def advance(points, got, v, tc, yo, ye, xo, xe, scales, loads, edge_x, edge_y, update_ref, strip_ref, out, field, parts, result, sems):
    comps, nx, ny, levels = v.shape
    turbines, slots, _ = loads.shape
    cells = nx * ny
    ev_x, ev_y = even("gx"), even("gy")
    total = got[0, 0:turbines, :]
    for k in range(1, got.shape[0]):
        total = total + got[k, 0:turbines, :]
    lane = iota((turbines, LANES), 1)

    def coefs(scale, sums):
        return -(scale * (FREE_WIND + sums / points))

    own, left, right = (coefs(scales[k], as_column(total[k : k + 1, :], turbines, SIDE)) for k in range(3))
    own_row = jnp.sum(jnp.where(iota((turbines, LANES), 0) == lane, own, 0.0), axis=0, keepdims=True)
    forced = jnp.sum(jnp.where(lane < turbines, total * own_row, 0.0), axis=1, keepdims=True)
    plain = jnp.sum(jnp.where(lane == turbines, total, 0.0), axis=1, keepdims=True)
    later = coefs(scales[0], plain + forced)

    for s in range(0, slots, 16):
        first = jnp.zeros((16, levels), F32)
        second = first
        for t in range(turbines):
            part = loads[t, s : s + 16, :]
            first = first + own[t : t + 1, :] * part
            second = second + later[t : t + 1, :] * part
        for i, rest in enumerate((first, second)):
            for k in range(2):
                piece = rest.astype(BF16)
                rest = rest - piece.astype(F32)
                at = (2 * i + k) * levels
                parts[s : s + 16, at : at + levels] = piece
    row = tc[0, :, :]
    put = jnp.where(iota((cells, slots), 0) == row, 1.0, 0.0).astype(BF16)
    spread_out = jnp.dot(put, parts[...], preferred_element_type=F32)
    pieces = [spread_out[:, k * levels : (k + 1) * levels] for k in range(4)]
    first = (pieces[0] + pieces[1]).reshape(nx, ny, levels)
    second = (pieces[2] + pieces[3]).reshape(nx, ny, levels)
    for c in range(comps):
        push = rounded(rounded(v[c, :, :, :]) * first)
        field[c, 1 : 1 + nx, OWN : OWN + ny, :] = update_ref[c, 1 : 1 + nx, :, :] + push

    sums = []
    for edge, coef in ((edge_x.at[0], left), (edge_x.at[1], right), (edge_y.at[0], own), (edge_y.at[1], own)):
        side = coef[0:1, :] * edge[0]
        for t in range(1, turbines):
            side = side + coef[t : t + 1, :] * edge[t]
        sums.append(side)
    ix, iy = lax.axis_index("gx"), lax.axis_index("gy")
    last_y = lax.axis_size("gy") - 1
    there_x = (ix > 0, ix < lax.axis_size("gx") - 1)
    there_y = (iy > 0, iy < last_y)
    beside_y = (jnp.maximum(iy - 1, 0), jnp.minimum(iy + 1, last_y))
    corner_rows = [jnp.where(there_y[k], got[beside_y[k], turbines : turbines + 8, :], 0.0) for k in range(2)]
    row_x, row_y = iota((nx, LANES), 0), iota((ny, LANES), 0)
    for c in range(comps):
        corner = [[corner_rows[y][c * 2 + x : c * 2 + x + 1, :] for y in range(2)] for x in range(2)]
        for k, (a, b) in enumerate(((xo, xe), (xe, xo))):
            at = (c * 2 + 1 - k) * ny
            x = k * (nx + 1)
            push = rounded(rounded(picked(ev_x, a, b, at, at + ny)) * sums[k])
            extra = jnp.where(row_y == 0, corner[k][0], 0.0) + jnp.where(row_y == ny - 1, corner[k][1], 0.0)
            value = update_ref[c, x, :, :] + SPREAD * extra + push
            field[c, x, OWN : OWN + ny, :] = jnp.where(there_x[k], value, 0.0)
        for k, (a, b) in enumerate(((yo, ye), (ye, yo))):
            at = (c * 2 + 1 - k) * nx
            y = OWN - 1 + k * (ny + 1)
            push = rounded(rounded(picked(ev_y, a, b, at, at + nx)) * sums[2 + k])
            extra = jnp.where(row_x == 0, (SPREAD + CARRY) * corner[0][k], 0.0)
            extra = extra + jnp.where(row_x == nx - 1, SPREAD * corner[1][k], 0.0)
            value = strip_ref[c, k] + extra + push
            field[c, 1 : 1 + nx, y, :] = jnp.where(there_y[k], value, 0.0)
    copies = []
    for c in range(comps):
        now = field[c, 1 : 1 + nx, OWN : OWN + ny, :]
        result[c] = stencil(field, c, 1, nx, ny) + rounded(rounded(now) * second)
        copies.append(pltpu.make_async_copy(result.at[c], out.at[c], sems.at[c]))
        copies[c].start()
    for copy in copies:
        copy.wait()


def body(velocity, tile_cells, owner, point_slot, point_z, loading):
    comps, nx, ny, levels = velocity.shape
    _, turbines, points = point_slot.shape
    slots = tile_cells.shape[2]
    tiles_y = lax.axis_size("gy")
    pieces = points // LANES
    rows_y = comps * 2 * nx + 8
    rows_x = comps * 2 * ny + 2 * pieces * turbines + 8
    args = (velocity, tile_cells, owner, point_slot, point_z, loading)
    work = {"flops": 26 * turbines * slots * points * levels, "nbytes": 1 << 20}

    def field(n, planes):
        return pltpu.VMEM((n, planes, PLANE, levels), F32)

    v, tc, own, slot, height, load, y_even, y_odd = call(
        stage,
        "stage",
        [(x.shape, x.dtype) for x in args] + [((rows_y, levels), F32)] * 2,
        args,
        [pltpu.SemaphoreType.DMA((len(args),))],
        space=pltpu.HBM,
    )
    yo, ye = swap(y_odd, "gy", 1), swap(y_even, "gy", 0)
    counts, line, x_even, x_odd = call(
        histogram,
        "histogram",
        [
            ((turbines, slots, levels), BF16),
            ((8, LANES), F32),
            ((rows_x, levels), F32),
            ((rows_x, levels), F32),
        ],
        (v, tc, own, slot, height, load),
        [pltpu.VMEM((turbines, levels), F32)],
        **work,
    )
    xo, xe = swap(x_odd, "gx", 1), swap(x_even, "gx", 0)
    loads, matrix, edge_counts = call(
        pair_up,
        "pair_up",
        [((turbines, slots, levels), F32), ((turbines, LANES), F32), ((turbines, 2 * ny, levels), F32)],
        (v, tc, slot, height, load, counts),
        [pltpu.VMEM((turbines, slots, levels), BF16)],
        **work,
    )
    (couple,) = call(
        beside,
        "beside",
        [((turbines, LANES), F32)],
        (v, tc, yo, ye, counts, matrix),
        [field(1, nx + 2), pltpu.VMEM((turbines, levels), F32)],
        flops=work["flops"] // 4,
        nbytes=work["nbytes"],
    )

    def reduce_of(*refs):
        return reduce_sums(comps, ny, *refs)

    (chunk,) = call(
        reduce_of,
        "reduce_sums",
        [((tiles_y, turbines + 8, LANES), F32)],
        (yo, ye, xo, xe, edge_counts, line, couple),
        [pltpu.VMEM((turbines, levels), F32), pltpu.VMEM((2, 8, LANES), F32)],
    )
    got = lax.all_to_all(chunk, "gy", 0, 0)

    def edges_of(*refs):
        return edges(slots, pieces, *refs)

    edge_x, edge_y, update, strip, scales = call(
        edges_of,
        "edges",
        [
            ((2, turbines, ny, levels), F32),
            ((2, turbines, nx, levels), F32),
            ((comps, nx + 2, ny, levels), F32),
            ((comps, 2, nx, levels), F32),
            ((3, turbines, LANES), F32),
        ],
        (v, slot, height, load, yo, ye, xo, xe, line),
        [field(comps, nx + 4)],
        **work,
    )

    def advance_by(*refs):
        return advance(points, *refs)

    (out,) = call(
        advance_by,
        "advance",
        [(velocity.shape, F32)],
        (got, v, tc, yo, ye, xo, xe, scales, loads, edge_x, edge_y, update, strip),
        [
            field(comps, nx + 2),
            pltpu.VMEM((slots, 4 * levels), BF16),
            pltpu.VMEM(velocity.shape, F32),
            pltpu.SemaphoreType.DMA((comps,)),
        ],
        out_space=pltpu.HBM,
    )
    return out


def solution(mesh):
    in_specs = (
        P(None, "gx", "gy", None),
        P("gx", "gy", None),
        P("gx", None),
        P("gx", None, None),
        P("gx", None, None),
        P("gx", None, None),
    )
    out_specs = P(None, "gx", "gy", None)
    return jax.shard_map(body, mesh=mesh, in_specs=in_specs, out_specs=out_specs, check_vma=False)
```

```python
import jax
import jax.numpy as jnp
from jax import lax
from jax.experimental import pallas as pl
from jax.experimental.pallas import tpu as pltpu
from jax.sharding import PartitionSpec as P

SPREAD = 0.12
CARRY = 0.25
FREE_WIND = 1.0
LOAD = 0.6

F32 = jnp.float32
BF16 = jnp.bfloat16
NT = (((1,), (1,)), ((), ()))
LANES = 128
OWN = 8
PLANE = 32
NO_SLOT = -30000.0
SUMS, SCALE, CELLS = 0, 1, 2


def iota(shape, axis):
    return lax.broadcasted_iota(jnp.int32, shape, axis)


def rounded(x):
    return x.astype(BF16).astype(F32)


def one_hot(count, row):
    places = iota((count, row.shape[1]), 0).astype(BF16)
    return places == row.astype(BF16)


def ones_at(mask):
    return jnp.where(mask, jnp.ones((), BF16), jnp.zeros((), BF16))


def pick_slots(tc, cells):
    slots = tc.shape[2]
    row = jnp.broadcast_to(tc[0, :, :].astype(F32), (slots, slots))
    same = iota((slots, slots), 0) == iota((slots, slots), 1)
    column = jnp.sum(jnp.where(same, row, 0.0), axis=1, keepdims=True).astype(jnp.int32)
    return jnp.where(iota((slots, cells), 1) == column, 1.0, 0.0).astype(BF16)


def even(axis):
    return lax.rem(lax.axis_index(axis), 2) == 0


def swap(x, axis, first):
    counts = {name: lax.axis_size(name) for name in ("gx", "gy")}
    other = "gy" if axis == "gx" else "gx"

    def device(along, across):
        at = {axis: along, other: across}
        return at["gx"] * counts["gy"] + at["gy"]

    last = counts[axis] - 1
    pairs = [(device(i, k), device(i + 1, k)) for i in range(first, last, 2) for k in range(counts[other])]
    if first:
        pairs += [(device(i, k), device(i, k + 1)) for i in (0, last) for k in range(0, counts[other], 2)]
    return lax.ppermute(x, ("gx", "gy"), pairs + [(b, a) for a, b in pairs])


def call(kernel, name, outs, args, scratch=(), flops=0, nbytes=0, space=pltpu.VMEM, out_space=pltpu.VMEM):
    return pl.pallas_call(
        kernel,
        out_shape=[jax.ShapeDtypeStruct(s, d) for s, d in outs],
        in_specs=[pl.BlockSpec(memory_space=space)] * len(args),
        out_specs=[pl.BlockSpec(memory_space=out_space)] * len(outs),
        scratch_shapes=list(scratch),
        compiler_params=pltpu.CompilerParams(vmem_limit_bytes=16 << 20),
        cost_estimate=pl.CostEstimate(flops=flops, bytes_accessed=nbytes, transcendentals=0),
        name=name,
    )(*(pltpu.with_memory_space_constraint(a, space) if space is pltpu.HBM else a for a in args))


def lane_edge(center):
    axis = center.ndim - 1
    lane = iota(center.shape, axis)
    last = center.shape[axis] - 1
    below = jnp.where(lane == 0, 0.0, pltpu.roll(center, 1, axis))
    above = jnp.where(lane == last, 0.0, pltpu.roll(center, last, axis))
    return below + above


def moved(center, before, after, beside):
    own = (1.0 - 6.0 * SPREAD - CARRY) * center
    return own + SPREAD * (beside + after) + (SPREAD + CARRY) * before


def stencil(ref, c, x0, nx, ny):
    center = ref[c, x0 : x0 + nx, OWN : OWN + ny, :]
    before = ref[c, x0 - 1 : x0 - 1 + nx, OWN : OWN + ny, :]
    after = ref[c, x0 + 1 : x0 + 1 + nx, OWN : OWN + ny, :]
    beside = ref[c, x0 : x0 + nx, OWN - 1 : OWN - 1 + ny, :] + ref[c, x0 : x0 + nx, OWN + 1 : OWN + 1 + ny, :]
    return moved(center, before, after, beside + lane_edge(center))


def as_column(row, n, start=0):
    shape = (n, row.shape[1])
    return jnp.sum(jnp.where(iota(shape, 0) + start == iota(shape, 1), row, 0.0), axis=1, keepdims=True)


def as_row(column, lanes, start=0):
    shape = (column.shape[0], lanes)
    return jnp.sum(jnp.where(iota(shape, 0) + start == iota(shape, 1), column, 0.0), axis=0, keepdims=True)


def packing(turbines):
    per_row = LANES // turbines
    rows = turbines // per_row
    return rows, per_row, 2 * rows + 3, -(-(2 * rows + 9) // 16) * 16


def in_parts(x, count):
    parts = []
    for _ in range(count):
        parts.append(rounded(x))
        x = x - parts[-1]
    return parts


def picked(flag, a, b, lo, hi):
    return jnp.where(flag, a[lo:hi, :], b[lo:hi, :])


def low_edge(axis, odd, even_, lo, hi):
    return jnp.where(lax.axis_index(axis) > 0, picked(even(axis), odd, even_, lo, hi), 0.0)


def high_edge(axis, odd, even_, lo, hi):
    there = lax.axis_index(axis) < lax.axis_size(axis) - 1
    return jnp.where(there, picked(even(axis), even_, odd, lo, hi), 0.0)


def prepare(
    v_hbm, tc_hbm, owner_hbm, slot_hbm, height_hbm, load_hbm,
    v, tc, slot, height, load, count_ref, line, y_even, y_odd, x_even, x_odd,
    owner, exact, sum_ref, sems,
):
    pairs = ((slot_hbm, slot), (height_hbm, height), (tc_hbm, tc), (load_hbm, load), (owner_hbm, owner), (v_hbm, v))
    copies = [pltpu.make_async_copy(a, b, sems.at[i]) for i, (a, b) in enumerate(pairs)]
    for copy in copies:
        copy.start()
    _, turbines, points = slot.shape
    slots, levels = count_ref.shape[1:]
    comps, nx, ny, _ = v.shape
    cells = nx * ny
    first = lax.axis_index("gy") * slots
    copies[0].wait()
    copies[1].wait()
    for t in range(turbines):
        a = ones_at(one_hot(slots, slot[0, t : t + 1, :] - first))
        b = ones_at(one_hot(levels, height[0, t : t + 1, :]))
        exact[t] = lax.dot_general(a, b, NT, preferred_element_type=F32)
    for copy in copies[2:]:
        copy.wait()

    ev = even("gy")
    at = 0
    for c in range(comps):
        for k in range(2):
            high = v[c, :, ny - 2 + k, :]
            low = v[c, :, k, :]
            y_even[at : at + nx, :] = jnp.where(ev, high, low)
            y_odd[at : at + nx, :] = jnp.where(ev, low, high)
            at += nx
    values = v[0, :, :, :].reshape(cells, levels).astype(BF16)
    rows = jnp.dot(pick_slots(tc, cells), values, preferred_element_type=F32)
    for t in range(turbines):
        count = exact[t]
        count_ref[t] = count.astype(BF16)
        sum_ref[t : t + 1, :] = jnp.sum(count * rows, axis=0, keepdims=True)

    owner_row = jnp.broadcast_to(owner[...].astype(F32), (turbines, turbines))
    member = owner_row == as_column(owner_row, turbines)
    load_row = as_row(jnp.sum(load[0, :, :], axis=1, keepdims=True), turbines)
    total = jnp.sum(jnp.where(member, load_row, 0.0), axis=1, keepdims=True)
    number = jnp.sum(jnp.where(member, 1.0, 0.0), axis=1, keepdims=True)
    line[...] = jnp.zeros((8, LANES), F32)
    line[SUMS : SUMS + 1, :] = as_row(jnp.sum(sum_ref[...], axis=1, keepdims=True), LANES)
    line[SCALE : SCALE + 1, :] = as_row(LOAD / (total / (number * points)), LANES)
    line[CELLS : CELLS + 1, 0:slots] = tc[0, :, :].astype(F32) + 1.0
    for out in (y_even, y_odd):
        out[at : at + 8, :] = jnp.zeros((8, LANES), F32)
        out[at : at + 1, :] = line[CELLS : CELLS + 1, :]

    local = slot[0, :, :] - first
    inside = (local >= 0) & (local < slots)
    code = jnp.where(inside, local * levels + height[0, :, :] + 1, 0).astype(F32)
    ev = even("gx")
    at = 0
    for c in range(comps):
        for k in range(2):
            right, left = v[c, nx - 2 + k, :, :], v[c, k, :, :]
            x_even[at : at + ny, :] = jnp.where(ev, right, left)
            x_odd[at : at + ny, :] = jnp.where(ev, left, right)
            at += ny
    for part in (code, load[0, :, :]):
        for k in range(0, points, LANES):
            for out in (x_even, x_odd):
                out[at : at + turbines, :] = part[:, k : k + LANES]
            at += turbines
    for out in (x_even, x_odd):
        out[at : at + 8, :] = line[...]


def extend(v, yo, ye, xo, xe, field, comps):
    _, nx, ny, _ = v.shape
    for c in comps:
        out = c if len(comps) > 1 else 0
        field[out, 2 : 2 + nx, OWN : OWN + ny, :] = v[c, :, :, :]
        for k in range(2):
            at = (c * 2 + k) * nx
            field[out, 2 : 2 + nx, OWN - 2 + k, :] = low_edge("gy", yo, ye, at, at + nx)
            field[out, 2 : 2 + nx, OWN + ny + k, :] = high_edge("gy", yo, ye, at, at + nx)
            at = (c * 2 + k) * ny
            for x, edge in ((k, low_edge), (2 + nx + k, high_edge)):
                field[out, x, 0:OWN, :] = jnp.zeros((OWN, LANES), F32)
                field[out, x, OWN + ny : PLANE, :] = jnp.zeros((PLANE - OWN - ny, LANES), F32)
                field[out, x, OWN : OWN + ny, :] = edge("gx", xo, xe, at, at + ny)


def edge_slots(cell_row, cells):
    n, slots = cells.shape[0], cell_row.shape[1]
    slot = iota((n, slots), 1).astype(F32)
    return jnp.max(jnp.where(cell_row == cells, slot, NO_SLOT), axis=1, keepdims=True).astype(BF16)


def spread(places, z, weight):
    high = weight.astype(BF16)
    low = (weight - high.astype(F32)).astype(BF16)
    zero = jnp.zeros((), BF16)
    at_z = ones_at(one_hot(LANES, z))
    left = []
    for edge, slot in places:
        here = edge == slot.astype(BF16)
        left += [jnp.where(here, high, zero), jnp.where(here, low, zero)]
    both = lax.dot_general(jnp.concatenate(left, axis=0), at_z, NT, preferred_element_type=F32)
    n = both.shape[0] // len(left)
    return [both[2 * k * n : (2 * k + 1) * n] + both[(2 * k + 1) * n : (2 * k + 2) * n] for k in range(len(places))]


def pair_up(v, tc, slot, height, load, counts, loads, matrix, edge_counts, products):
    turbines, slots, levels = counts.shape
    _, nx, ny, _ = v.shape
    cells = nx * ny
    first = lax.axis_index("gy") * slots
    zero = jnp.zeros((), BF16)
    values = v[0, :, :, :].reshape(cells, levels).astype(BF16)
    rows = jnp.dot(pick_slots(tc, cells), values, preferred_element_type=F32)
    row_x = iota((2 * ny, slots), 0)
    edge = jnp.where(row_x < ny, row_x, row_x + (nx - 2) * ny)
    select = jnp.where(edge == tc[0, :, :], 1.0, 0.0).astype(BF16)
    for t in range(turbines):
        a = ones_at(one_hot(slots, slot[0, t : t + 1, :] - first))
        at_z = one_hot(levels, height[0, t : t + 1, :])
        weight = load[0, t : t + 1, :]
        high = weight.astype(BF16)
        low = (weight - high.astype(F32)).astype(BF16)
        b = jnp.concatenate([jnp.where(at_z, high, zero), jnp.where(at_z, low, zero)], axis=0)
        both = lax.dot_general(a, b, NT, preferred_element_type=F32)
        both = both[:, :levels] + both[:, levels:]
        loads[t] = both
        products[t] = (rows * both).astype(BF16)
    for t in range(0, turbines, 2):
        pair = jnp.concatenate([counts[t], counts[t + 1]], axis=1)
        both = jnp.dot(select, pair, preferred_element_type=F32)
        edge_counts[t], edge_counts[t + 1] = both[:, :levels], both[:, levels:]
    block = 16
    wide = turbines * block
    gram = jnp.zeros((wide, wide), F32)
    for b in range(0, slots, block):
        left = counts[:, b : b + block, :].reshape(wide, levels)
        right = products[:, b : b + block, :].reshape(wide, levels)
        gram = gram + lax.dot_general(left, right, NT, preferred_element_type=F32)
    keep = (iota((wide, wide), 0) & (block - 1)) == (iota((wide, wide), 1) & (block - 1))
    gram = jnp.sum(jnp.where(keep, gram, 0.0).reshape(turbines, block, wide), axis=1)
    select = jnp.where(iota((wide, LANES), 0) // block == iota((wide, LANES), 1) % turbines, 1.0, 0.0).astype(BF16)
    both = jnp.dot(jnp.concatenate(in_parts(gram, 2), axis=0).astype(BF16), select, preferred_element_type=F32)
    both = both[:turbines] + both[turbines:]
    rows, per_row, _, _ = packing(turbines)
    row, lane = iota((turbines, LANES), 0), iota((turbines, LANES), 1)
    for r in range(rows):
        here = (row // per_row == r) & (lane // turbines == row % per_row)
        matrix[r : r + 1, :] = jnp.sum(jnp.where(here, both, 0.0), axis=0, keepdims=True)


def beside(v, tc, yo, ye, counts, part, field, sums):
    turbines, _, levels = counts.shape
    _, nx, ny, _ = v.shape
    cells = nx * ny
    field[0, 1 : 1 + nx, OWN : OWN + ny, :] = v[0, :, :, :]
    field[0, 1 : 1 + nx, OWN - 1, :] = low_edge("gy", yo, ye, nx, 2 * nx)
    field[0, 1 : 1 + nx, OWN + ny, :] = high_edge("gy", yo, ye, 0, nx)
    for x in (0, nx + 1):
        field[0, x, OWN : OWN + ny, :] = jnp.zeros((ny, levels), F32)
    update = stencil(field, 0, 1, nx, ny).reshape(cells, levels).astype(BF16)
    later = jnp.dot(pick_slots(tc, cells), update, preferred_element_type=F32)
    for t in range(turbines):
        sums[t : t + 1, :] = jnp.sum(counts[t].astype(F32) * later, axis=0, keepdims=True)
    row = as_row(jnp.sum(sums[...], axis=1, keepdims=True), LANES, 3 * turbines)
    part[...] = jnp.broadcast_to(row, (8, LANES))


def reduce_sums(comps, ny, yo, ye, xo, xe, edge_counts, line, matrix, part, out, sums, box):
    turbines = edge_counts.shape[0]
    ev_x = even("gx")
    left = (SPREAD + CARRY) * low_edge("gx", xo, xe, ny, 2 * ny)
    right = SPREAD * high_edge("gx", xo, xe, 0, ny)
    for t in range(turbines):
        sides = edge_counts[t, 0:ny, :] * left + edge_counts[t, ny : 2 * ny, :] * right
        sums[t : t + 1, :] = jnp.sum(sides, axis=0, keepdims=True)
    rows, _, corner, _ = packing(turbines)
    box[...] = jnp.zeros(box.shape, F32)
    for c in range(comps):
        for i, (edge, at) in enumerate(((low_edge, (c * 2 + 1) * ny), (high_edge, c * 2 * ny))):
            to = corner + 2 * c + i
            box[0, to : to + 1, :] = edge("gx", xo, xe, at, at + 1)
            box[1, to : to + 1, :] = edge("gx", xo, xe, at + ny - 1, at + ny)
    at = xe.shape[0] - 8 + SUMS
    before, after = picked(ev_x, xo, xe, at, at + 1), picked(ev_x, xe, xo, at, at + 1)
    row = part[0:1, :] + line[SUMS : SUMS + 1, :]
    row = row + as_row(jnp.sum(sums[...], axis=1, keepdims=True), LANES, 3 * turbines)
    for k, other in ((1, before), (2, after)):
        row = row + pltpu.roll(jnp.broadcast_to(other, (8, LANES)), k * turbines, 1)[0:1, :]
    for side in range(2):
        for k, piece in enumerate(in_parts(matrix[0:rows, :], 2)):
            box[side, k * rows : (k + 1) * rows, :] = piece
        for k, piece in enumerate(in_parts(row, 3)):
            box[side, 2 * rows + k : 2 * rows + k + 1, :] = piece
    me = lax.axis_index("gy")
    below, above = box[0], box[1]
    for k in range(out.shape[0]):
        out[k] = jnp.where(me + 1 == k, above, below).astype(BF16)


def edges(slots, pieces, v, slot, height, load, yo, ye, xo, xe, line, edge_x, edge_y, update_ref, strip_ref, scales, field):
    comps, nx, ny, levels = v.shape
    turbines = edge_x.shape[1]
    ev, ev_y = even("gx"), even("gy")
    extend(v, yo, ye, xo, xe, field, tuple(range(comps)))
    ends = iota((nx, LANES), 0)
    for c in range(comps):
        update_ref[c] = stencil(field, c, 1, nx + 2, ny)
        for k, (a, b, y) in enumerate(((yo, ye, 0), (ye, yo, ny - 1))):
            near, far = (c * 2 + 1 - k) * nx, (c * 2 + k) * nx
            center = picked(ev_y, a, b, near, near + nx)
            before = jnp.where(ends == 0, 0.0, pltpu.roll(center, 1, 0))
            after = jnp.where(ends == nx - 1, 0.0, pltpu.roll(center, nx - 1, 0))
            others = picked(ev_y, a, b, far, far + nx) + v[c, :, y, :] + lane_edge(center)
            strip_ref[c, k] = moved(center, before, after, others)

    at = xe.shape[0] - 8 + SCALE
    rows_of = (line[SCALE : SCALE + 1, :], picked(ev, xo, xe, at, at + 1), picked(ev, xe, xo, at, at + 1))
    for k, row in enumerate(rows_of):
        scales[k] = jnp.broadcast_to(as_column(row, turbines), (turbines, LANES))
    at = xe.shape[0] - 8 + CELLS
    code_at = comps * 2 * ny
    load_at = code_at + pieces * turbines
    shift = levels.bit_length() - 1
    for k, (a, b) in enumerate(((xo, xe), (xe, xo))):
        cell = picked(ev, a, b, at, at + 1)[:, :slots].astype(jnp.int32) - 1
        edge = edge_slots(cell, iota((ny, slots), 0) + (1 - k) * (nx - 1) * ny)
        codes = [picked(ev, a, b, code_at + i * turbines, code_at + (i + 1) * turbines) for i in range(pieces)]
        codes = jnp.concatenate(codes, axis=1).astype(jnp.int32) - 1
        there = [picked(ev, a, b, load_at + i * turbines, load_at + (i + 1) * turbines) for i in range(pieces)]
        there = jnp.concatenate(there, axis=1)
        for t in range(turbines):
            code = codes[t : t + 1, :]
            (edge_x[k, t],) = spread([(edge, code >> shift)], code & (levels - 1), there[t : t + 1, :])

    me = lax.axis_index("gy")
    at = ye.shape[0] - 8
    lists = []
    for a, b, y in ((yo, ye, ny - 1), (ye, yo, 0)):
        cell = picked(ev_y, a, b, at, at + 1)[:, :slots].astype(jnp.int32) - 1
        lists.append(edge_slots(cell, iota((nx, slots), 0) * ny + y))
    for t in range(turbines):
        row = slot[0, t : t + 1, :]
        places = [(edge, row - (me + k) * slots) for edge, k in zip(lists, (-1, 1))]
        edge_y[0, t], edge_y[1, t] = spread(places, height[0, t : t + 1, :], load[0, t : t + 1, :])


def advance(points, got, v, tc, yo, ye, xo, xe, scales, loads, edge_x, edge_y, update_ref, strip_ref, out, field, parts, result, sems):
    comps, nx, ny, levels = v.shape
    turbines, slots, _ = loads.shape
    cells = nx * ny
    ev_x, ev_y = even("gx"), even("gy")
    rows, per_row, corner, _ = packing(turbines)
    total = got[0].astype(F32)
    for k in range(1, got.shape[0]):
        total = total + got[k].astype(F32)
    matrix = total[0:rows, :] + total[rows : 2 * rows, :]
    sums_row = total[2 * rows : 2 * rows + 1, :] + total[2 * rows + 1 : 2 * rows + 2, :]
    sums_row = sums_row + total[2 * rows + 2 : 2 * rows + 3, :]

    def coefs(scale, sums):
        return -(scale * (FREE_WIND + sums / points))

    own, left, right = (coefs(scales[k], as_column(sums_row, turbines, k * turbines)) for k in range(3))
    row, lane = iota((turbines, LANES), 0), iota((turbines, LANES), 1)
    own_row = jnp.sum(jnp.where(row == lane % turbines, own, 0.0), axis=0, keepdims=True)
    products = matrix * own_row
    forced = jnp.zeros((turbines, LANES), F32)
    for r in range(rows):
        here = (row // per_row == r) & (lane // turbines == row % per_row)
        forced = forced + jnp.where(here, products[r : r + 1, :], 0.0)
    forced = jnp.sum(forced, axis=1, keepdims=True)
    later = coefs(scales[0], as_column(sums_row, turbines, 3 * turbines) + forced)

    for s in range(0, slots, 16):
        first = jnp.zeros((16, levels), F32)
        second = first
        for t in range(turbines):
            part = loads[t, s : s + 16, :]
            first = first + own[t : t + 1, :] * part
            second = second + later[t : t + 1, :] * part
        for i, rest in enumerate((first, second)):
            for k in range(2):
                piece = rest.astype(BF16)
                rest = rest - piece.astype(F32)
                at = (2 * i + k) * levels
                parts[s : s + 16, at : at + levels] = piece
    row = tc[0, :, :]
    put = jnp.where(iota((cells, slots), 0) == row, 1.0, 0.0).astype(BF16)
    spread_out = jnp.dot(put, parts[...], preferred_element_type=F32)
    pieces = [spread_out[:, k * levels : (k + 1) * levels] for k in range(4)]
    first = (pieces[0] + pieces[1]).reshape(nx, ny, levels)
    second = (pieces[2] + pieces[3]).reshape(nx, ny, levels)
    for c in range(comps):
        push = rounded(rounded(v[c, :, :, :]) * first)
        field[c, 1 : 1 + nx, OWN : OWN + ny, :] = update_ref[c, 1 : 1 + nx, :, :] + push

    sums = []
    for edge, coef in ((edge_x.at[0], left), (edge_x.at[1], right), (edge_y.at[0], own), (edge_y.at[1], own)):
        side = coef[0:1, :] * edge[0]
        for t in range(1, turbines):
            side = side + coef[t : t + 1, :] * edge[t]
        sums.append(side)
    ix, iy = lax.axis_index("gx"), lax.axis_index("gy")
    last_y = lax.axis_size("gy") - 1
    there_x = (ix > 0, ix < lax.axis_size("gx") - 1)
    there_y = (iy > 0, iy < last_y)
    beside_y = (jnp.maximum(iy - 1, 0), jnp.minimum(iy + 1, last_y))
    corner_rows = [jnp.where(there_y[k], got[beside_y[k]].astype(F32), 0.0) for k in range(2)]
    row_x, row_y = iota((nx, LANES), 0), iota((ny, LANES), 0)
    for c in range(comps):
        at_corner = [[corner_rows[y][corner + c * 2 + x : corner + c * 2 + x + 1, :] for y in range(2)] for x in range(2)]
        for k, (a, b) in enumerate(((xo, xe), (xe, xo))):
            at = (c * 2 + 1 - k) * ny
            x = k * (nx + 1)
            push = rounded(rounded(picked(ev_x, a, b, at, at + ny)) * sums[k])
            extra = jnp.where(row_y == 0, at_corner[k][0], 0.0) + jnp.where(row_y == ny - 1, at_corner[k][1], 0.0)
            value = update_ref[c, x, :, :] + SPREAD * extra + push
            field[c, x, OWN : OWN + ny, :] = jnp.where(there_x[k], value, 0.0)
        for k, (a, b) in enumerate(((yo, ye), (ye, yo))):
            at = (c * 2 + 1 - k) * nx
            y = OWN - 1 + k * (ny + 1)
            push = rounded(rounded(picked(ev_y, a, b, at, at + nx)) * sums[2 + k])
            extra = jnp.where(row_x == 0, (SPREAD + CARRY) * at_corner[0][k], 0.0)
            extra = extra + jnp.where(row_x == nx - 1, SPREAD * at_corner[1][k], 0.0)
            value = strip_ref[c, k] + extra + push
            field[c, 1 : 1 + nx, y, :] = jnp.where(there_y[k], value, 0.0)
    copies = []
    for c in range(comps):
        now = field[c, 1 : 1 + nx, OWN : OWN + ny, :]
        result[c] = stencil(field, c, 1, nx, ny) + rounded(rounded(now) * second)
        copies.append(pltpu.make_async_copy(result.at[c], out.at[c], sems.at[c]))
        copies[c].start()
    for copy in copies:
        copy.wait()


def body(velocity, tile_cells, owner, point_slot, point_z, loading):
    comps, nx, ny, levels = velocity.shape
    _, turbines, points = point_slot.shape
    slots = tile_cells.shape[2]
    tiles_y = lax.axis_size("gy")
    pieces = points // LANES
    chunk_rows = packing(turbines)[3]
    rows_y = comps * 2 * nx + 8
    rows_x = comps * 2 * ny + 2 * pieces * turbines + 8
    args = (velocity, tile_cells, owner, point_slot, point_z, loading)
    work = {"flops": 26 * turbines * slots * points * levels, "nbytes": 1 << 20}

    def field(n, planes):
        return pltpu.VMEM((n, planes, PLANE, levels), F32)

    v, tc, slot, height, load, counts, line, y_even, y_odd, x_even, x_odd = call(
        prepare,
        "prepare",
        [(x.shape, x.dtype) for x in (velocity, tile_cells, point_slot, point_z, loading)]
        + [((turbines, slots, levels), BF16), ((8, LANES), F32)]
        + [((rows_y, levels), F32)] * 2
        + [((rows_x, levels), F32)] * 2,
        args,
        [
            pltpu.VMEM(owner.shape, jnp.int32),
            pltpu.VMEM((turbines, slots, levels), F32),
            pltpu.VMEM((turbines, levels), F32),
            pltpu.SemaphoreType.DMA((len(args),)),
        ],
        space=pltpu.HBM,
        **work,
    )
    yo, ye = swap(y_odd, "gy", 1), swap(y_even, "gy", 0)
    xo, xe = swap(x_odd, "gx", 1), swap(x_even, "gx", 0)
    loads, matrix, edge_counts = call(
        pair_up,
        "pair_up",
        [((turbines, slots, levels), F32), ((8, LANES), F32), ((turbines, 2 * ny, levels), F32)],
        (v, tc, slot, height, load, counts),
        [pltpu.VMEM((turbines, slots, levels), BF16)],
        **work,
    )
    (part,) = call(
        beside,
        "beside",
        [((8, LANES), F32)],
        (v, tc, yo, ye, counts),
        [field(1, nx + 2), pltpu.VMEM((turbines, levels), F32)],
        flops=work["flops"] // 4,
        nbytes=work["nbytes"],
    )

    def reduce_of(*refs):
        return reduce_sums(comps, ny, *refs)

    (chunk,) = call(
        reduce_of,
        "reduce_sums",
        [((tiles_y, chunk_rows, LANES), BF16)],
        (yo, ye, xo, xe, edge_counts, line, matrix, part),
        [pltpu.VMEM((turbines, levels), F32), pltpu.VMEM((2, chunk_rows, LANES), F32)],
    )
    got = lax.all_to_all(chunk, "gy", 0, 0)

    def edges_of(*refs):
        return edges(slots, pieces, *refs)

    edge_x, edge_y, update, strip, scales = call(
        edges_of,
        "edges",
        [
            ((2, turbines, ny, levels), F32),
            ((2, turbines, nx, levels), F32),
            ((comps, nx + 2, ny, levels), F32),
            ((comps, 2, nx, levels), F32),
            ((3, turbines, LANES), F32),
        ],
        (v, slot, height, load, yo, ye, xo, xe, line),
        [field(comps, nx + 4)],
        **work,
    )

    def advance_by(*refs):
        return advance(points, *refs)

    (out,) = call(
        advance_by,
        "advance",
        [(velocity.shape, F32)],
        (got, v, tc, yo, ye, xo, xe, scales, loads, edge_x, edge_y, update, strip),
        [
            field(comps, nx + 2),
            pltpu.VMEM((slots, 4 * levels), BF16),
            pltpu.VMEM(velocity.shape, F32),
            pltpu.SemaphoreType.DMA((comps,)),
        ],
        out_space=pltpu.HBM,
    )
    return out


def solution(mesh):
    in_specs = (
        P(None, "gx", "gy", None),
        P("gx", "gy", None),
        P("gx", None),
        P("gx", None, None),
        P("gx", None, None),
        P("gx", None, None),
    )
    out_specs = P(None, "gx", "gy", None)
    return jax.shard_map(body, mesh=mesh, in_specs=in_specs, out_specs=out_specs, check_vma=False)
```

```python
import jax
import jax.numpy as jnp
from jax import lax
from jax.experimental import pallas as pl
from jax.experimental.pallas import tpu as pltpu
from jax.sharding import PartitionSpec as P

SPREAD = 0.12
CARRY = 0.25
FREE_WIND = 1.0
LOAD = 0.6

F32 = jnp.float32
BF16 = jnp.bfloat16
NT = (((1,), (1,)), ((), ()))
LANES = 128
OWN = 8
PLANE = 32
NO_SLOT = -30000.0
SUMS, SCALE, CELLS = 0, 1, 2


def iota(shape, axis):
    return lax.broadcasted_iota(jnp.int32, shape, axis)


def rounded(x):
    return x.astype(BF16).astype(F32)


def one_hot(count, row):
    places = iota((count, row.shape[1]), 0).astype(BF16)
    return places == row.astype(BF16)


def ones_at(mask):
    return jnp.where(mask, jnp.ones((), BF16), jnp.zeros((), BF16))


def pick_slots(tc, cells):
    slots = tc.shape[2]
    row = jnp.broadcast_to(tc[0, :, :].astype(F32), (slots, slots))
    same = iota((slots, slots), 0) == iota((slots, slots), 1)
    column = jnp.sum(jnp.where(same, row, 0.0), axis=1, keepdims=True).astype(jnp.int32)
    return jnp.where(iota((slots, cells), 1) == column, 1.0, 0.0).astype(BF16)


def even(axis):
    return lax.rem(lax.axis_index(axis), 2) == 0


def swap(x, axis, first):
    counts = {name: lax.axis_size(name) for name in ("gx", "gy")}
    other = "gy" if axis == "gx" else "gx"

    def device(along, across):
        at = {axis: along, other: across}
        return at["gx"] * counts["gy"] + at["gy"]

    last = counts[axis] - 1
    pairs = [(device(i, k), device(i + 1, k)) for i in range(first, last, 2) for k in range(counts[other])]
    if first:
        pairs += [(device(i, k), device(i, k + 1)) for i in (0, last) for k in range(0, counts[other], 2)]
    return lax.ppermute(x, ("gx", "gy"), pairs + [(b, a) for a, b in pairs])


def call(kernel, name, outs, args, scratch=(), flops=0, nbytes=0, space=pltpu.VMEM, out_space=pltpu.VMEM):
    return pl.pallas_call(
        kernel,
        out_shape=[jax.ShapeDtypeStruct(s, d) for s, d in outs],
        in_specs=[pl.BlockSpec(memory_space=space)] * len(args),
        out_specs=[pl.BlockSpec(memory_space=out_space)] * len(outs),
        scratch_shapes=list(scratch),
        compiler_params=pltpu.CompilerParams(vmem_limit_bytes=16 << 20),
        cost_estimate=pl.CostEstimate(flops=flops, bytes_accessed=nbytes, transcendentals=0),
        name=name,
    )(*(pltpu.with_memory_space_constraint(a, space) if space is pltpu.HBM else a for a in args))


def lane_edge(center):
    axis = center.ndim - 1
    lane = iota(center.shape, axis)
    last = center.shape[axis] - 1
    below = jnp.where(lane == 0, 0.0, pltpu.roll(center, 1, axis))
    above = jnp.where(lane == last, 0.0, pltpu.roll(center, last, axis))
    return below + above


def moved(center, before, after, beside):
    own = (1.0 - 6.0 * SPREAD - CARRY) * center
    return own + SPREAD * (beside + after) + (SPREAD + CARRY) * before


def stencil(ref, c, x0, nx, ny):
    center = ref[c, x0 : x0 + nx, OWN : OWN + ny, :]
    before = ref[c, x0 - 1 : x0 - 1 + nx, OWN : OWN + ny, :]
    after = ref[c, x0 + 1 : x0 + 1 + nx, OWN : OWN + ny, :]
    beside = ref[c, x0 : x0 + nx, OWN - 1 : OWN - 1 + ny, :] + ref[c, x0 : x0 + nx, OWN + 1 : OWN + 1 + ny, :]
    return moved(center, before, after, beside + lane_edge(center))


def as_column(row, n, start=0):
    shape = (n, row.shape[1])
    return jnp.sum(jnp.where(iota(shape, 0) + start == iota(shape, 1), row, 0.0), axis=1, keepdims=True)


def as_row(column, lanes, start=0):
    shape = (column.shape[0], lanes)
    return jnp.sum(jnp.where(iota(shape, 0) + start == iota(shape, 1), column, 0.0), axis=0, keepdims=True)


def packing(turbines):
    per_row = LANES // turbines
    rows = turbines // per_row
    return rows, per_row, 2 * rows + 3, -(-(2 * rows + 9) // 16) * 16


def in_parts(x, count):
    parts = []
    for _ in range(count):
        parts.append(rounded(x))
        x = x - parts[-1]
    return parts


def picked(flag, a, b, lo, hi):
    return jnp.where(flag, a[lo:hi, :], b[lo:hi, :])


def low_edge(axis, odd, even_, lo, hi):
    return jnp.where(lax.axis_index(axis) > 0, picked(even(axis), odd, even_, lo, hi), 0.0)


def high_edge(axis, odd, even_, lo, hi):
    there = lax.axis_index(axis) < lax.axis_size(axis) - 1
    return jnp.where(there, picked(even(axis), even_, odd, lo, hi), 0.0)


def prepare(
    v_hbm, tc_hbm, owner_hbm, slot_hbm, height_hbm, load_hbm,
    v, tc, slot, height, load, count_ref, line, y_even, y_odd, x_even, x_odd,
    owner, exact, sum_ref, sems,
):
    pairs = ((slot_hbm, slot), (height_hbm, height), (tc_hbm, tc), (load_hbm, load), (owner_hbm, owner), (v_hbm, v))
    copies = [pltpu.make_async_copy(a, b, sems.at[i]) for i, (a, b) in enumerate(pairs)]
    for copy in copies:
        copy.start()
    _, turbines, points = slot.shape
    slots, levels = count_ref.shape[1:]
    comps, nx, ny, _ = v.shape
    cells = nx * ny
    first = lax.axis_index("gy") * slots
    copies[0].wait()
    copies[1].wait()
    for t in range(turbines):
        a = ones_at(one_hot(slots, slot[0, t : t + 1, :] - first))
        b = ones_at(one_hot(levels, height[0, t : t + 1, :]))
        exact[t] = lax.dot_general(a, b, NT, preferred_element_type=F32)
    for copy in copies[2:]:
        copy.wait()

    ev = even("gy")
    at = 0
    for c in range(comps):
        for k in range(2):
            high = v[c, :, ny - 2 + k, :]
            low = v[c, :, k, :]
            y_even[at : at + nx, :] = jnp.where(ev, high, low)
            y_odd[at : at + nx, :] = jnp.where(ev, low, high)
            at += nx
    values = v[0, :, :, :].reshape(cells, levels).astype(BF16)
    rows = jnp.dot(pick_slots(tc, cells), values, preferred_element_type=F32)
    for t in range(turbines):
        count = exact[t]
        count_ref[t] = count.astype(BF16)
        sum_ref[t : t + 1, :] = jnp.sum(count * rows, axis=0, keepdims=True)

    owner_row = jnp.broadcast_to(owner[...].astype(F32), (turbines, turbines))
    member = owner_row == as_column(owner_row, turbines)
    load_row = as_row(jnp.sum(load[0, :, :], axis=1, keepdims=True), turbines)
    total = jnp.sum(jnp.where(member, load_row, 0.0), axis=1, keepdims=True)
    number = jnp.sum(jnp.where(member, 1.0, 0.0), axis=1, keepdims=True)
    line[...] = jnp.zeros((8, LANES), F32)
    line[SUMS : SUMS + 1, :] = as_row(jnp.sum(sum_ref[...], axis=1, keepdims=True), LANES)
    line[SCALE : SCALE + 1, :] = as_row(LOAD / (total / (number * points)), LANES)
    line[CELLS : CELLS + 1, 0:slots] = tc[0, :, :].astype(F32) + 1.0
    for out in (y_even, y_odd):
        out[at : at + 8, :] = jnp.zeros((8, LANES), F32)
        out[at : at + 1, :] = line[CELLS : CELLS + 1, :]

    local = slot[0, :, :] - first
    inside = (local >= 0) & (local < slots)
    code = jnp.where(inside, local * levels + height[0, :, :] + 1, 0).astype(F32)
    ev = even("gx")
    at = 0
    for c in range(comps):
        for k in range(2):
            right, left = v[c, nx - 2 + k, :, :], v[c, k, :, :]
            x_even[at : at + ny, :] = jnp.where(ev, right, left)
            x_odd[at : at + ny, :] = jnp.where(ev, left, right)
            at += ny
    for part in (code, load[0, :, :]):
        for k in range(0, points, LANES):
            for out in (x_even, x_odd):
                out[at : at + turbines, :] = part[:, k : k + LANES]
            at += turbines
    for out in (x_even, x_odd):
        out[at : at + 8, :] = line[...]


def extend(v, yo, ye, xo, xe, field, comps):
    _, nx, ny, _ = v.shape
    for c in comps:
        out = c if len(comps) > 1 else 0
        field[out, 2 : 2 + nx, OWN : OWN + ny, :] = v[c, :, :, :]
        for k in range(2):
            at = (c * 2 + k) * nx
            field[out, 2 : 2 + nx, OWN - 2 + k, :] = low_edge("gy", yo, ye, at, at + nx)
            field[out, 2 : 2 + nx, OWN + ny + k, :] = high_edge("gy", yo, ye, at, at + nx)
            at = (c * 2 + k) * ny
            for x, edge in ((k, low_edge), (2 + nx + k, high_edge)):
                field[out, x, 0:OWN, :] = jnp.zeros((OWN, LANES), F32)
                field[out, x, OWN + ny : PLANE, :] = jnp.zeros((PLANE - OWN - ny, LANES), F32)
                field[out, x, OWN : OWN + ny, :] = edge("gx", xo, xe, at, at + ny)


def edge_slots(cell_row, cells):
    n, slots = cells.shape[0], cell_row.shape[1]
    slot = iota((n, slots), 1).astype(F32)
    return jnp.max(jnp.where(cell_row == cells, slot, NO_SLOT), axis=1, keepdims=True).astype(BF16)


def spread(places, z, weight):
    high = weight.astype(BF16)
    low = (weight - high.astype(F32)).astype(BF16)
    zero = jnp.zeros((), BF16)
    at_z = ones_at(one_hot(LANES, z))
    left = []
    for edge, slot in places:
        here = edge == slot.astype(BF16)
        left += [jnp.where(here, high, zero), jnp.where(here, low, zero)]
    both = lax.dot_general(jnp.concatenate(left, axis=0), at_z, NT, preferred_element_type=F32)
    n = both.shape[0] // len(left)
    return [both[2 * k * n : (2 * k + 1) * n] + both[(2 * k + 1) * n : (2 * k + 2) * n] for k in range(len(places))]


def pair_up(v, tc, slot, height, load, counts, loads, matrix, edge_counts, single, products):
    turbines, slots, levels = counts.shape
    _, nx, ny, _ = v.shape
    cells = nx * ny
    first = lax.axis_index("gy") * slots
    zero = jnp.zeros((), BF16)
    values = v[0, :, :, :].reshape(cells, levels).astype(BF16)
    rows = jnp.dot(pick_slots(tc, cells), values, preferred_element_type=F32)
    row_x = iota((2 * ny, slots), 0)
    edge = jnp.where(row_x < ny, row_x, row_x + (nx - 2) * ny)
    select = jnp.where(edge == tc[0, :, :], 1.0, 0.0).astype(BF16)
    for t in range(turbines):
        a = ones_at(one_hot(slots, slot[0, t : t + 1, :] - first))
        at_z = one_hot(levels, height[0, t : t + 1, :])
        weight = load[0, t : t + 1, :]
        high = weight.astype(BF16)
        low = (weight - high.astype(F32)).astype(BF16)
        b = jnp.concatenate([jnp.where(at_z, high, zero), jnp.where(at_z, low, zero)], axis=0)
        both = lax.dot_general(a, b, NT, preferred_element_type=F32)
        both = both[:, :levels] + both[:, levels:]
        loads[t] = both
        for k, piece in enumerate(in_parts(rows * both, 2)):
            products[k, t] = piece.astype(BF16)
    for t in range(0, turbines, 2):
        pair = jnp.concatenate([counts[t], counts[t + 1]], axis=1)
        both = jnp.dot(select, pair, preferred_element_type=F32)
        edge_counts[t], edge_counts[t + 1] = both[:, :levels], both[:, levels:]
    hits = counts[0].astype(F32)
    for t in range(1, turbines):
        hits = hits + counts[t].astype(F32)
    single[...] = jnp.where(hits == 1.0, 1.0, 0.0).astype(BF16)
    block = 16
    wide = turbines * block
    gram = jnp.zeros((wide, wide), F32)
    for b in range(0, slots, block):
        left = counts[:, b : b + block, :].reshape(wide, levels)
        for k in range(2):
            right = products[k, :, b : b + block, :].reshape(wide, levels)
            gram = gram + lax.dot_general(left, right, NT, preferred_element_type=F32)
    keep = (iota((wide, wide), 0) & (block - 1)) == (iota((wide, wide), 1) & (block - 1))
    gram = jnp.sum(jnp.where(keep, gram, 0.0).reshape(turbines, block, wide), axis=1)
    select = jnp.where(iota((wide, LANES), 0) // block == iota((wide, LANES), 1) % turbines, 1.0, 0.0).astype(BF16)
    both = jnp.dot(jnp.concatenate(in_parts(gram, 2), axis=0).astype(BF16), select, preferred_element_type=F32)
    both = both[:turbines] + both[turbines:]
    rows, per_row, _, _ = packing(turbines)
    row, lane = iota((turbines, LANES), 0), iota((turbines, LANES), 1)
    for r in range(rows):
        here = (row // per_row == r) & (lane // turbines == row % per_row)
        matrix[r : r + 1, :] = jnp.sum(jnp.where(here, both, 0.0), axis=0, keepdims=True)


def beside(v, tc, yo, ye, counts, part, field, sums):
    turbines, _, levels = counts.shape
    _, nx, ny, _ = v.shape
    cells = nx * ny
    field[0, 1 : 1 + nx, OWN : OWN + ny, :] = v[0, :, :, :]
    field[0, 1 : 1 + nx, OWN - 1, :] = low_edge("gy", yo, ye, nx, 2 * nx)
    field[0, 1 : 1 + nx, OWN + ny, :] = high_edge("gy", yo, ye, 0, nx)
    for x in (0, nx + 1):
        field[0, x, OWN : OWN + ny, :] = jnp.zeros((ny, levels), F32)
    update = stencil(field, 0, 1, nx, ny).reshape(cells, levels)
    update = jnp.concatenate(in_parts(update, 2), axis=1).astype(BF16)
    later = jnp.dot(pick_slots(tc, cells), update, preferred_element_type=F32)
    later = later[:, :levels] + later[:, levels:]
    for t in range(turbines):
        sums[t : t + 1, :] = jnp.sum(counts[t].astype(F32) * later, axis=0, keepdims=True)
    row = as_row(jnp.sum(sums[...], axis=1, keepdims=True), LANES, 3 * turbines)
    part[...] = jnp.broadcast_to(row, (8, LANES))


def reduce_sums(comps, ny, yo, ye, xo, xe, edge_counts, line, matrix, part, out, sums, box):
    turbines = edge_counts.shape[0]
    ev_x = even("gx")
    left = (SPREAD + CARRY) * low_edge("gx", xo, xe, ny, 2 * ny)
    right = SPREAD * high_edge("gx", xo, xe, 0, ny)
    for t in range(turbines):
        sides = edge_counts[t, 0:ny, :] * left + edge_counts[t, ny : 2 * ny, :] * right
        sums[t : t + 1, :] = jnp.sum(sides, axis=0, keepdims=True)
    rows, _, corner, _ = packing(turbines)
    box[...] = jnp.zeros(box.shape, F32)
    for c in range(comps):
        for i, (edge, at) in enumerate(((low_edge, (c * 2 + 1) * ny), (high_edge, c * 2 * ny))):
            to = corner + 2 * c + i
            box[0, to : to + 1, :] = edge("gx", xo, xe, at, at + 1)
            box[1, to : to + 1, :] = edge("gx", xo, xe, at + ny - 1, at + ny)
    at = xe.shape[0] - 8 + SUMS
    before, after = picked(ev_x, xo, xe, at, at + 1), picked(ev_x, xe, xo, at, at + 1)
    row = part[0:1, :] + line[SUMS : SUMS + 1, :]
    row = row + as_row(jnp.sum(sums[...], axis=1, keepdims=True), LANES, 3 * turbines)
    for k, other in ((1, before), (2, after)):
        row = row + pltpu.roll(jnp.broadcast_to(other, (8, LANES)), k * turbines, 1)[0:1, :]
    for side in range(2):
        for k, piece in enumerate(in_parts(matrix[0:rows, :], 2)):
            box[side, k * rows : (k + 1) * rows, :] = piece
        for k, piece in enumerate(in_parts(row, 3)):
            box[side, 2 * rows + k : 2 * rows + k + 1, :] = piece
    me = lax.axis_index("gy")
    below, above = box[0], box[1]
    for k in range(out.shape[0]):
        out[k] = jnp.where(me + 1 == k, above, below).astype(BF16)


def edges(slots, pieces, v, slot, height, load, yo, ye, xo, xe, line, edge_x, edge_y, update_ref, strip_ref, scales, field):
    comps, nx, ny, levels = v.shape
    turbines = edge_x.shape[1]
    ev, ev_y = even("gx"), even("gy")
    extend(v, yo, ye, xo, xe, field, tuple(range(comps)))
    ends = iota((nx, LANES), 0)
    for c in range(comps):
        update_ref[c] = stencil(field, c, 1, nx + 2, ny)
        for k, (a, b, y) in enumerate(((yo, ye, 0), (ye, yo, ny - 1))):
            near, far = (c * 2 + 1 - k) * nx, (c * 2 + k) * nx
            center = picked(ev_y, a, b, near, near + nx)
            before = jnp.where(ends == 0, 0.0, pltpu.roll(center, 1, 0))
            after = jnp.where(ends == nx - 1, 0.0, pltpu.roll(center, nx - 1, 0))
            others = picked(ev_y, a, b, far, far + nx) + v[c, :, y, :] + lane_edge(center)
            strip_ref[c, k] = moved(center, before, after, others)

    at = xe.shape[0] - 8 + SCALE
    rows_of = (line[SCALE : SCALE + 1, :], picked(ev, xo, xe, at, at + 1), picked(ev, xe, xo, at, at + 1))
    for k, row in enumerate(rows_of):
        scales[k] = jnp.broadcast_to(as_column(row, turbines), (turbines, LANES))
    at = xe.shape[0] - 8 + CELLS
    code_at = comps * 2 * ny
    load_at = code_at + pieces * turbines
    shift = levels.bit_length() - 1
    for k, (a, b) in enumerate(((xo, xe), (xe, xo))):
        cell = picked(ev, a, b, at, at + 1)[:, :slots].astype(jnp.int32) - 1
        edge = edge_slots(cell, iota((ny, slots), 0) + (1 - k) * (nx - 1) * ny)
        codes = [picked(ev, a, b, code_at + i * turbines, code_at + (i + 1) * turbines) for i in range(pieces)]
        codes = jnp.concatenate(codes, axis=1).astype(jnp.int32) - 1
        there = [picked(ev, a, b, load_at + i * turbines, load_at + (i + 1) * turbines) for i in range(pieces)]
        there = jnp.concatenate(there, axis=1)
        for t in range(turbines):
            code = codes[t : t + 1, :]
            (edge_x[k, t],) = spread([(edge, code >> shift)], code & (levels - 1), there[t : t + 1, :])

    me = lax.axis_index("gy")
    at = ye.shape[0] - 8
    lists = []
    for a, b, y in ((yo, ye, ny - 1), (ye, yo, 0)):
        cell = picked(ev_y, a, b, at, at + 1)[:, :slots].astype(jnp.int32) - 1
        lists.append(edge_slots(cell, iota((nx, slots), 0) * ny + y))
    for t in range(turbines):
        row = slot[0, t : t + 1, :]
        places = [(edge, row - (me + k) * slots) for edge, k in zip(lists, (-1, 1))]
        edge_y[0, t], edge_y[1, t] = spread(places, height[0, t : t + 1, :], load[0, t : t + 1, :])


def advance(points, got, v, tc, yo, ye, xo, xe, scales, loads, single, edge_x, edge_y, update_ref, strip_ref, out, field, parts, result, sems):
    comps, nx, ny, levels = v.shape
    turbines, slots, _ = loads.shape
    cells = nx * ny
    ev_x, ev_y = even("gx"), even("gy")
    rows, per_row, corner, _ = packing(turbines)
    total = got[0].astype(F32)
    for k in range(1, got.shape[0]):
        total = total + got[k].astype(F32)
    matrix = total[0:rows, :] + total[rows : 2 * rows, :]
    sums_row = total[2 * rows : 2 * rows + 1, :] + total[2 * rows + 1 : 2 * rows + 2, :]
    sums_row = sums_row + total[2 * rows + 2 : 2 * rows + 3, :]

    def coefs(scale, sums):
        return -(scale * (FREE_WIND + sums / points))

    own, left, right = (coefs(scales[k], as_column(sums_row, turbines, k * turbines)) for k in range(3))
    row, lane = iota((turbines, LANES), 0), iota((turbines, LANES), 1)
    own_row = jnp.sum(jnp.where(row == lane % turbines, own, 0.0), axis=0, keepdims=True)
    products = matrix * own_row
    forced = jnp.zeros((turbines, LANES), F32)
    for r in range(rows):
        here = (row // per_row == r) & (lane // turbines == row % per_row)
        forced = forced + jnp.where(here, products[r : r + 1, :], 0.0)
    forced = jnp.sum(forced, axis=1, keepdims=True)
    later = coefs(scales[0], as_column(sums_row, turbines, 3 * turbines) + forced)

    for s in range(0, slots, 16):
        first = jnp.zeros((16, levels), F32)
        second = first
        for t in range(turbines):
            part = loads[t, s : s + 16, :]
            first = first + own[t : t + 1, :] * part
            second = second + later[t : t + 1, :] * part
        for i, rest in enumerate((first, second)):
            for k in range(2):
                piece = rest.astype(BF16)
                rest = rest - piece.astype(F32)
                at = (2 * i + k) * levels
                parts[s : s + 16, at : at + levels] = piece
    parts[:, 4 * levels :] = single[...]
    row = tc[0, :, :]
    put = jnp.where(iota((cells, slots), 0) == row, 1.0, 0.0).astype(BF16)
    spread_out = jnp.dot(put, parts[...], preferred_element_type=F32)
    pieces = [spread_out[:, k * levels : (k + 1) * levels] for k in range(5)]
    first = (pieces[0] + pieces[1]).reshape(nx, ny, levels)
    second = (pieces[2] + pieces[3]).reshape(nx, ny, levels)
    alone = pieces[4].reshape(nx, ny, levels) > 0.5

    def force(values, weight):
        push = rounded(values) * weight
        return jnp.where(alone, rounded(push), push)

    for c in range(comps):
        field[c, 1 : 1 + nx, OWN : OWN + ny, :] = update_ref[c, 1 : 1 + nx, :, :] + force(v[c, :, :, :], first)

    sums = []
    for edge, coef in ((edge_x.at[0], left), (edge_x.at[1], right), (edge_y.at[0], own), (edge_y.at[1], own)):
        side = coef[0:1, :] * edge[0]
        for t in range(1, turbines):
            side = side + coef[t : t + 1, :] * edge[t]
        sums.append(side)
    ix, iy = lax.axis_index("gx"), lax.axis_index("gy")
    last_y = lax.axis_size("gy") - 1
    there_x = (ix > 0, ix < lax.axis_size("gx") - 1)
    there_y = (iy > 0, iy < last_y)
    beside_y = (jnp.maximum(iy - 1, 0), jnp.minimum(iy + 1, last_y))
    corner_rows = [jnp.where(there_y[k], got[beside_y[k]].astype(F32), 0.0) for k in range(2)]
    row_x, row_y = iota((nx, LANES), 0), iota((ny, LANES), 0)
    for c in range(comps):
        at_corner = [[corner_rows[y][corner + c * 2 + x : corner + c * 2 + x + 1, :] for y in range(2)] for x in range(2)]
        for k, (a, b) in enumerate(((xo, xe), (xe, xo))):
            at = (c * 2 + 1 - k) * ny
            x = k * (nx + 1)
            push = rounded(rounded(picked(ev_x, a, b, at, at + ny)) * sums[k])
            extra = jnp.where(row_y == 0, at_corner[k][0], 0.0) + jnp.where(row_y == ny - 1, at_corner[k][1], 0.0)
            value = update_ref[c, x, :, :] + SPREAD * extra + push
            field[c, x, OWN : OWN + ny, :] = jnp.where(there_x[k], value, 0.0)
        for k, (a, b) in enumerate(((yo, ye), (ye, yo))):
            at = (c * 2 + 1 - k) * nx
            y = OWN - 1 + k * (ny + 1)
            push = rounded(rounded(picked(ev_y, a, b, at, at + nx)) * sums[2 + k])
            extra = jnp.where(row_x == 0, (SPREAD + CARRY) * at_corner[0][k], 0.0)
            extra = extra + jnp.where(row_x == nx - 1, SPREAD * at_corner[1][k], 0.0)
            value = strip_ref[c, k] + extra + push
            field[c, 1 : 1 + nx, y, :] = jnp.where(there_y[k], value, 0.0)
    copies = []
    for c in range(comps):
        now = field[c, 1 : 1 + nx, OWN : OWN + ny, :]
        result[c] = stencil(field, c, 1, nx, ny) + force(now, second)
        copies.append(pltpu.make_async_copy(result.at[c], out.at[c], sems.at[c]))
        copies[c].start()
    for copy in copies:
        copy.wait()


def body(velocity, tile_cells, owner, point_slot, point_z, loading):
    comps, nx, ny, levels = velocity.shape
    _, turbines, points = point_slot.shape
    slots = tile_cells.shape[2]
    tiles_y = lax.axis_size("gy")
    pieces = points // LANES
    chunk_rows = packing(turbines)[3]
    rows_y = comps * 2 * nx + 8
    rows_x = comps * 2 * ny + 2 * pieces * turbines + 8
    args = (velocity, tile_cells, owner, point_slot, point_z, loading)
    work = {"flops": 26 * turbines * slots * points * levels, "nbytes": 1 << 20}

    def field(n, planes):
        return pltpu.VMEM((n, planes, PLANE, levels), F32)

    v, tc, slot, height, load, counts, line, y_even, y_odd, x_even, x_odd = call(
        prepare,
        "prepare",
        [(x.shape, x.dtype) for x in (velocity, tile_cells, point_slot, point_z, loading)]
        + [((turbines, slots, levels), BF16), ((8, LANES), F32)]
        + [((rows_y, levels), F32)] * 2
        + [((rows_x, levels), F32)] * 2,
        args,
        [
            pltpu.VMEM(owner.shape, jnp.int32),
            pltpu.VMEM((turbines, slots, levels), F32),
            pltpu.VMEM((turbines, levels), F32),
            pltpu.SemaphoreType.DMA((len(args),)),
        ],
        space=pltpu.HBM,
        **work,
    )
    yo, ye = swap(y_odd, "gy", 1), swap(y_even, "gy", 0)
    xo, xe = swap(x_odd, "gx", 1), swap(x_even, "gx", 0)
    loads, matrix, edge_counts, single = call(
        pair_up,
        "pair_up",
        [
            ((turbines, slots, levels), F32),
            ((8, LANES), F32),
            ((turbines, 2 * ny, levels), F32),
            ((slots, levels), BF16),
        ],
        (v, tc, slot, height, load, counts),
        [pltpu.VMEM((2, turbines, slots, levels), BF16)],
        **work,
    )
    (part,) = call(
        beside,
        "beside",
        [((8, LANES), F32)],
        (v, tc, yo, ye, counts),
        [field(1, nx + 2), pltpu.VMEM((turbines, levels), F32)],
        flops=work["flops"] // 4,
        nbytes=work["nbytes"],
    )

    def reduce_of(*refs):
        return reduce_sums(comps, ny, *refs)

    (chunk,) = call(
        reduce_of,
        "reduce_sums",
        [((tiles_y, chunk_rows, LANES), BF16)],
        (yo, ye, xo, xe, edge_counts, line, matrix, part),
        [pltpu.VMEM((turbines, levels), F32), pltpu.VMEM((2, chunk_rows, LANES), F32)],
    )
    got = lax.all_to_all(chunk, "gy", 0, 0)

    def edges_of(*refs):
        return edges(slots, pieces, *refs)

    edge_x, edge_y, update, strip, scales = call(
        edges_of,
        "edges",
        [
            ((2, turbines, ny, levels), F32),
            ((2, turbines, nx, levels), F32),
            ((comps, nx + 2, ny, levels), F32),
            ((comps, 2, nx, levels), F32),
            ((3, turbines, LANES), F32),
        ],
        (v, slot, height, load, yo, ye, xo, xe, line),
        [field(comps, nx + 4)],
        **work,
    )

    def advance_by(*refs):
        return advance(points, *refs)

    (out,) = call(
        advance_by,
        "advance",
        [(velocity.shape, F32)],
        (got, v, tc, yo, ye, xo, xe, scales, loads, single, edge_x, edge_y, update, strip),
        [
            field(comps, nx + 2),
            pltpu.VMEM((slots, 5 * levels), BF16),
            pltpu.VMEM(velocity.shape, F32),
            pltpu.SemaphoreType.DMA((comps,)),
        ],
        out_space=pltpu.HBM,
    )
    return out


def solution(mesh):
    in_specs = (
        P(None, "gx", "gy", None),
        P("gx", "gy", None),
        P("gx", None),
        P("gx", None, None),
        P("gx", None, None),
        P("gx", None, None),
    )
    out_specs = P(None, "gx", "gy", None)
    return jax.shard_map(body, mesh=mesh, in_specs=in_specs, out_specs=out_specs, check_vma=False)
```

```python
import jax
import jax.numpy as jnp
from jax import lax
from jax.experimental import pallas as pl
from jax.experimental.pallas import tpu as pltpu
from jax.sharding import PartitionSpec as P

SPREAD = 0.12
CARRY = 0.25
FREE_WIND = 1.0
LOAD = 0.6

F32 = jnp.float32
BF16 = jnp.bfloat16
NT = (((1,), (1,)), ((), ()))
LANES = 128
OWN = 8
PLANE = 32
NO_SLOT = -30000.0
SUMS, SCALE, CELLS = 0, 1, 2


def iota(shape, axis):
    return lax.broadcasted_iota(jnp.int32, shape, axis)


def rounded(x):
    return x.astype(BF16).astype(F32)


def one_hot(count, row):
    places = iota((count, row.shape[1]), 0).astype(BF16)
    return places == row.astype(BF16)


def ones_at(mask):
    return jnp.where(mask, jnp.ones((), BF16), jnp.zeros((), BF16))


def pick_slots(tc, cells):
    slots = tc.shape[2]
    row = jnp.broadcast_to(tc[0, :, :].astype(F32), (slots, slots))
    same = iota((slots, slots), 0) == iota((slots, slots), 1)
    column = jnp.sum(jnp.where(same, row, 0.0), axis=1, keepdims=True).astype(jnp.int32)
    return jnp.where(iota((slots, cells), 1) == column, 1.0, 0.0).astype(BF16)


def even(axis):
    return lax.rem(lax.axis_index(axis), 2) == 0


def swap(x, axis, first):
    counts = {name: lax.axis_size(name) for name in ("gx", "gy")}
    other = "gy" if axis == "gx" else "gx"

    def device(along, across):
        at = {axis: along, other: across}
        return at["gx"] * counts["gy"] + at["gy"]

    last = counts[axis] - 1
    pairs = [(device(i, k), device(i + 1, k)) for i in range(first, last, 2) for k in range(counts[other])]
    if first:
        pairs += [(device(i, k), device(i, k + 1)) for i in (0, last) for k in range(0, counts[other], 2)]
    return lax.ppermute(x, ("gx", "gy"), pairs + [(b, a) for a, b in pairs])


def call(kernel, name, outs, args, scratch=(), flops=0, nbytes=0, space=pltpu.VMEM, out_space=pltpu.VMEM):
    return pl.pallas_call(
        kernel,
        out_shape=[jax.ShapeDtypeStruct(s, d) for s, d in outs],
        in_specs=[pl.BlockSpec(memory_space=space)] * len(args),
        out_specs=[pl.BlockSpec(memory_space=out_space)] * len(outs),
        scratch_shapes=list(scratch),
        compiler_params=pltpu.CompilerParams(vmem_limit_bytes=16 << 20),
        cost_estimate=pl.CostEstimate(flops=flops, bytes_accessed=nbytes, transcendentals=0),
        name=name,
    )(*(pltpu.with_memory_space_constraint(a, space) if space is pltpu.HBM else a for a in args))


def lane_edge(center):
    axis = center.ndim - 1
    lane = iota(center.shape, axis)
    last = center.shape[axis] - 1
    below = jnp.where(lane == 0, 0.0, pltpu.roll(center, 1, axis))
    above = jnp.where(lane == last, 0.0, pltpu.roll(center, last, axis))
    return below + above


def moved(center, before, after, beside):
    own = (1.0 - 6.0 * SPREAD - CARRY) * center
    return own + SPREAD * (beside + after) + (SPREAD + CARRY) * before


def stencil(ref, c, x0, nx, ny):
    center = ref[c, x0 : x0 + nx, OWN : OWN + ny, :]
    before = ref[c, x0 - 1 : x0 - 1 + nx, OWN : OWN + ny, :]
    after = ref[c, x0 + 1 : x0 + 1 + nx, OWN : OWN + ny, :]
    beside = ref[c, x0 : x0 + nx, OWN - 1 : OWN - 1 + ny, :] + ref[c, x0 : x0 + nx, OWN + 1 : OWN + 1 + ny, :]
    return moved(center, before, after, beside + lane_edge(center))


def as_column(row, n, start=0):
    shape = (n, row.shape[1])
    return jnp.sum(jnp.where(iota(shape, 0) + start == iota(shape, 1), row, 0.0), axis=1, keepdims=True)


def as_row(column, lanes, start=0):
    shape = (column.shape[0], lanes)
    return jnp.sum(jnp.where(iota(shape, 0) + start == iota(shape, 1), column, 0.0), axis=0, keepdims=True)


def packing(turbines):
    per_row = LANES // turbines
    rows = turbines // per_row
    return rows, per_row, 2 * rows + 3, -(-(2 * rows + 9) // 16) * 16


def in_parts(x, count):
    parts = []
    for _ in range(count):
        parts.append(rounded(x))
        x = x - parts[-1]
    return parts


def picked(flag, a, b, lo, hi):
    return jnp.where(flag, a[lo:hi, :], b[lo:hi, :])


def low_edge(axis, odd, even_, lo, hi):
    return jnp.where(lax.axis_index(axis) > 0, picked(even(axis), odd, even_, lo, hi), 0.0)


def high_edge(axis, odd, even_, lo, hi):
    there = lax.axis_index(axis) < lax.axis_size(axis) - 1
    return jnp.where(there, picked(even(axis), even_, odd, lo, hi), 0.0)


def prepare(
    v_hbm, tc_hbm, owner_hbm, slot_hbm, height_hbm, load_hbm,
    v, tc, slot, height, load, count_ref, line, y_even, y_odd, x_even, x_odd,
    owner, exact, sum_ref, sems,
):
    pairs = ((slot_hbm, slot), (height_hbm, height), (tc_hbm, tc), (load_hbm, load), (owner_hbm, owner), (v_hbm, v))
    copies = [pltpu.make_async_copy(a, b, sems.at[i]) for i, (a, b) in enumerate(pairs)]
    for copy in copies:
        copy.start()
    _, turbines, points = slot.shape
    slots, levels = count_ref.shape[1:]
    comps, nx, ny, _ = v.shape
    cells = nx * ny
    first = lax.axis_index("gy") * slots
    copies[0].wait()
    copies[1].wait()
    for t in range(turbines):
        a = ones_at(one_hot(slots, slot[0, t : t + 1, :] - first))
        b = ones_at(one_hot(levels, height[0, t : t + 1, :]))
        exact[t] = lax.dot_general(a, b, NT, preferred_element_type=F32)
    for copy in copies[2:]:
        copy.wait()

    ev = even("gy")
    at = 0
    for c in range(comps):
        for k in range(2):
            high = v[c, :, ny - 2 + k, :]
            low = v[c, :, k, :]
            y_even[at : at + nx, :] = jnp.where(ev, high, low)
            y_odd[at : at + nx, :] = jnp.where(ev, low, high)
            at += nx
    values = v[0, :, :, :].reshape(cells, levels).astype(BF16)
    rows = jnp.dot(pick_slots(tc, cells), values, preferred_element_type=F32)
    for t in range(turbines):
        count = exact[t]
        count_ref[t] = count.astype(BF16)
        sum_ref[t : t + 1, :] = jnp.sum(count * rows, axis=0, keepdims=True)

    owner_row = jnp.broadcast_to(owner[...].astype(F32), (turbines, turbines))
    member = owner_row == as_column(owner_row, turbines)
    load_row = as_row(jnp.sum(load[0, :, :], axis=1, keepdims=True), turbines)
    total = jnp.sum(jnp.where(member, load_row, 0.0), axis=1, keepdims=True)
    number = jnp.sum(jnp.where(member, 1.0, 0.0), axis=1, keepdims=True)
    line[...] = jnp.zeros((8, LANES), F32)
    line[SUMS : SUMS + 1, :] = as_row(jnp.sum(sum_ref[...], axis=1, keepdims=True), LANES)
    line[SCALE : SCALE + 1, :] = as_row(LOAD / (total / (number * points)), LANES)
    line[CELLS : CELLS + 1, 0:slots] = tc[0, :, :].astype(F32) + 1.0
    for out in (y_even, y_odd):
        out[at : at + 8, :] = jnp.zeros((8, LANES), F32)
        out[at : at + 1, :] = line[CELLS : CELLS + 1, :]

    local = slot[0, :, :] - first
    inside = (local >= 0) & (local < slots)
    code = jnp.where(inside, local * levels + height[0, :, :] + 1, 0).astype(F32)
    ev = even("gx")
    at = 0
    for c in range(comps):
        for k in range(2):
            right, left = v[c, nx - 2 + k, :, :], v[c, k, :, :]
            x_even[at : at + ny, :] = jnp.where(ev, right, left)
            x_odd[at : at + ny, :] = jnp.where(ev, left, right)
            at += ny
    for part in (code, load[0, :, :]):
        for k in range(0, points, LANES):
            for out in (x_even, x_odd):
                out[at : at + turbines, :] = part[:, k : k + LANES]
            at += turbines
    for out in (x_even, x_odd):
        out[at : at + 8, :] = line[...]


def extend(v, yo, ye, xo, xe, field, comps):
    _, nx, ny, _ = v.shape
    for c in comps:
        out = c if len(comps) > 1 else 0
        field[out, 2 : 2 + nx, OWN : OWN + ny, :] = v[c, :, :, :]
        for k in range(2):
            at = (c * 2 + k) * nx
            field[out, 2 : 2 + nx, OWN - 2 + k, :] = low_edge("gy", yo, ye, at, at + nx)
            field[out, 2 : 2 + nx, OWN + ny + k, :] = high_edge("gy", yo, ye, at, at + nx)
            at = (c * 2 + k) * ny
            for x, edge in ((k, low_edge), (2 + nx + k, high_edge)):
                field[out, x, 0:OWN, :] = jnp.zeros((OWN, LANES), F32)
                field[out, x, OWN + ny : PLANE, :] = jnp.zeros((PLANE - OWN - ny, LANES), F32)
                field[out, x, OWN : OWN + ny, :] = edge("gx", xo, xe, at, at + ny)


def edge_slots(cell_row, cells):
    n, slots = cells.shape[0], cell_row.shape[1]
    slot = iota((n, slots), 1).astype(F32)
    return jnp.max(jnp.where(cell_row == cells, slot, NO_SLOT), axis=1, keepdims=True).astype(BF16)


def spread(places, z, weight):
    high = weight.astype(BF16)
    low = (weight - high.astype(F32)).astype(BF16)
    zero = jnp.zeros((), BF16)
    at_z = ones_at(one_hot(LANES, z))
    left = []
    for edge, slot in places:
        here = edge == slot.astype(BF16)
        left += [jnp.where(here, high, zero), jnp.where(here, low, zero)]
    both = lax.dot_general(jnp.concatenate(left, axis=0), at_z, NT, preferred_element_type=F32)
    n = both.shape[0] // len(left)
    return [both[2 * k * n : (2 * k + 1) * n] + both[(2 * k + 1) * n : (2 * k + 2) * n] for k in range(len(places))]


def pair_up(v, tc, slot, height, load, counts, loads, matrix, edge_counts, single, products):
    turbines, slots, levels = counts.shape
    _, nx, ny, _ = v.shape
    cells = nx * ny
    first = lax.axis_index("gy") * slots
    zero = jnp.zeros((), BF16)
    values = v[0, :, :, :].reshape(cells, levels).astype(BF16)
    rows = jnp.dot(pick_slots(tc, cells), values, preferred_element_type=F32)
    row_x = iota((2 * ny, slots), 0)
    edge = jnp.where(row_x < ny, row_x, row_x + (nx - 2) * ny)
    select = jnp.where(edge == tc[0, :, :], 1.0, 0.0).astype(BF16)
    for t in range(turbines):
        a = ones_at(one_hot(slots, slot[0, t : t + 1, :] - first))
        at_z = one_hot(levels, height[0, t : t + 1, :])
        weight = load[0, t : t + 1, :]
        high = weight.astype(BF16)
        low = (weight - high.astype(F32)).astype(BF16)
        b = jnp.concatenate([jnp.where(at_z, high, zero), jnp.where(at_z, low, zero)], axis=0)
        both = lax.dot_general(a, b, NT, preferred_element_type=F32)
        both = both[:, :levels] + both[:, levels:]
        loads[t] = both
        for k, piece in enumerate(in_parts(rows * both, 2)):
            products[k, t] = piece.astype(BF16)
    for t in range(0, turbines, 2):
        pair = jnp.concatenate([counts[t], counts[t + 1]], axis=1)
        both = jnp.dot(select, pair, preferred_element_type=F32)
        edge_counts[t], edge_counts[t + 1] = both[:, :levels], both[:, levels:]
    hits = counts[0].astype(F32)
    for t in range(1, turbines):
        hits = hits + counts[t].astype(F32)
    single[...] = jnp.where(hits == 1.0, 1.0, 0.0).astype(BF16)
    block = 16
    wide = turbines * block
    gram = jnp.zeros((wide, wide), F32)
    for b in range(0, slots, block):
        left = counts[:, b : b + block, :].reshape(wide, levels)
        for k in range(2):
            right = products[k, :, b : b + block, :].reshape(wide, levels)
            gram = gram + lax.dot_general(left, right, NT, preferred_element_type=F32)
    keep = (iota((wide, wide), 0) & (block - 1)) == (iota((wide, wide), 1) & (block - 1))
    gram = jnp.sum(jnp.where(keep, gram, 0.0).reshape(turbines, block, wide), axis=1)
    select = jnp.where(iota((wide, LANES), 0) // block == iota((wide, LANES), 1) % turbines, 1.0, 0.0).astype(BF16)
    both = jnp.dot(jnp.concatenate(in_parts(gram, 2), axis=0).astype(BF16), select, preferred_element_type=F32)
    both = both[:turbines] + both[turbines:]
    rows, per_row, _, _ = packing(turbines)
    row, lane = iota((turbines, LANES), 0), iota((turbines, LANES), 1)
    for r in range(rows):
        here = (row // per_row == r) & (lane // turbines == row % per_row)
        matrix[r : r + 1, :] = jnp.sum(jnp.where(here, both, 0.0), axis=0, keepdims=True)


def beside(v, tc, yo, ye, counts, part, field, sums):
    turbines, _, levels = counts.shape
    _, nx, ny, _ = v.shape
    cells = nx * ny
    field[0, 1 : 1 + nx, OWN : OWN + ny, :] = v[0, :, :, :]
    field[0, 1 : 1 + nx, OWN - 1, :] = low_edge("gy", yo, ye, nx, 2 * nx)
    field[0, 1 : 1 + nx, OWN + ny, :] = high_edge("gy", yo, ye, 0, nx)
    for x in (0, nx + 1):
        field[0, x, OWN : OWN + ny, :] = jnp.zeros((ny, levels), F32)
    update = stencil(field, 0, 1, nx, ny).reshape(cells, levels)
    update = jnp.concatenate(in_parts(update, 2), axis=1).astype(BF16)
    later = jnp.dot(pick_slots(tc, cells), update, preferred_element_type=F32)
    later = later[:, :levels] + later[:, levels:]
    for t in range(turbines):
        sums[t : t + 1, :] = jnp.sum(counts[t].astype(F32) * later, axis=0, keepdims=True)
    row = as_row(jnp.sum(sums[...], axis=1, keepdims=True), LANES, 3 * turbines)
    part[...] = jnp.broadcast_to(row, (8, LANES))


def reduce_sums(comps, ny, yo, ye, xo, xe, edge_counts, line, matrix, part, out, sums, box):
    turbines = edge_counts.shape[0]
    ev_x = even("gx")
    left = (SPREAD + CARRY) * low_edge("gx", xo, xe, ny, 2 * ny)
    right = SPREAD * high_edge("gx", xo, xe, 0, ny)
    for t in range(turbines):
        sides = edge_counts[t, 0:ny, :] * left + edge_counts[t, ny : 2 * ny, :] * right
        sums[t : t + 1, :] = jnp.sum(sides, axis=0, keepdims=True)
    rows, _, corner, _ = packing(turbines)
    box[...] = jnp.zeros(box.shape, F32)
    for c in range(comps):
        for i, (edge, at) in enumerate(((low_edge, (c * 2 + 1) * ny), (high_edge, c * 2 * ny))):
            to = corner + 2 * c + i
            box[0, to : to + 1, :] = edge("gx", xo, xe, at, at + 1)
            box[1, to : to + 1, :] = edge("gx", xo, xe, at + ny - 1, at + ny)
    at = xe.shape[0] - 8 + SUMS
    before, after = picked(ev_x, xo, xe, at, at + 1), picked(ev_x, xe, xo, at, at + 1)
    row = part[0:1, :] + line[SUMS : SUMS + 1, :]
    row = row + as_row(jnp.sum(sums[...], axis=1, keepdims=True), LANES, 3 * turbines)
    for k, other in ((1, before), (2, after)):
        row = row + pltpu.roll(jnp.broadcast_to(other, (8, LANES)), k * turbines, 1)[0:1, :]
    for side in range(2):
        for k, piece in enumerate(in_parts(matrix[0:rows, :], 2)):
            box[side, k * rows : (k + 1) * rows, :] = piece
        for k, piece in enumerate(in_parts(row, 3)):
            box[side, 2 * rows + k : 2 * rows + k + 1, :] = piece
    me = lax.axis_index("gy")
    below, above = box[0], box[1]
    for k in range(out.shape[0]):
        out[k] = jnp.where(me + 1 == k, above, below).astype(BF16)


def edges(slots, pieces, v, slot, height, load, yo, ye, xo, xe, line, edge_x, edge_y, update_ref, strip_ref, scales, field):
    comps, nx, ny, levels = v.shape
    turbines = edge_x.shape[1]
    ev, ev_y = even("gx"), even("gy")
    extend(v, yo, ye, xo, xe, field, tuple(range(comps)))
    ends = iota((nx, LANES), 0)
    for c in range(comps):
        update_ref[c] = stencil(field, c, 1, nx + 2, ny)
        for k, (a, b, y) in enumerate(((yo, ye, 0), (ye, yo, ny - 1))):
            near, far = (c * 2 + 1 - k) * nx, (c * 2 + k) * nx
            center = picked(ev_y, a, b, near, near + nx)
            before = jnp.where(ends == 0, 0.0, pltpu.roll(center, 1, 0))
            after = jnp.where(ends == nx - 1, 0.0, pltpu.roll(center, nx - 1, 0))
            others = picked(ev_y, a, b, far, far + nx) + v[c, :, y, :] + lane_edge(center)
            strip_ref[c, k] = moved(center, before, after, others)

    at = xe.shape[0] - 8 + SCALE
    rows_of = (line[SCALE : SCALE + 1, :], picked(ev, xo, xe, at, at + 1), picked(ev, xe, xo, at, at + 1))
    for k, row in enumerate(rows_of):
        scales[k] = jnp.broadcast_to(as_column(row, turbines), (turbines, LANES))
    at = xe.shape[0] - 8 + CELLS
    code_at = comps * 2 * ny
    load_at = code_at + pieces * turbines
    shift = levels.bit_length() - 1
    for k, (a, b) in enumerate(((xo, xe), (xe, xo))):
        cell = picked(ev, a, b, at, at + 1)[:, :slots].astype(jnp.int32) - 1
        edge = edge_slots(cell, iota((ny, slots), 0) + (1 - k) * (nx - 1) * ny)
        codes = [picked(ev, a, b, code_at + i * turbines, code_at + (i + 1) * turbines) for i in range(pieces)]
        codes = jnp.concatenate(codes, axis=1).astype(jnp.int32) - 1
        there = [picked(ev, a, b, load_at + i * turbines, load_at + (i + 1) * turbines) for i in range(pieces)]
        there = jnp.concatenate(there, axis=1)
        for t in range(turbines):
            code = codes[t : t + 1, :]
            (edge_x[k, t],) = spread([(edge, code >> shift)], code & (levels - 1), there[t : t + 1, :])

    me = lax.axis_index("gy")
    at = ye.shape[0] - 8
    lists = []
    for a, b, y in ((yo, ye, ny - 1), (ye, yo, 0)):
        cell = picked(ev_y, a, b, at, at + 1)[:, :slots].astype(jnp.int32) - 1
        lists.append(edge_slots(cell, iota((nx, slots), 0) * ny + y))
    for t in range(turbines):
        row = slot[0, t : t + 1, :]
        places = [(edge, row - (me + k) * slots) for edge, k in zip(lists, (-1, 1))]
        edge_y[0, t], edge_y[1, t] = spread(places, height[0, t : t + 1, :], load[0, t : t + 1, :])


def advance(points, got, v, tc, yo, ye, xo, xe, scales, loads, single, edge_x, edge_y, update_ref, strip_ref, out, field, parts, result, sems):
    comps, nx, ny, levels = v.shape
    turbines, slots, _ = loads.shape
    cells = nx * ny
    ev_x, ev_y = even("gx"), even("gy")
    rows, per_row, corner, _ = packing(turbines)
    total = got[0].astype(F32)
    for k in range(1, got.shape[0]):
        total = total + got[k].astype(F32)
    matrix = total[0:rows, :] + total[rows : 2 * rows, :]
    sums_row = total[2 * rows : 2 * rows + 1, :] + total[2 * rows + 1 : 2 * rows + 2, :]
    sums_row = sums_row + total[2 * rows + 2 : 2 * rows + 3, :]

    def coefs(scale, sums):
        return -(scale * (FREE_WIND + sums / points))

    own, left, right = (coefs(scales[k], as_column(sums_row, turbines, k * turbines)) for k in range(3))
    row, lane = iota((turbines, LANES), 0), iota((turbines, LANES), 1)
    own_row = jnp.sum(jnp.where(row == lane % turbines, own, 0.0), axis=0, keepdims=True)
    products = matrix * own_row
    forced = jnp.zeros((turbines, LANES), F32)
    for r in range(rows):
        here = (row // per_row == r) & (lane // turbines == row % per_row)
        forced = forced + jnp.where(here, products[r : r + 1, :], 0.0)
    forced = jnp.sum(forced, axis=1, keepdims=True)
    later = coefs(scales[0], as_column(sums_row, turbines, 3 * turbines) + forced)

    for s in range(0, slots, 16):
        first = jnp.zeros((16, levels), F32)
        second = first
        for t in range(turbines):
            part = loads[t, s : s + 16, :]
            first = first + own[t : t + 1, :] * part
            second = second + later[t : t + 1, :] * part
        for i, rest in enumerate((first, second)):
            for k in range(2):
                piece = rest.astype(BF16)
                rest = rest - piece.astype(F32)
                at = (2 * i + k) * levels
                parts[s : s + 16, at : at + levels] = piece
    parts[:, 4 * levels :] = single[...]
    row = tc[0, :, :]
    put = jnp.where(iota((cells, slots), 0) == row, 1.0, 0.0).astype(BF16)
    spread_out = jnp.dot(put, parts[...], preferred_element_type=F32)
    pieces = [spread_out[:, k * levels : (k + 1) * levels] for k in range(5)]
    first = (pieces[0] + pieces[1]).reshape(nx, ny, levels)
    second = (pieces[2] + pieces[3]).reshape(nx, ny, levels)
    alone = pieces[4].reshape(nx, ny, levels) > 0.5

    def force(values, weight):
        push = rounded(values) * weight
        return jnp.where(alone, rounded(push), push)

    for c in range(comps):
        field[c, 1 : 1 + nx, OWN : OWN + ny, :] = update_ref[c, 1 : 1 + nx, :, :] + force(v[c, :, :, :], first)

    sums = []
    for edge, coef in ((edge_x.at[0], left), (edge_x.at[1], right), (edge_y.at[0], own), (edge_y.at[1], own)):
        side = coef[0:1, :] * edge[0]
        for t in range(1, turbines):
            side = side + coef[t : t + 1, :] * edge[t]
        sums.append(side)
    ix, iy = lax.axis_index("gx"), lax.axis_index("gy")
    last_y = lax.axis_size("gy") - 1
    there_x = (ix > 0, ix < lax.axis_size("gx") - 1)
    there_y = (iy > 0, iy < last_y)
    beside_y = (jnp.maximum(iy - 1, 0), jnp.minimum(iy + 1, last_y))
    corner_rows = [jnp.where(there_y[k], got[beside_y[k]].astype(F32), 0.0) for k in range(2)]
    row_x, row_y = iota((nx, LANES), 0), iota((ny, LANES), 0)
    for c in range(comps):
        at_corner = [[corner_rows[y][corner + c * 2 + x : corner + c * 2 + x + 1, :] for y in range(2)] for x in range(2)]
        for k, (a, b) in enumerate(((xo, xe), (xe, xo))):
            at = (c * 2 + 1 - k) * ny
            x = k * (nx + 1)
            push = rounded(rounded(picked(ev_x, a, b, at, at + ny)) * sums[k])
            extra = jnp.where(row_y == 0, at_corner[k][0], 0.0) + jnp.where(row_y == ny - 1, at_corner[k][1], 0.0)
            value = update_ref[c, x, :, :] + SPREAD * extra + push
            field[c, x, OWN : OWN + ny, :] = jnp.where(there_x[k], value, 0.0)
        for k, (a, b) in enumerate(((yo, ye), (ye, yo))):
            at = (c * 2 + 1 - k) * nx
            y = OWN - 1 + k * (ny + 1)
            push = rounded(rounded(picked(ev_y, a, b, at, at + nx)) * sums[2 + k])
            extra = jnp.where(row_x == 0, (SPREAD + CARRY) * at_corner[0][k], 0.0)
            extra = extra + jnp.where(row_x == nx - 1, SPREAD * at_corner[1][k], 0.0)
            value = strip_ref[c, k] + extra + push
            field[c, 1 : 1 + nx, y, :] = jnp.where(there_y[k], value, 0.0)
    copies = []
    half = nx // 2
    for c in range(comps):
        for x in (0, half):
            now = field[c, 1 + x : 1 + x + half, OWN : OWN + ny, :]
            push = rounded(now) * second[x : x + half]
            push = jnp.where(alone[x : x + half], rounded(push), push)
            result[c, x : x + half] = stencil(field, c, 1 + x, half, ny) + push
            part = (c, pl.ds(x, half))
            copies.append(pltpu.make_async_copy(result.at[part], out.at[part], sems.at[len(copies)]))
            copies[-1].start()
    for copy in copies:
        copy.wait()


def body(velocity, tile_cells, owner, point_slot, point_z, loading):
    comps, nx, ny, levels = velocity.shape
    _, turbines, points = point_slot.shape
    slots = tile_cells.shape[2]
    tiles_y = lax.axis_size("gy")
    pieces = points // LANES
    chunk_rows = packing(turbines)[3]
    rows_y = comps * 2 * nx + 8
    rows_x = comps * 2 * ny + 2 * pieces * turbines + 8
    args = (velocity, tile_cells, owner, point_slot, point_z, loading)
    work = {"flops": 26 * turbines * slots * points * levels, "nbytes": 1 << 20}

    def field(n, planes):
        return pltpu.VMEM((n, planes, PLANE, levels), F32)

    v, tc, slot, height, load, counts, line, y_even, y_odd, x_even, x_odd = call(
        prepare,
        "prepare",
        [(x.shape, x.dtype) for x in (velocity, tile_cells, point_slot, point_z, loading)]
        + [((turbines, slots, levels), BF16), ((8, LANES), F32)]
        + [((rows_y, levels), F32)] * 2
        + [((rows_x, levels), F32)] * 2,
        args,
        [
            pltpu.VMEM(owner.shape, jnp.int32),
            pltpu.VMEM((turbines, slots, levels), F32),
            pltpu.VMEM((turbines, levels), F32),
            pltpu.SemaphoreType.DMA((len(args),)),
        ],
        space=pltpu.HBM,
        **work,
    )
    yo, ye = swap(y_odd, "gy", 1), swap(y_even, "gy", 0)
    xo, xe = swap(x_odd, "gx", 1), swap(x_even, "gx", 0)
    loads, matrix, edge_counts, single = call(
        pair_up,
        "pair_up",
        [
            ((turbines, slots, levels), F32),
            ((8, LANES), F32),
            ((turbines, 2 * ny, levels), F32),
            ((slots, levels), BF16),
        ],
        (v, tc, slot, height, load, counts),
        [pltpu.VMEM((2, turbines, slots, levels), BF16)],
        **work,
    )
    (part,) = call(
        beside,
        "beside",
        [((8, LANES), F32)],
        (v, tc, yo, ye, counts),
        [field(1, nx + 2), pltpu.VMEM((turbines, levels), F32)],
        flops=work["flops"] // 4,
        nbytes=work["nbytes"],
    )

    def reduce_of(*refs):
        return reduce_sums(comps, ny, *refs)

    (chunk,) = call(
        reduce_of,
        "reduce_sums",
        [((tiles_y, chunk_rows, LANES), BF16)],
        (yo, ye, xo, xe, edge_counts, line, matrix, part),
        [pltpu.VMEM((turbines, levels), F32), pltpu.VMEM((2, chunk_rows, LANES), F32)],
    )
    got = lax.all_to_all(chunk, "gy", 0, 0)

    def edges_of(*refs):
        return edges(slots, pieces, *refs)

    edge_x, edge_y, update, strip, scales = call(
        edges_of,
        "edges",
        [
            ((2, turbines, ny, levels), F32),
            ((2, turbines, nx, levels), F32),
            ((comps, nx + 2, ny, levels), F32),
            ((comps, 2, nx, levels), F32),
            ((3, turbines, LANES), F32),
        ],
        (v, slot, height, load, yo, ye, xo, xe, line),
        [field(comps, nx + 4)],
        **work,
    )

    def advance_by(*refs):
        return advance(points, *refs)

    (out,) = call(
        advance_by,
        "advance",
        [(velocity.shape, F32)],
        (got, v, tc, yo, ye, xo, xe, scales, loads, single, edge_x, edge_y, update, strip),
        [
            field(comps, nx + 2),
            pltpu.VMEM((slots, 5 * levels), BF16),
            pltpu.VMEM(velocity.shape, F32),
            pltpu.SemaphoreType.DMA((2 * comps,)),
        ],
        out_space=pltpu.HBM,
    )
    return out


def solution(mesh):
    in_specs = (
        P(None, "gx", "gy", None),
        P("gx", "gy", None),
        P("gx", None),
        P("gx", None, None),
        P("gx", None, None),
        P("gx", None, None),
    )
    out_specs = P(None, "gx", "gy", None)
    return jax.shard_map(body, mesh=mesh, in_specs=in_specs, out_specs=out_specs, check_vma=False)
```
